32 devices in a mesh: fsdp: 8 (over z, y), dp: 4 (over x, core).
Axes of the slice: x: 2, y: 2, z: 4, core: 2. Of those that a mesh axis runs over, the one named last changes fastest.
Arguments:
- series_values: float32 [24960, 96], P(('fsdp', 'dp')), may hold values from -15 to 15
- quarter_index: int32 [128], P(('fsdp', 'dp')), may hold values from 0 to 3, as said below
- patch_weight: bfloat16 [96, 1024], P(None, 'fsdp'), may hold values from -0.625 to 0.625
- heads_in: bfloat16 [1024, 3072], P('fsdp'), may hold values from -0.1875 to 0.1875
- heads_out: bfloat16 [1024, 1024], P('fsdp'), may hold values from -0.375 to 0.375
- expand_weight: bfloat16 [1024, 2048], P('fsdp'), may hold values from -0.1875 to 0.1875
- reduce_weight: bfloat16 [2048, 1024], P('fsdp'), may hold values from -0.125 to 0.125
- norm_gains: bfloat16 [2, 1024], P(None, 'fsdp'), may hold values from 0.5 to 1.5
- bias_rows: bfloat16 [4, 1024], P(None, 'fsdp'), may hold values from -1.796875 to 1.796875
- expand_bias: bfloat16 [2048], P('fsdp'), may hold values from -1.796875 to 1.796875
- cotangent: bfloat16 [24960, 1024], P(('fsdp', 'dp')), may hold values from -6 to 6
Outputs:
- layer_output: bfloat16 [24960, 1024], P(('fsdp', 'dp'))
- series_grad: float32 [24960, 96], P(('fsdp', 'dp'))
- grad_patch: float32 [96, 1024], P(None, 'fsdp')
- grad_heads_in: float32 [1024, 3072], P('fsdp')
- grad_heads_out: float32 [1024, 1024], P('fsdp')
- grad_expand: float32 [1024, 2048], P('fsdp')
- grad_reduce: float32 [2048, 1024], P('fsdp')
- grad_gains: float32 [2, 1024], P(None, 'fsdp')
- grad_biases: float32 [4, 1024], P(None, 'fsdp')
- grad_expand_bias: float32 [2048], P('fsdp')
The draws below stay inside these ranges and needn't reach their ends.
Inputs may be any that keep to these rules, and one draw needn't show every extreme that they name: `quarter_index`: along fsdp the quarters of one slot position run 0, 1, 2, 3 and then again from 0, closing the loop: the device at fsdp index i whose slot holds quarter q shares that long series with the same slot position at the same dp index on fsdp indices i - q to i - q + 3, modulo 8.
All inputs are finite; a program needn't handle non-finite values.
Results may differ from the reference program's by a relative error of at most 0.014.
Values may be sent and summed in bfloat16 or wider, within the bound.
No kernel may reach another device: no remote copies, remote signals or barrier semaphores. Data moves between devices by JAX's collectives and lax.ppermute only.
A program may use at most 256 MiB of HBM per device.

```python
import math
import jax
import jax.numpy as jnp
from jax import lax

D = 1024
HEADS = 8
HEAD_DIM = 128
FF = 2048
PATCH = 96
SPAN = 15
SHORT_SLOTS = 48
LONG_SLOTS = 4
TOKENS = 24960
N_FSDP = 8
N_DP = 4


def draw_series_values(key, part):
    slot_count = TOKENS // SPAN
    key_offset = jax.random.fold_in(key, 11)
    key_scale = jax.random.fold_in(key, 12)
    key_noise = jax.random.fold_in(key, 13)
    offsets = jax.random.uniform(key_offset, (slot_count, 1, 1), jnp.float32, -1.0, 1.0)
    scales = jnp.exp(jax.random.uniform(key_scale, (slot_count, 1, 1), jnp.float32, math.log(0.3), math.log(3.0)))
    noise = jnp.clip(jax.random.normal(key_noise, (slot_count, SPAN, PATCH), jnp.float32), -4.5, 4.5)
    return (offsets + scales * noise).reshape(TOKENS, PATCH)


def draw_quarter_index(key, part):
    phases = jax.random.randint(jax.random.fold_in(key, 21), (1, N_DP * LONG_SLOTS), 0, 4)
    position = jnp.arange(N_FSDP, dtype=jnp.int32)[:, None]
    return ((position - phases) % 4).astype(jnp.int32).reshape(N_FSDP * N_DP * LONG_SLOTS)


def draw_cotangent(key, part):
    slot_count = TOKENS // SPAN
    key_common = jax.random.fold_in(key, 31)
    key_noise = jax.random.fold_in(key, 32)
    common = 0.8 * jax.random.normal(key_common, (slot_count, 1, D), jnp.float32)
    noise = 0.6 * jax.random.normal(key_noise, (slot_count, SPAN, D), jnp.float32)
    return jnp.clip(common + noise, -6.0, 6.0).reshape(TOKENS, D).astype(jnp.bfloat16)


def steps_of(rng, dims, split, least, top_value):
    def one(axis_at, parts):
        draws = jax.random.uniform(jax.random.fold_in(jax.random.fold_in(rng, 6), axis_at), (parts,), jnp.float32, least / len(split), top_value / len(split))
        return jnp.repeat(jnp.exp(draws), dims[axis_at] // parts).reshape((-1,) + (1,) * (len(dims) - axis_at - 1))

    gain = one(*split[0])
    for cut in split[1:]:
        gain = gain * one(*cut)
    return gain


def bell_draw(rng, extent, deviation, bound, shards=(), kind=jnp.bfloat16):
    array = deviation * jax.random.normal(rng, extent, jnp.float32)
    if shards:
        array = array * steps_of(rng, extent, shards, -0.22, 0.18)
    return jnp.clip(array, -bound, bound).astype(kind)


def setup_inputs(seed: int = 0) -> dict:
    keys = jax.random.split(jax.random.key(seed), 12)
    return {
        "series_values": draw_series_values(jax.random.fold_in(keys[11], 71), 0),
        "quarter_index": draw_quarter_index(jax.random.fold_in(keys[11], 71), 0),
        "patch_weight": bell_draw(keys[2], (PATCH, D), PATCH ** -0.5, 0.625, ((1, 8),)),
        "heads_in": bell_draw(keys[3], (D, 3 * D), D ** -0.5, 0.1875, ((0, 8),)),
        "heads_out": bell_draw(keys[4], (D, D), (D // 4) ** -0.5, 0.375, ((0, 8),)),
        "expand_weight": bell_draw(keys[5], (D, FF), D ** -0.5, 0.1875, ((0, 8),)),
        "reduce_weight": bell_draw(keys[6], (FF, D), FF ** -0.5, 0.125, ((0, 8),)),
        "norm_gains": jnp.clip(1.0 + 0.1 * jax.random.normal(keys[7], (2, D), jnp.float32), 0.5, 1.5).astype(jnp.bfloat16),
        "bias_rows": bell_draw(keys[8], (4, D), 0.3, 1.796875, ((1, 8),)),
        "expand_bias": bell_draw(keys[9], (FF,), 0.3, 1.796875, ((0, 8),)),
        "cotangent": draw_cotangent(jax.random.fold_in(keys[11], 71), 0),
    }


EPSILON = 1e-05
NEG_LARGE = -1e+30
HIGH = lax.Precision.HIGHEST

@jax.custom_vjp
def low(v):
    return lax.optimization_barrier(v.astype(jnp.bfloat16)).astype(jnp.float32)

@jax.custom_vjp
def low_back(v):
    return v

def low_keep(v):
    return (low(v), None)

def low_pass(kept, grad):
    return (grad,)

def back_keep(v):
    return (v, None)

def back_low(kept, grad):
    return (low(grad),)
low.defvjp(low_keep, low_pass)
low_back.defvjp(back_keep, back_low)

def exact_dot(left, right):
    return jnp.dot(left, right, precision=HIGH)

def layer_norm(inputs, gain_row, shift_row):
    center = inputs - lax.optimization_barrier(jnp.mean(inputs, axis=-1, keepdims=True))
    spread = lax.optimization_barrier(jnp.mean(center * center, axis=-1, keepdims=True))
    return center * lax.rsqrt(spread + EPSILON) * gain_row + shift_row

def attend(query_rows, key_rows, value_rows, allowed):
    scaling = HEAD_DIM ** (-0.5)
    scores = low_back(jnp.einsum('...ihx,...jhx->...hij', query_rows, key_rows, precision=HIGH) * scaling)
    scores = jnp.where(allowed[..., None, :, :], scores, NEG_LARGE)
    weights = low(jax.nn.softmax(scores, axis=-1))
    return low(low_back(jnp.einsum('...hij,...jhx->...ihx', weights, value_rows, precision=HIGH)))

def embed_project(inputs, params):
    patch_mat, heads_mat, out_mat, expand_mat, reduce_mat, gain_rows, shift_rows, expand_shift = params
    embedded = low_back(exact_dot(low(inputs), patch_mat) + shift_rows[0])
    first_norm = low(layer_norm(embedded, gain_rows[0], shift_rows[1]))
    projected = low(low_back(exact_dot(first_norm, heads_mat)))
    return (embedded, projected)

def finish(embedded, mixture, params):
    patch_mat, heads_mat, out_mat, expand_mat, reduce_mat, gain_rows, shift_rows, expand_shift = params
    middle = embedded + low_back(exact_dot(mixture, out_mat))
    second_norm = low(layer_norm(middle, gain_rows[1], shift_rows[2]))
    pre_act = low_back(exact_dot(second_norm, expand_mat) + expand_shift)
    activation = low(jax.nn.gelu(pre_act, approximate=False))
    return middle + low_back(exact_dot(activation, reduce_mat) + shift_rows[3])

def layer_forward(series_values, quarter, params):
    device_count = N_FSDP * N_DP
    slot_count = SHORT_SLOTS + LONG_SLOTS
    short_rows = SHORT_SLOTS * SPAN
    long_rows = LONG_SLOTS * SPAN
    grouped = series_values.reshape(N_FSDP, N_DP, slot_count, SPAN * PATCH)
    slot_sums = jnp.stack([lax.optimization_barrier(jnp.sum(grouped, -1)), lax.optimization_barrier(jnp.sum(grouped * grouped, -1))], -1)
    long_sums = slot_sums[:, :, SHORT_SLOTS:]
    chain_sum = long_sums
    for offset in (1, 2, 3, -1, -2, -3):
        keep = (offset >= -quarter) & (offset <= 3 - quarter)
        chain_sum = chain_sum + jnp.where(keep[..., None], jnp.roll(long_sums, -offset, axis=0), 0.0)
    totals = jnp.concatenate([slot_sums[:, :, :SHORT_SLOTS], chain_sum], 2)
    counts = jnp.where(jnp.arange(slot_count) < SHORT_SLOTS, SPAN * PATCH, 4 * SPAN * PATCH).astype(jnp.float32)
    slot_mean = totals[..., 0] / counts
    inv_spread = lax.rsqrt(totals[..., 1] / counts - slot_mean * slot_mean + EPSILON)
    normed = (grouped - slot_mean[..., None]) * inv_spread[..., None]
    short_in = normed[:, :, :SHORT_SLOTS].reshape(device_count, short_rows, PATCH)
    long_in = normed[:, :, SHORT_SLOTS:].reshape(device_count * long_rows, PATCH)
    causal = jnp.arange(SPAN)[None, :] <= jnp.arange(SPAN)[:, None]

    def short_device(inputs):
        embedded, projected = embed_project(inputs, params)
        head_split = projected.reshape(SHORT_SLOTS, SPAN, 3, HEADS, HEAD_DIM)
        mixture = attend(head_split[:, :, 0], head_split[:, :, 1], head_split[:, :, 2], causal)
        return finish(embedded, mixture.reshape(short_rows, D), params)
    short_out = lax.map(jax.checkpoint(short_device), short_in)
    long_embedded, long_projected = embed_project(long_in, params)
    head_split = long_projected.reshape(N_FSDP, N_DP, LONG_SLOTS, SPAN, 3, HEADS, HEAD_DIM)
    key_own = head_split[:, :, :, :, 1]
    value_own = head_split[:, :, :, :, 2]
    key_all = jnp.concatenate([key_own] + [jnp.roll(key_own, shift_by, axis=0) for shift_by in (1, 2, 3)], 3)
    value_all = jnp.concatenate([value_own] + [jnp.roll(value_own, shift_by, axis=0) for shift_by in (1, 2, 3)], 3)
    own_mask = jnp.broadcast_to(causal, (N_FSDP, N_DP, LONG_SLOTS, SPAN, SPAN))
    prior_masks = [jnp.broadcast_to((shift_by <= quarter)[..., None, None], own_mask.shape) for shift_by in (1, 2, 3)]
    allowed = jnp.concatenate([own_mask] + prior_masks, -1)
    mixture = attend(head_split[:, :, :, :, 0], key_all, value_all, allowed)
    long_out = finish(long_embedded, mixture.reshape(device_count * long_rows, D), params)
    merged = jnp.concatenate([short_out.reshape(N_FSDP, N_DP, short_rows, D), long_out.reshape(N_FSDP, N_DP, long_rows, D)], 2)
    return merged.reshape(device_count * (short_rows + long_rows), D)

def reference(series_values, quarter_index, patch_weight, heads_in, heads_out, expand_weight, reduce_weight, norm_gains, bias_rows, expand_bias, cotangent):
    quarter = quarter_index.reshape(N_FSDP, N_DP, LONG_SLOTS)
    params = tuple((member.astype(jnp.float32) for member in (patch_weight, heads_in, heads_out, expand_weight, reduce_weight, norm_gains, bias_rows, expand_bias)))

    def forward(values, *weights_in):
        return layer_forward(values, quarter, weights_in)
    output, pullback = jax.vjp(forward, series_values, *params)
    gradients = pullback(cotangent.astype(jnp.float32))
    return (output.astype(jnp.bfloat16), gradients[0], gradients[1], gradients[2], gradients[3], gradients[4], gradients[5], gradients[6], gradients[7], gradients[8])
```

```python
import jax
import jax.numpy as jnp
from jax import lax
from jax.experimental import pallas as pl
from jax.experimental.pallas import tpu as pltpu
from jax.sharding import PartitionSpec as P

D = 1024
HEADS = 8
HEAD_DIM = 128
PATCH = 96
SPAN = 15
SHORT_SLOTS = 48
LONG_SLOTS = 4
CHUNK = 16 * SPAN

EPSILON = 1e-05
NEG_LARGE = -1e30
SCALE = HEAD_DIM ** (-0.5)
AXES = ("fsdp", "dp")
F32 = jnp.float32
BF16 = jnp.bfloat16


class Place:
    def __init__(self):
        self.fsdp = lax.axis_size("fsdp")
        self.dp = lax.axis_size("dp")
        self.tuned = self.fsdp == 8 and self.dp == 4
        self.f = lax.axis_index("fsdp")
        d = lax.axis_index("dp")
        self.line = self.fsdp // 2
        self.z, self.y = self.f // 2, self.f % 2
        self.x, self.c = d // 2, d % 2

    def move(self, value, line=0, pair=0, side=0, core=0):
        pairs = []
        for f in range(self.fsdp):
            for d in range(self.dp):
                z, y, x, c = f // 2, f % 2, d // 2, d % 2
                to_f = ((z + line) % self.line) * 2 + (y ^ pair)
                to_d = (x ^ side) * 2 + (c ^ core)
                pairs.append((f * self.dp + d, to_f * self.dp + to_d))
        return lax.ppermute(value, AXES, pairs)

    def along(self, value, steps):
        pairs = [(s, (s + steps) % self.fsdp) for s in range(self.fsdp)]
        return lax.ppermute(value, "fsdp", pairs)


def pick(value, index, axis):
    return lax.dynamic_index_in_dim(value, index, axis, keepdims=False)


def assemble_kernel(rows, info, own, a1, a2, a3, b1, b2, n1, n2, n3, m1, m2, out, sem):
    z, y, x, c = info[0], info[1], info[2], info[3]
    half, quarter = rows // 2, rows // 4
    jobs = []

    def add(src, src_row, dst_row, count):
        jobs.append(
            pltpu.make_async_copy(
                src.at[pl.ds(src_row, count), :],
                out.at[pl.ds(pl.multiple_of(dst_row, 16), count), :],
                sem.at[len(jobs)],
            )
        )

    add(own, 0, (z * 2 + y) * rows, rows)
    for step, (mine, other) in enumerate(((a1, n1), (a2, n2), (a3, n3)), 1):
        base = (lax.rem(z + 4 - step, 4) * 2 + y) * rows
        add(mine, 0, base + c * half, half)
        add(other, 0, base + (1 - c) * half, half)
    for step in range(4):
        base = (lax.rem(z + 4 - step, 4) * 2 + (1 - y)) * rows
        for core, side, src in ((c, x, b1), (c, 1 - x, b2), (1 - c, x, m1), (1 - c, 1 - x, m2)):
            add(src, step * quarter, base + core * half + side * quarter, quarter)
    for job in jobs:
        job.start()
    for job in jobs:
        job.wait()


def gather_weight(place, info, shard):
    rows, columns = shard.shape
    if not place.tuned:
        return lax.all_gather(shard, "fsdp", axis=0, tiled=True)
    half, quarter = rows // 2, rows // 4
    a0 = lax.dynamic_slice_in_dim(shard, place.c * half, half, 0)
    a1 = place.move(a0, line=1)
    a2 = place.move(a1, line=1)
    a3 = place.move(a2, line=1)
    piece = lambda a: lax.dynamic_slice_in_dim(a, place.x * quarter, quarter, 0)
    b1 = place.move(jnp.concatenate([piece(a) for a in (a0, a1, a2, a3)], 0), pair=1)
    b2 = place.move(b1, side=1)
    n1, n2, n3, m1, m2 = [place.move(a, core=1) for a in (a1, a2, a3, b1, b2)]
    return pl.pallas_call(
        lambda *refs: assemble_kernel(rows, *refs),
        out_shape=jax.ShapeDtypeStruct((8 * rows, columns), shard.dtype),
        in_specs=[pl.BlockSpec(memory_space=pltpu.SMEM)]
        + [pl.BlockSpec(memory_space=pl.ANY)] * 11,
        out_specs=pl.BlockSpec(memory_space=pltpu.VMEM),
        scratch_shapes=[pltpu.SemaphoreType.DMA((23,))],
        cost_estimate=pl.CostEstimate(
            flops=0, bytes_accessed=32 * rows * columns, transcendentals=0
        ),
        name="assemble",
    )(info, shard, a1, a2, a3, b1, b2, n1, n2, n3, m1, m2)


def gather_small(place, packed):
    if not place.tuned:
        return lax.all_gather(packed, "fsdp", axis=0, tiled=False)
    other = place.move(packed, pair=1)
    low = jnp.where(place.y == 0, packed, other)
    high = jnp.where(place.y == 0, other, packed)
    both = jnp.stack([low, high])
    steps = jnp.stack([both] + [place.move(both, line=k) for k in (1, 2, 3)])
    ordered = [pick(steps, (place.z + 4 - line) % 4, 0) for line in range(4)]
    return jnp.concatenate(ordered, 0)


def reduce_weight(place, grad):
    if not place.tuned:
        part = lax.psum_scatter(grad.astype(F32), "fsdp", scatter_dimension=0, tiled=True)
        return lax.psum(part.astype(BF16), "dp").astype(F32)
    rows, columns = grad.shape[0] // 8, grad.shape[1]
    half = rows // 2
    z, y, x, c = place.z, place.y, place.x, place.c
    view = grad.reshape(8, 2, half, columns)
    got = place.move(pick(view, 1 - c, 1), core=1)
    one = (pick(view, c, 1).astype(F32) + got.astype(F32)).astype(BF16)
    one = one.reshape(4, 2, half, columns)
    got = place.move(pick(one, 1 - y, 1), pair=1)
    two = (pick(one, y, 1).astype(F32) + got.astype(F32)).astype(BF16)
    three = pick(two, z, 0).astype(F32)
    for k in (1, 2, 3):
        three = three + place.move(pick(two, (z + k) % 4, 0), line=k).astype(F32)
    three = three.astype(BF16)
    four = (three.astype(F32) + place.move(three, side=1).astype(F32)).astype(BF16)
    got = place.move(four, core=1)
    low = jnp.where(c == 0, four, got)
    high = jnp.where(c == 0, got, four)
    return jnp.concatenate([low, high], 0).astype(F32)


def reduce_small(place, packed):
    if not place.tuned:
        part = lax.psum_scatter(packed, "fsdp", scatter_dimension=0, tiled=True)[0]
        return lax.psum(part, "dp")
    z, y = place.z, place.y
    packed = packed.astype(BF16)
    one = packed.astype(F32)
    for side, core in ((0, 1), (1, 0), (1, 1)):
        one = one + place.move(packed, side=side, core=core).astype(F32)
    one = one.astype(BF16).reshape(4, 2, *packed.shape[1:])
    got = place.move(pick(one, 1 - y, 1), pair=1)
    two = (pick(one, y, 1).astype(F32) + got.astype(F32)).astype(BF16)
    three = pick(two, z, 0).astype(F32)
    for k in (1, 2, 3):
        three = three + place.move(pick(two, (z + k) % 4, 0), line=k).astype(F32)
    return three


def layer_norm(inputs, gain_row, shift_row):
    center = inputs - jnp.mean(inputs, axis=-1, keepdims=True)
    spread = jnp.mean(center * center, axis=-1, keepdims=True)
    return center * lax.rsqrt(spread + EPSILON) * gain_row + shift_row


def exact_gelu(inputs):
    return jax.nn.gelu(inputs, approximate=False)


def dot_t(a, b):
    return lax.dot_general(a, b, (((1,), (1,)), ((), ())), preferred_element_type=F32)


def dot_l(a, b):
    return lax.dot_general(a, b, (((0,), (0,)), ((), ())), preferred_element_type=F32)


def dot_n(a, b):
    return lax.dot_general(a, b, (((1,), (0,)), ((), ())), preferred_element_type=F32)


def slot_of(index):
    return jnp.floor((index.astype(F32) + 0.5) * (1.0 / SPAN))


def short_bias():
    row = lax.broadcasted_iota(jnp.int32, (CHUNK, CHUNK), 0)
    column = lax.broadcasted_iota(jnp.int32, (CHUNK, CHUNK), 1)
    keep = (slot_of(row) == slot_of(column)) & (column <= row)
    return jnp.where(keep, 0.0, NEG_LARGE)


def short_forward_kernel(q_ref, k_ref, v_ref, out_ref, bias_ref):
    @pl.when(pl.program_id(0) == 0)
    def _():
        bias_ref[...] = short_bias()

    bias = bias_ref[...]
    for chunk in range(SHORT_SLOTS * SPAN // CHUNK):
        rows = pl.ds(chunk * CHUNK, CHUNK)
        scores = dot_t(q_ref[rows, :], k_ref[rows, :]) * SCALE + bias
        top = jnp.max(scores, axis=-1, keepdims=True)
        weights = jnp.exp(scores - top)
        total = jnp.sum(weights, axis=-1, keepdims=True)
        low = (weights * (1.0 / total)).astype(BF16)
        out_ref[rows, :] = dot_n(low, v_ref[rows, :]).astype(BF16)


def short_forward(projected):
    rows = projected.shape[0]
    short_rows = SHORT_SLOTS * SPAN
    block = lambda part: pl.BlockSpec((short_rows, HEAD_DIM), lambda h: (0, part * HEADS + h))
    return pl.pallas_call(
        short_forward_kernel,
        grid=(HEADS,),
        out_shape=jax.ShapeDtypeStruct((rows, D), BF16),
        in_specs=[block(0), block(1), block(2)],
        out_specs=block(0),
        scratch_shapes=[pltpu.VMEM((CHUNK, CHUNK), F32)],
        cost_estimate=pl.CostEstimate(
            flops=4 * short_rows * CHUNK * D,
            bytes_accessed=8 * rows * D,
            transcendentals=short_rows * CHUNK * HEADS,
        ),
        name="short_forward",
    )(projected, projected, projected)


def short_backward_kernel(q_ref, k_ref, v_ref, g_ref, out_ref, bias_ref):
    head = pl.program_id(0)

    @pl.when(head == 0)
    def _():
        bias_ref[...] = short_bias()

    bias = bias_ref[...]
    lanes = lambda part: pl.ds(pl.multiple_of((part * HEADS + head) * HEAD_DIM, HEAD_DIM), HEAD_DIM)
    for chunk in range(SHORT_SLOTS * SPAN // CHUNK):
        rows = pl.ds(chunk * CHUNK, CHUNK)
        query, key, grad = q_ref[rows, :], k_ref[rows, :], g_ref[rows, :]
        scores = dot_t(query, key) * SCALE + bias
        top = jnp.max(scores, axis=-1, keepdims=True)
        weights = jnp.exp(scores - top)
        probs = weights * (1.0 / jnp.sum(weights, axis=-1, keepdims=True))
        grad_probs = dot_t(grad, v_ref[rows, :])
        inner = jnp.sum(probs * grad_probs, axis=-1, keepdims=True)
        grad_scores = (probs * (grad_probs - inner)).astype(BF16)
        out_ref[rows, lanes(0)] = (dot_n(grad_scores, key) * SCALE).astype(BF16)
        out_ref[rows, lanes(1)] = (dot_l(grad_scores, query) * SCALE).astype(BF16)
        out_ref[rows, lanes(2)] = dot_l(probs.astype(BF16), grad).astype(BF16)


def short_backward(projected, grad_mixture):
    rows = projected.shape[0]
    short_rows = SHORT_SLOTS * SPAN
    block = lambda part: pl.BlockSpec((short_rows, HEAD_DIM), lambda h: (0, part * HEADS + h))
    return pl.pallas_call(
        short_backward_kernel,
        grid=(HEADS,),
        out_shape=jax.ShapeDtypeStruct((rows, 3 * D), BF16),
        in_specs=[block(0), block(1), block(2), block(0)],
        out_specs=pl.BlockSpec((rows, 3 * D), lambda h: (0, 0)),
        scratch_shapes=[pltpu.VMEM((CHUNK, CHUNK), F32)],
        cost_estimate=pl.CostEstimate(
            flops=10 * short_rows * CHUNK * D,
            bytes_accessed=14 * rows * D,
            transcendentals=short_rows * CHUNK * HEADS,
        ),
        name="short_backward",
    )(projected, projected, projected, grad_mixture)


def long_biases(quarter_ref):
    rows = LONG_SLOTS * SPAN
    row = lax.broadcasted_iota(jnp.int32, (rows, rows), 0)
    column = lax.broadcasted_iota(jnp.int32, (rows, rows), 1)
    slot = slot_of(row)
    same = slot == slot_of(column)
    quarter = jnp.zeros((rows, rows), jnp.int32)
    for index in range(LONG_SLOTS):
        quarter = jnp.where(slot == float(index), quarter_ref[index], quarter)
    keeps = [same & (column <= row)] + [same & (step <= quarter) for step in (1, 2, 3)]
    return [jnp.where(keep, 0.0, NEG_LARGE) for keep in keeps]


def long_probs(query, keys, biases):
    scores = [dot_t(query, key) * SCALE + bias for key, bias in zip(keys, biases)]
    top = scores[0]
    for member in scores[1:]:
        top = jnp.maximum(top, member)
    top = jnp.max(top, axis=-1, keepdims=True)
    weights = [jnp.exp(member - top) for member in scores]
    total = weights[0] + weights[1] + weights[2] + weights[3]
    scale = 1.0 / jnp.sum(total, axis=-1, keepdims=True)
    return [member * scale for member in weights]


def long_forward_kernel(quarter_ref, q, k0, v0, k1, v1, k2, v2, k3, v3, out_ref):
    biases = long_biases(quarter_ref)
    probs = long_probs(q[...], [k[...] for k in (k0, k1, k2, k3)], biases)
    total = None
    for member, value in zip(probs, (v0, v1, v2, v3)):
        part = dot_n(member.astype(BF16), value[...])
        total = part if total is None else total + part
    out_ref[...] = total.astype(BF16)


def long_specs(rows):
    block = lambda part: pl.BlockSpec((rows, HEAD_DIM), lambda h: (0, part * HEADS + h))
    return [block(0), block(1), block(2)] + [block(0), block(1)] * 3


def long_forward(quarter_index, own, priors):
    rows = own.shape[0]
    spread = [member for prior in priors for member in (prior, prior)]
    return pl.pallas_call(
        long_forward_kernel,
        grid=(HEADS,),
        out_shape=jax.ShapeDtypeStruct((rows, D), BF16),
        in_specs=[pl.BlockSpec(memory_space=pltpu.SMEM)] + long_specs(rows),
        out_specs=pl.BlockSpec((rows, HEAD_DIM), lambda h: (0, h)),
        cost_estimate=pl.CostEstimate(
            flops=16 * rows * rows * D, bytes_accessed=20 * rows * D, transcendentals=0
        ),
        name="long_forward",
    )(quarter_index, own, own, own, *spread)


def long_backward_kernel(
    quarter_ref, q, k0, v0, k1, v1, k2, v2, k3, v3, g, dq_ref, own_ref, s1_ref, s2_ref, s3_ref
):
    biases = long_biases(quarter_ref)
    query, grad = q[...], g[...]
    keys = [k[...] for k in (k0, k1, k2, k3)]
    probs = long_probs(query, keys, biases)
    grads = [dot_t(grad, value[...]) for value in (v0, v1, v2, v3)]
    inner = None
    for member, part in zip(probs, grads):
        inner = member * part if inner is None else inner + member * part
    inner = jnp.sum(inner, axis=-1, keepdims=True)
    total = None
    for index, out in enumerate((own_ref, s1_ref, s2_ref, s3_ref)):
        grad_scores = (probs[index] * (grads[index] - inner)).astype(BF16)
        part = dot_n(grad_scores, keys[index])
        total = part if total is None else total + part
        out[0, :, :] = (dot_l(grad_scores, query) * SCALE).astype(out.dtype)
        out[1, :, :] = dot_l(probs[index].astype(BF16), grad).astype(out.dtype)
    dq_ref[...] = (total * SCALE).astype(BF16)


def long_backward(quarter_index, own, priors, grad_mixture):
    rows = own.shape[0]
    spread = [member for prior in priors for member in (prior, prior)]
    flat = pl.BlockSpec((rows, HEAD_DIM), lambda h: (0, h))
    pair = pl.BlockSpec((2, rows, HEAD_DIM), lambda h: (0, 0, h))
    return pl.pallas_call(
        long_backward_kernel,
        grid=(HEADS,),
        out_shape=[jax.ShapeDtypeStruct((rows, D), BF16)]
        + [jax.ShapeDtypeStruct((2, rows, D), kind) for kind in (F32, BF16, BF16, BF16)],
        in_specs=[pl.BlockSpec(memory_space=pltpu.SMEM)] + long_specs(rows) + [flat],
        out_specs=[flat] + [pair] * 4,
        cost_estimate=pl.CostEstimate(
            flops=40 * rows * rows * D, bytes_accessed=40 * rows * D, transcendentals=0
        ),
        name="long_backward",
    )(quarter_index, own, own, own, *spread, grad_mixture)


def body(
    series_values,
    quarter_index,
    patch_weight,
    heads_in,
    heads_out,
    expand_weight,
    reduce_weight_shard,
    norm_gains,
    bias_rows,
    expand_bias,
    cotangent,
):
    place = Place()
    fsdp = place.fsdp
    width = patch_weight.shape[1]
    info = jnp.stack([place.z, place.y, place.x, place.c]).astype(jnp.int32)
    row_count = series_values.shape[0]
    slot_count = row_count // SPAN
    short_rows = SHORT_SLOTS * SPAN
    long_rows = row_count - short_rows

    grouped = series_values.reshape(slot_count, SPAN * PATCH)
    slot_sums = jnp.stack([jnp.sum(grouped, 1), jnp.sum(grouped * grouped, 1)], 1)
    long_sums = slot_sums[SHORT_SLOTS:]
    rows_of = lambda a: a.astype(F32).reshape(-1, width)
    pieces = [rows_of(a) for a in (patch_weight, norm_gains, bias_rows, expand_bias)]
    small = gather_small(place, jnp.concatenate(pieces, 0))
    chain = gather_small(place, long_sums)
    offset = jnp.arange(fsdp)[:, None] - place.f + quarter_index[None, :]
    member = ((offset + fsdp) % fsdp < 4).astype(F32)[:, :, None]
    chain_sum = jnp.sum(chain * member, 0)

    wide = lambda low, high: small[:, low:high].transpose(1, 0, 2).reshape(high - low, D)
    patch_all = wide(0, PATCH).astype(BF16)
    gains_all = wide(PATCH, PATCH + 2)
    biases_all = wide(PATCH + 2, PATCH + 6)
    expand_shift = small[:, PATCH + 6 :].reshape(-1)

    heads_in_all = gather_weight(place, info, heads_in)
    heads_out_all = gather_weight(place, info, heads_out)
    reduce_all = gather_weight(place, info, reduce_weight_shard)
    expand_all = gather_weight(place, info, expand_weight)

    totals = jnp.concatenate([slot_sums[:SHORT_SLOTS], chain_sum], 0)
    counts = jnp.where(jnp.arange(slot_count) < SHORT_SLOTS, SPAN * PATCH, 4 * SPAN * PATCH).astype(
        F32
    )
    slot_mean = totals[:, 0] / counts
    inv_spread = lax.rsqrt(totals[:, 1] / counts - slot_mean * slot_mean + EPSILON)
    normed_slots = (grouped - slot_mean[:, None]) * inv_spread[:, None]
    normed_low = normed_slots.reshape(row_count, PATCH).astype(BF16)
    embedded = dot_n(normed_low, patch_all) + biases_all[0]
    first_value, first_back = jax.vjp(layer_norm, embedded, gains_all[0], biases_all[1])
    first_norm = first_value.astype(BF16)
    projected = dot_n(first_norm, heads_in_all).astype(BF16)

    own_long = projected[short_rows:]
    long_pairs = own_long[:, D:]
    priors = [place.along(long_pairs, step) for step in (1, 2, 3)]
    mixed_short = short_forward(projected)
    mixed_long = long_forward(quarter_index, own_long, priors)
    mixed_all = lax.dynamic_update_slice(mixed_short, mixed_long, (short_rows, 0))
    middle = embedded + dot_n(mixed_all, heads_out_all)
    second_value, second_back = jax.vjp(layer_norm, middle, gains_all[1], biases_all[2])
    second_norm = second_value.astype(BF16)

    pre_act = dot_n(second_norm, expand_all) + expand_shift
    act_value, gelu_back = jax.vjp(exact_gelu, pre_act)
    activation = act_value.astype(BF16)
    layer_output = (middle + dot_n(activation, reduce_all) + biases_all[3]).astype(BF16)

    grad_reduce = reduce_weight(place, dot_l(activation, cotangent).astype(BF16))
    grad_act = dot_t(cotangent, reduce_all)
    grad_pre = gelu_back(grad_act)[0].astype(BF16)
    grad_expand = reduce_weight(place, dot_l(second_norm, grad_pre).astype(BF16))
    grad_expand_bias = jnp.sum(grad_pre.astype(F32), 0)
    grad_second = dot_t(grad_pre, expand_all)
    middle_back, gain_two, shift_two = second_back(grad_second)
    grad_middle = cotangent.astype(F32) + middle_back
    grad_branch = grad_middle.astype(BF16)
    grad_heads_out = reduce_weight(place, dot_l(mixed_all, grad_branch).astype(BF16))
    grad_mixture = dot_t(grad_branch, heads_out_all).astype(BF16)

    long_query, own_grads, *sent = long_backward(
        quarter_index, own_long, priors, grad_mixture[short_rows:]
    )
    for step, sent_back in zip((1, 2, 3), sent):
        own_grads = own_grads + place.along(sent_back, -step).astype(F32)
    own_grads = own_grads.astype(BF16)
    grad_short = short_backward(projected, grad_mixture)
    grad_long = jnp.concatenate([long_query, own_grads[0], own_grads[1]], 1)
    grad_projected = lax.dynamic_update_slice(grad_short, grad_long, (short_rows, 0))
    grad_heads_in = reduce_weight(place, dot_l(first_norm, grad_projected).astype(BF16))
    grad_first = dot_t(grad_projected, heads_in_all)
    embed_back, gain_one, shift_one = first_back(grad_first)
    grad_embedded = (grad_middle + embed_back).astype(BF16)
    grad_patch = dot_l(normed_low, grad_embedded)
    shift_zero = jnp.sum(grad_embedded.astype(F32), 0)
    grad_normed = dot_t(grad_embedded, patch_all).reshape(slot_count, SPAN * PATCH)
    slot_grads = jnp.stack([jnp.sum(grad_normed, 1), jnp.sum(grad_normed * normed_slots, 1)], 1)
    chain_grads = gather_small(place, slot_grads[SHORT_SLOTS:])
    chain_grad = jnp.sum(chain_grads * member, 0)
    grad_totals = jnp.concatenate([slot_grads[:SHORT_SLOTS], chain_grad], 0)
    series_grad = (
        inv_spread[:, None]
        * (
            grad_normed
            - grad_totals[:, 0:1] / counts[:, None]
            - normed_slots * grad_totals[:, 1:2] / counts[:, None]
        )
    ).reshape(row_count, PATCH)
    shift_three = jnp.sum(cotangent.astype(F32), 0)

    split = lambda a: a.reshape(-1, fsdp, width).transpose(1, 0, 2)
    packed = jnp.concatenate(
        [
            split(grad_patch),
            split(jnp.stack([gain_one, gain_two, shift_zero, shift_one, shift_two, shift_three])),
            grad_expand_bias.reshape(fsdp, -1, width),
        ],
        1,
    )
    small_grads = reduce_small(place, packed)
    return (
        layer_output,
        series_grad,
        small_grads[:PATCH],
        grad_heads_in,
        grad_heads_out,
        grad_expand,
        grad_reduce,
        small_grads[PATCH : PATCH + 2],
        small_grads[PATCH + 2 : PATCH + 6],
        small_grads[PATCH + 6 :].reshape(-1),
    )


def solution(mesh):
    in_specs = (
        P(("fsdp", "dp"), None),
        P(("fsdp", "dp")),
        P(None, "fsdp"),
        P("fsdp", None),
        P("fsdp", None),
        P("fsdp", None),
        P("fsdp", None),
        P(None, "fsdp"),
        P(None, "fsdp"),
        P("fsdp"),
        P(("fsdp", "dp"), None),
    )
    out_specs = (
        P(("fsdp", "dp"), None),
        P(("fsdp", "dp"), None),
        P(None, "fsdp"),
        P("fsdp", None),
        P("fsdp", None),
        P("fsdp", None),
        P("fsdp", None),
        P(None, "fsdp"),
        P(None, "fsdp"),
        P("fsdp"),
    )
    return jax.shard_map(body, mesh=mesh, in_specs=in_specs, out_specs=out_specs, check_vma=False)
```

```python
import jax
import jax.numpy as jnp
from jax import lax
from jax.experimental import pallas as pl
from jax.experimental.pallas import tpu as pltpu
from jax.sharding import PartitionSpec as P

D = 1024
HEADS = 8
HEAD_DIM = 128
PATCH = 96
SPAN = 15
SHORT_SLOTS = 48
LONG_SLOTS = 4
CHUNK = 16 * SPAN
GROUPS = 2
GROUP = HEADS // GROUPS
WIDE = 3 * GROUP * HEAD_DIM

EPSILON = 1e-05
NEG_LARGE = -1e30
SCALE = HEAD_DIM ** (-0.5)
AXES = ("fsdp", "dp")
F32 = jnp.float32
BF16 = jnp.bfloat16


class Place:
    def __init__(self):
        self.fsdp = lax.axis_size("fsdp")
        self.dp = lax.axis_size("dp")
        self.tuned = self.fsdp == 8 and self.dp == 4
        self.f = lax.axis_index("fsdp")
        d = lax.axis_index("dp")
        self.line = self.fsdp // 2
        self.z, self.y = self.f // 2, self.f % 2
        self.x, self.c = d // 2, d % 2

    def move(self, value, line=0, pair=0, side=0, core=0):
        pairs = []
        for f in range(self.fsdp):
            for d in range(self.dp):
                z, y, x, c = f // 2, f % 2, d // 2, d % 2
                to_f = ((z + line) % self.line) * 2 + (y ^ pair)
                to_d = (x ^ side) * 2 + (c ^ core)
                pairs.append((f * self.dp + d, to_f * self.dp + to_d))
        return lax.ppermute(value, AXES, pairs)

    def along(self, value, steps):
        pairs = [(s, (s + steps) % self.fsdp) for s in range(self.fsdp)]
        return lax.ppermute(value, "fsdp", pairs)


def pick(value, index, axis):
    return lax.dynamic_index_in_dim(value, index, axis, keepdims=False)


class Chain:
    def __init__(self, place, stages):
        self.place, self.stages, self.result = place, stages, None
        self.sends = self.take(None)

    def take(self, got):
        try:
            return self.stages.send(got)
        except StopIteration as end:
            self.result = end.value
            return []

    def launch(self, arrays):
        if self.sends:
            got = [self.place.move(a, **where) for a, (_, where) in zip(arrays, self.sends)]
            self.sends = self.take(got)

    def finish(self):
        while self.sends:
            self.launch([a for a, _ in self.sends])
        return self.result


def tied(value, *chains):
    pending = [[a for a, _ in chain.sends] for chain in chains]
    if not any(pending):
        return value
    value, pending = lax.optimization_barrier((value, pending))
    for chain, arrays in zip(chains, pending):
        chain.launch(arrays)
    return value


def assemble_kernel(rows, info, own, *refs):
    z, y, x, c = info[0], info[1], info[2], info[3]
    half, quarter = rows // 2, rows // 4
    *parts, out, sem = refs
    near, far = parts[:6], parts[6:]
    count = len(far) // 4
    each = 4 // count
    jobs = []

    def add(src, src_row, dst_row, count):
        jobs.append(
            pltpu.make_async_copy(
                src.at[pl.ds(src_row, count), :],
                out.at[pl.ds(pl.multiple_of(dst_row, 16), count), :],
                sem.at[len(jobs)],
            )
        )

    add(own, 0, (z * 2 + y) * rows, rows)
    for step in (1, 2, 3):
        base = (lax.rem(z + 4 - step, 4) * 2 + y) * rows
        add(near[step - 1], 0, base + c * half, half)
        add(near[step + 2], 0, base + (1 - c) * half, half)
    for step in range(4):
        base = (lax.rem(z + 4 - step, 4) * 2 + (1 - y)) * rows
        for kind, (core, side) in enumerate(((c, x), (c, 1 - x), (1 - c, x), (1 - c, 1 - x))):
            src = far[kind * count + step // each]
            add(src, (step % each) * quarter, base + core * half + side * quarter, quarter)
    for job in jobs:
        job.start()
    for job in jobs:
        job.wait()


def assemble(info, shard, near, far):
    rows, columns = shard.shape
    parts = list(near) + list(far)
    return pl.pallas_call(
        lambda *refs: assemble_kernel(rows, *refs),
        out_shape=jax.ShapeDtypeStruct((8 * rows, columns), shard.dtype),
        in_specs=[pl.BlockSpec(memory_space=pltpu.SMEM)]
        + [pl.BlockSpec(memory_space=pl.ANY)] * (1 + len(parts)),
        out_specs=pl.BlockSpec(memory_space=pltpu.VMEM),
        scratch_shapes=[pltpu.SemaphoreType.DMA((23,))],
        cost_estimate=pl.CostEstimate(
            flops=0, bytes_accessed=32 * rows * columns, transcendentals=0
        ),
        name="assemble",
    )(info, shard, *parts)


def gather_stages(place, info, shard):
    if not place.tuned:
        return lax.all_gather(shard, "fsdp", axis=0, tiled=True)
    half, quarter = shard.shape[0] // 2, shard.shape[0] // 4
    own = lax.dynamic_slice_in_dim(shard, place.c * half, half, 0)
    piece = lambda a: lax.dynamic_slice_in_dim(a, place.x * quarter, quarter, 0)
    a = yield [(own, dict(line=k)) for k in (1, 2, 3)]
    mine = jnp.concatenate([piece(m) for m in (own, *a)], 0)
    b1, *n = yield [(mine, dict(pair=1))] + [(m, dict(core=1)) for m in a]
    b2, m1 = yield [(b1, dict(side=1)), (b1, dict(core=1))]
    (m2,) = yield [(b2, dict(core=1))]
    return assemble(info, shard, [*a, *n], [b1, b2, m1, m2])


def gather_first(place, info, shard, chains):
    if not place.tuned:
        return lax.all_gather(shard, "fsdp", axis=0, tiled=True)
    half, quarter = shard.shape[0] // 2, shard.shape[0] // 4
    own = lax.dynamic_slice_in_dim(shard, place.c * half, half, 0)
    piece = lambda a: lax.dynamic_slice_in_dim(a, place.x * quarter, quarter, 0)
    move = place.move
    a1 = move(own, line=1)
    b01 = move(jnp.concatenate([piece(own), piece(a1)], 0), pair=1)
    a2 = move(a1, line=1)
    n1 = move(a1, core=1)
    a2 = tied(a2, chains[0])
    a3 = move(a2, line=1)
    x01 = move(b01, side=1)
    n2, m01 = move(a2, core=1), move(b01, core=1)
    a3 = tied(a3, chains[1])
    b23 = move(jnp.concatenate([piece(a2), piece(a3)], 0), pair=1)
    n3, w01 = move(a3, core=1), move(x01, core=1)
    b23 = tied(b23, chains[2])
    x23, m23 = move(b23, side=1), move(b23, core=1)
    w23 = move(x23, core=1)
    return assemble(info, shard, [a1, a2, a3, n1, n2, n3], [b01, b23, x01, x23, m01, m23, w01, w23])


def gather_small(place, packed):
    if not place.tuned:
        return lax.all_gather(packed, "fsdp", axis=0, tiled=False)
    other = place.move(packed, pair=1)
    low = jnp.where(place.y == 0, packed, other)
    high = jnp.where(place.y == 0, other, packed)
    both = jnp.stack([low, high])
    steps = jnp.stack([both] + [place.move(both, line=k) for k in (1, 2, 3)])
    ordered = [pick(steps, (place.z + 4 - line) % 4, 0) for line in range(4)]
    return jnp.concatenate(ordered, 0)


def plus(a, *others):
    total = a.astype(F32)
    for other in others:
        total = total + other.astype(F32)
    return total.astype(BF16)


def reduce_stages(place, grad, side_first):
    if not place.tuned:
        part = lax.psum_scatter(grad.astype(F32), "fsdp", scatter_dimension=0, tiled=True)
        return lax.psum(part.astype(BF16), "dp").astype(F32)
    rows, columns = grad.shape[0] // 8, grad.shape[1]
    half, quarter = rows // 2, rows // 4
    z, y, x, c = place.z, place.y, place.x, place.c
    value = grad.reshape(8, 2, half, columns)
    (got,) = yield [(pick(value, 1 - c, 1), dict(core=1))]
    value = plus(pick(value, c, 1), got)
    if side_first:
        value = value.reshape(8, 2, quarter, columns)
        (got,) = yield [(pick(value, 1 - x, 1), dict(side=1))]
        value = plus(pick(value, x, 1), got)
    value = value.reshape(4, 2, *value.shape[1:])
    (got,) = yield [(pick(value, 1 - y, 1), dict(pair=1))]
    value = plus(pick(value, y, 1), got)
    got = yield [(pick(value, (z + k) % 4, 0), dict(line=k)) for k in (1, 2, 3)]
    value = plus(pick(value, z, 0), *got)
    (got,) = yield [(value, dict(side=1))]
    if side_first:
        low, high = jnp.where(x == 0, value, got), jnp.where(x == 0, got, value)
        value = jnp.concatenate([low, high], 0)
    else:
        value = plus(value, got)
    (got,) = yield [(value, dict(core=1))]
    low, high = jnp.where(c == 0, value, got), jnp.where(c == 0, got, value)
    return jnp.concatenate([low, high], 0).astype(F32)


def reduce_small(place, packed):
    if not place.tuned:
        part = lax.psum_scatter(packed, "fsdp", scatter_dimension=0, tiled=True)[0]
        return lax.psum(part, "dp")
    z, y = place.z, place.y
    packed = packed.astype(BF16)
    one = packed.astype(F32)
    for side, core in ((0, 1), (1, 0), (1, 1)):
        one = one + place.move(packed, side=side, core=core).astype(F32)
    one = one.astype(BF16).reshape(4, 2, *packed.shape[1:])
    got = place.move(pick(one, 1 - y, 1), pair=1)
    two = (pick(one, y, 1).astype(F32) + got.astype(F32)).astype(BF16)
    three = pick(two, z, 0).astype(F32)
    for k in (1, 2, 3):
        three = three + place.move(pick(two, (z + k) % 4, 0), line=k).astype(F32)
    return three


def layer_norm(inputs, gain_row, shift_row):
    center = inputs - jnp.mean(inputs, axis=-1, keepdims=True)
    spread = jnp.mean(center * center, axis=-1, keepdims=True)
    return center * lax.rsqrt(spread + EPSILON) * gain_row + shift_row


def exact_gelu(inputs):
    return jax.nn.gelu(inputs, approximate=False)


def dot_t(a, b):
    return lax.dot_general(a, b, (((1,), (1,)), ((), ())), preferred_element_type=F32)


def dot_l(a, b):
    return lax.dot_general(a, b, (((0,), (0,)), ((), ())), preferred_element_type=F32)


def dot_n(a, b):
    return lax.dot_general(a, b, (((1,), (0,)), ((), ())), preferred_element_type=F32)


def slot_of(index):
    return jnp.floor((index.astype(F32) + 0.5) * (1.0 / SPAN))


def short_bias():
    row = lax.broadcasted_iota(jnp.int32, (CHUNK, CHUNK), 0)
    column = lax.broadcasted_iota(jnp.int32, (CHUNK, CHUNK), 1)
    keep = (slot_of(row) == slot_of(column)) & (column <= row)
    return jnp.where(keep, 0.0, NEG_LARGE)


def short_forward_kernel(q_ref, k_ref, v_ref, out_ref, bias_ref):
    @pl.when(pl.program_id(0) == 0)
    def _():
        bias_ref[...] = short_bias()

    bias = bias_ref[...]
    for chunk in range(SHORT_SLOTS * SPAN // CHUNK):
        rows = pl.ds(chunk * CHUNK, CHUNK)
        scores = dot_t(q_ref[rows, :], k_ref[rows, :]) * SCALE + bias
        top = jnp.max(scores, axis=-1, keepdims=True)
        weights = jnp.exp(scores - top)
        total = jnp.sum(weights, axis=-1, keepdims=True)
        low = (weights * (1.0 / total)).astype(BF16)
        out_ref[rows, :] = dot_n(low, v_ref[rows, :]).astype(BF16)


def block_of(rows, part):
    return pl.BlockSpec(
        (rows, HEAD_DIM), lambda h: (0, (h // GROUP) * 3 * GROUP + part * GROUP + h % GROUP)
    )


def short_forward(projected):
    rows = projected.shape[0]
    short_rows = SHORT_SLOTS * SPAN
    return pl.pallas_call(
        short_forward_kernel,
        grid=(HEADS,),
        out_shape=jax.ShapeDtypeStruct((rows, D), BF16),
        in_specs=[block_of(short_rows, part) for part in range(3)],
        out_specs=pl.BlockSpec((short_rows, HEAD_DIM), lambda h: (0, h)),
        scratch_shapes=[pltpu.VMEM((CHUNK, CHUNK), F32)],
        cost_estimate=pl.CostEstimate(
            flops=4 * short_rows * CHUNK * D,
            bytes_accessed=8 * rows * D,
            transcendentals=short_rows * CHUNK * HEADS,
        ),
        name="short_forward",
    )(projected, projected, projected)


def short_backward_kernel(q_ref, k_ref, v_ref, g_ref, out_ref, bias_ref):
    head = pl.program_id(0)

    @pl.when(head == 0)
    def _():
        bias_ref[...] = short_bias()

    bias = bias_ref[...]
    lanes = lambda part: pl.ds(pl.multiple_of((part * GROUP + head) * HEAD_DIM, HEAD_DIM), HEAD_DIM)
    for chunk in range(SHORT_SLOTS * SPAN // CHUNK):
        rows = pl.ds(chunk * CHUNK, CHUNK)
        query, key, grad = q_ref[rows, :], k_ref[rows, :], g_ref[rows, :]
        scores = dot_t(query, key) * SCALE + bias
        top = jnp.max(scores, axis=-1, keepdims=True)
        weights = jnp.exp(scores - top)
        probs = weights * (1.0 / jnp.sum(weights, axis=-1, keepdims=True))
        grad_probs = dot_t(grad, v_ref[rows, :])
        inner = jnp.sum(probs * grad_probs, axis=-1, keepdims=True)
        grad_scores = (probs * (grad_probs - inner)).astype(BF16)
        out_ref[rows, lanes(0)] = (dot_n(grad_scores, key) * SCALE).astype(BF16)
        out_ref[rows, lanes(1)] = (dot_l(grad_scores, query) * SCALE).astype(BF16)
        out_ref[rows, lanes(2)] = dot_l(probs.astype(BF16), grad).astype(BF16)


def short_backward(projected, grad_mixture, group):
    rows = projected.shape[0]
    short_rows = SHORT_SLOTS * SPAN
    block = lambda first: pl.BlockSpec((short_rows, HEAD_DIM), lambda h: (0, first + h))
    return pl.pallas_call(
        short_backward_kernel,
        grid=(GROUP,),
        out_shape=jax.ShapeDtypeStruct((rows, WIDE), BF16),
        in_specs=[block((group * 3 + part) * GROUP) for part in range(3)] + [block(group * GROUP)],
        out_specs=pl.BlockSpec((rows, WIDE), lambda h: (0, 0)),
        scratch_shapes=[pltpu.VMEM((CHUNK, CHUNK), F32)],
        cost_estimate=pl.CostEstimate(
            flops=10 * short_rows * CHUNK * D // GROUPS,
            bytes_accessed=14 * rows * D // GROUPS,
            transcendentals=short_rows * CHUNK * GROUP,
        ),
        name="short_backward",
    )(projected, projected, projected, grad_mixture)


def long_biases(quarter_ref):
    rows = LONG_SLOTS * SPAN
    row = lax.broadcasted_iota(jnp.int32, (rows, rows), 0)
    column = lax.broadcasted_iota(jnp.int32, (rows, rows), 1)
    slot = slot_of(row)
    same = slot == slot_of(column)
    quarter = jnp.zeros((rows, rows), jnp.int32)
    for index in range(LONG_SLOTS):
        quarter = jnp.where(slot == float(index), quarter_ref[index], quarter)
    keeps = [same & (column <= row)] + [same & (step <= quarter) for step in (1, 2, 3)]
    return [jnp.where(keep, 0.0, NEG_LARGE) for keep in keeps]


def long_probs(query, keys, biases):
    scores = [dot_t(query, key) * SCALE + bias for key, bias in zip(keys, biases)]
    top = scores[0]
    for member in scores[1:]:
        top = jnp.maximum(top, member)
    top = jnp.max(top, axis=-1, keepdims=True)
    weights = [jnp.exp(member - top) for member in scores]
    total = weights[0] + weights[1] + weights[2] + weights[3]
    scale = 1.0 / jnp.sum(total, axis=-1, keepdims=True)
    return [member * scale for member in weights]


def long_forward_kernel(quarter_ref, q, k0, v0, k1, v1, k2, v2, k3, v3, out_ref):
    biases = long_biases(quarter_ref)
    probs = long_probs(q[...], [k[...] for k in (k0, k1, k2, k3)], biases)
    total = None
    for member, value in zip(probs, (v0, v1, v2, v3)):
        part = dot_n(member.astype(BF16), value[...])
        total = part if total is None else total + part
    out_ref[...] = total.astype(BF16)


def long_specs(rows):
    sent = lambda part: pl.BlockSpec(
        (rows, HEAD_DIM), lambda h: (0, (h // GROUP) * 2 * GROUP + part * GROUP + h % GROUP)
    )
    return [block_of(rows, part) for part in range(3)] + [sent(0), sent(1)] * 3


def long_forward(quarter_index, own, priors):
    rows = own.shape[0]
    spread = [member for prior in priors for member in (prior, prior)]
    return pl.pallas_call(
        long_forward_kernel,
        grid=(HEADS,),
        out_shape=jax.ShapeDtypeStruct((rows, D), BF16),
        in_specs=[pl.BlockSpec(memory_space=pltpu.SMEM)] + long_specs(rows),
        out_specs=pl.BlockSpec((rows, HEAD_DIM), lambda h: (0, h)),
        cost_estimate=pl.CostEstimate(
            flops=16 * rows * rows * D, bytes_accessed=20 * rows * D, transcendentals=0
        ),
        name="long_forward",
    )(quarter_index, own, own, own, *spread)


def long_backward_kernel(
    quarter_ref, q, k0, v0, k1, v1, k2, v2, k3, v3, g, dq_ref, own_ref, s1_ref, s2_ref, s3_ref
):
    biases = long_biases(quarter_ref)
    query, grad = q[...], g[...]
    keys = [k[...] for k in (k0, k1, k2, k3)]
    probs = long_probs(query, keys, biases)
    grads = [dot_t(grad, value[...]) for value in (v0, v1, v2, v3)]
    inner = None
    for member, part in zip(probs, grads):
        inner = member * part if inner is None else inner + member * part
    inner = jnp.sum(inner, axis=-1, keepdims=True)
    total = None
    for index, out in enumerate((own_ref, s1_ref, s2_ref, s3_ref)):
        grad_scores = (probs[index] * (grads[index] - inner)).astype(BF16)
        part = dot_n(grad_scores, keys[index])
        total = part if total is None else total + part
        out[0, :, :] = (dot_l(grad_scores, query) * SCALE).astype(out.dtype)
        out[1, :, :] = dot_l(probs[index].astype(BF16), grad).astype(out.dtype)
    dq_ref[...] = (total * SCALE).astype(BF16)


def long_backward(quarter_index, own, priors, grad_mixture):
    rows = own.shape[0]
    spread = [member for prior in priors for member in (prior, prior)]
    flat = pl.BlockSpec((rows, HEAD_DIM), lambda h: (0, h))
    pair = pl.BlockSpec((2, rows, HEAD_DIM), lambda h: (0, 0, h))
    return pl.pallas_call(
        long_backward_kernel,
        grid=(HEADS,),
        out_shape=[jax.ShapeDtypeStruct((rows, D), BF16)]
        + [jax.ShapeDtypeStruct((2, rows, D), kind) for kind in (F32, BF16, BF16, BF16)],
        in_specs=[pl.BlockSpec(memory_space=pltpu.SMEM)] + long_specs(rows) + [flat],
        out_specs=[flat] + [pair] * 4,
        cost_estimate=pl.CostEstimate(
            flops=40 * rows * rows * D, bytes_accessed=40 * rows * D, transcendentals=0
        ),
        name="long_backward",
    )(quarter_index, own, own, own, *spread, grad_mixture)


def body(
    series_values,
    quarter_index,
    patch_weight,
    heads_in,
    heads_out,
    expand_weight,
    reduce_weight_shard,
    norm_gains,
    bias_rows,
    expand_bias,
    cotangent,
):
    place = Place()
    fsdp = place.fsdp
    width = patch_weight.shape[1]
    info = jnp.stack([place.z, place.y, place.x, place.c]).astype(jnp.int32)
    row_count = series_values.shape[0]
    slot_count = row_count // SPAN
    short_rows = SHORT_SLOTS * SPAN
    long_rows = row_count - short_rows

    grouped = series_values.reshape(slot_count, SPAN * PATCH)
    slot_sums = jnp.stack([jnp.sum(grouped, 1), jnp.sum(grouped * grouped, 1)], 1)
    rows_of = lambda a: a.astype(F32).reshape(-1, width)
    sums_row = slot_sums[SHORT_SLOTS:].reshape(1, 2 * LONG_SLOTS)
    sums_row = jnp.pad(sums_row, ((0, 7), (0, width - 2 * LONG_SLOTS)))
    pieces = [rows_of(a) for a in (patch_weight, norm_gains, bias_rows, expand_bias)]
    small_rows = sum(piece.shape[0] for piece in pieces)
    small = gather_small(place, jnp.concatenate(pieces + [sums_row], 0))
    chain = small[:, small_rows, : 2 * LONG_SLOTS].reshape(fsdp, LONG_SLOTS, 2)
    offset = jnp.arange(fsdp)[:, None] - place.f + quarter_index[None, :]
    member = ((offset + fsdp) % fsdp < 4).astype(F32)[:, :, None]
    chain_sum = jnp.sum(chain * member, 0)

    wide = lambda low, high: small[:, low:high].transpose(1, 0, 2).reshape(high - low, D)
    patch_all = wide(0, PATCH).astype(BF16)
    gains_all = wide(PATCH, PATCH + 2)
    biases_all = wide(PATCH + 2, PATCH + 6)
    expand_shift = small[:, PATCH + 6 : small_rows].reshape(-1)

    mixed_columns = heads_in.reshape(-1, 3, GROUPS, GROUP * HEAD_DIM).transpose(0, 2, 1, 3)
    gather_out, gather_expand, gather_reduce = [
        Chain(place, gather_stages(place, info, shard))
        for shard in (heads_out, expand_weight, reduce_weight_shard)
    ]
    heads_in_all = gather_first(
        place,
        info,
        mixed_columns.reshape(-1, 3 * D),
        (gather_out, gather_expand, gather_reduce),
    )

    totals = jnp.concatenate([slot_sums[:SHORT_SLOTS], chain_sum], 0)
    counts = jnp.where(jnp.arange(slot_count) < SHORT_SLOTS, SPAN * PATCH, 4 * SPAN * PATCH).astype(
        F32
    )
    slot_mean = totals[:, 0] / counts
    inv_spread = lax.rsqrt(totals[:, 1] / counts - slot_mean * slot_mean + EPSILON)
    normed_slots = (grouped - slot_mean[:, None]) * inv_spread[:, None]
    normed_low = normed_slots.reshape(row_count, PATCH).astype(BF16)
    embedded = dot_n(normed_low, patch_all) + biases_all[0]
    first_value, first_back = jax.vjp(layer_norm, embedded, gains_all[0], biases_all[1])
    first_norm = first_value.astype(BF16)
    heads_in_all = tied(heads_in_all, gather_out)
    projected = dot_n(first_norm, heads_in_all).astype(BF16)
    projected = tied(projected, gather_out, gather_expand)

    own_long = projected[short_rows:]
    group_columns = lambda g, low, high: slice(
        (g * 3 + low) * GROUP * HEAD_DIM, (g * 3 + high) * GROUP * HEAD_DIM
    )
    long_pairs = jnp.concatenate([own_long[:, group_columns(g, 1, 3)] for g in range(GROUPS)], 1)
    priors = [place.along(long_pairs, step) for step in (1, 2, 3)]
    mixed_short = short_forward(projected)
    own_long, mixed_short = tied((own_long, mixed_short), gather_out, gather_expand)
    mixed_long = long_forward(quarter_index, own_long, priors)
    heads_out_all = gather_out.finish()
    heads_out_all, mixed_long = tied((heads_out_all, mixed_long), gather_expand, gather_reduce)
    mixed_all = lax.dynamic_update_slice(mixed_short, mixed_long, (short_rows, 0))
    middle = embedded + dot_n(mixed_all, heads_out_all)
    second_value, second_back = jax.vjp(layer_norm, middle, gains_all[1], biases_all[2])
    second_norm = second_value.astype(BF16)

    expand_all = gather_expand.finish()
    pre_act = dot_n(second_norm, expand_all) + expand_shift
    act_value, gelu_back = jax.vjp(exact_gelu, pre_act)
    activation = tied(act_value.astype(BF16), gather_reduce)
    grad_reduce = Chain(
        place, reduce_stages(place, dot_l(activation, cotangent).astype(BF16), False)
    )
    cotangent = tied(cotangent, gather_reduce, grad_reduce)
    reduce_all = gather_reduce.finish()

    grad_act = dot_t(cotangent, reduce_all)
    grad_pre = tied(gelu_back(grad_act)[0].astype(BF16), grad_reduce)
    grad_expand = Chain(
        place, reduce_stages(place, dot_l(second_norm, grad_pre).astype(BF16), True)
    )
    grad_expand_bias = jnp.sum(grad_pre.astype(F32), 0)
    expand_all = tied(expand_all, grad_expand)
    grad_second = dot_t(grad_pre, expand_all)
    middle_back, gain_two, shift_two = second_back(grad_second)
    grad_middle = cotangent.astype(F32) + middle_back
    grad_branch = tied(grad_middle.astype(BF16), grad_expand)
    grad_heads_out = Chain(
        place, reduce_stages(place, dot_l(mixed_all, grad_branch).astype(BF16), False)
    )
    heads_out_all = tied(heads_out_all, grad_heads_out)
    grad_mixture = dot_t(grad_branch, heads_out_all).astype(BF16)
    grad_mixture, activation = tied((grad_mixture, activation), grad_reduce, grad_heads_out)
    layer_output = (middle + dot_n(activation, reduce_all) + biases_all[3]).astype(BF16)

    long_query, own_grads, *sent = long_backward(
        quarter_index, own_long, priors, grad_mixture[short_rows:]
    )
    for step, sent_back in zip((1, 2, 3), sent):
        own_grads = own_grads + place.along(sent_back, -step).astype(F32)
    own_grads = own_grads.astype(BF16)

    def grad_group(g, grad_mixture):
        columns = slice(g * GROUP * HEAD_DIM, (g + 1) * GROUP * HEAD_DIM)
        grad_long = jnp.concatenate([a[:, columns] for a in (long_query, *own_grads)], 1)
        short = short_backward(projected, grad_mixture, g)
        return lax.dynamic_update_slice(short, grad_long, (short_rows, 0))

    grad_mixture, long_query = tied((grad_mixture, long_query), grad_expand)
    low_grad = tied(grad_group(0, grad_mixture), grad_reduce, grad_heads_out)
    grad_low = Chain(place, reduce_stages(place, dot_l(first_norm, low_grad).astype(BF16), False))
    grad_mixture = tied(grad_mixture, grad_low, grad_expand)
    high_grad = tied(grad_group(1, grad_mixture), grad_low, grad_reduce)
    grad_high = Chain(place, reduce_stages(place, dot_l(first_norm, high_grad).astype(BF16), True))
    heads_in_all = tied(heads_in_all, grad_high, grad_expand, grad_heads_out)
    grad_first = dot_t(low_grad, heads_in_all[:, :WIDE]) + dot_t(high_grad, heads_in_all[:, WIDE:])
    embed_back, gain_one, shift_one = first_back(grad_first)
    grad_embedded = (grad_middle + embed_back).astype(BF16)
    grad_embedded = tied(grad_embedded, grad_high, grad_low, grad_expand, grad_heads_out)
    grad_patch = dot_l(normed_low, grad_embedded)
    shift_zero = jnp.sum(grad_embedded.astype(F32), 0)
    grad_normed = dot_t(grad_embedded, patch_all).reshape(slot_count, SPAN * PATCH)
    slot_grads = jnp.stack([jnp.sum(grad_normed, 1), jnp.sum(grad_normed * normed_slots, 1)], 1)
    chain_grads = gather_small(place, slot_grads[SHORT_SLOTS:])
    chain_grad = jnp.sum(chain_grads * member, 0)
    grad_totals = jnp.concatenate([slot_grads[:SHORT_SLOTS], chain_grad], 0)
    series_grad = (
        inv_spread[:, None]
        * (
            grad_normed
            - grad_totals[:, 0:1] / counts[:, None]
            - normed_slots * grad_totals[:, 1:2] / counts[:, None]
        )
    ).reshape(row_count, PATCH)
    shift_three = jnp.sum(cotangent.astype(F32), 0)

    split = lambda a: a.reshape(-1, fsdp, width).transpose(1, 0, 2)
    packed = jnp.concatenate(
        [
            split(grad_patch),
            split(jnp.stack([gain_one, gain_two, shift_zero, shift_one, shift_two, shift_three])),
            grad_expand_bias.reshape(fsdp, -1, width),
        ],
        1,
    )
    small_grads = reduce_small(place, packed)
    grouped_grads = jnp.stack([grad_low.finish(), grad_high.finish()], 1)
    grad_heads_in = grouped_grads.reshape(-1, GROUPS, 3, GROUP * HEAD_DIM).transpose(0, 2, 1, 3)
    return (
        layer_output,
        series_grad,
        small_grads[:PATCH],
        grad_heads_in.reshape(-1, 3 * D),
        grad_heads_out.finish(),
        grad_expand.finish(),
        grad_reduce.finish(),
        small_grads[PATCH : PATCH + 2],
        small_grads[PATCH + 2 : PATCH + 6],
        small_grads[PATCH + 6 :].reshape(-1),
    )


def solution(mesh):
    in_specs = (
        P(("fsdp", "dp"), None),
        P(("fsdp", "dp")),
        P(None, "fsdp"),
        P("fsdp", None),
        P("fsdp", None),
        P("fsdp", None),
        P("fsdp", None),
        P(None, "fsdp"),
        P(None, "fsdp"),
        P("fsdp"),
        P(("fsdp", "dp"), None),
    )
    out_specs = (
        P(("fsdp", "dp"), None),
        P(("fsdp", "dp"), None),
        P(None, "fsdp"),
        P("fsdp", None),
        P("fsdp", None),
        P("fsdp", None),
        P("fsdp", None),
        P(None, "fsdp"),
        P(None, "fsdp"),
        P("fsdp"),
    )
    return jax.shard_map(body, mesh=mesh, in_specs=in_specs, out_specs=out_specs, check_vma=False)
```

```python
import jax
import jax.numpy as jnp
from jax import lax
from jax.experimental import pallas as pl
from jax.experimental.pallas import tpu as pltpu
from jax.sharding import PartitionSpec as P

D = 1024
HEADS = 8
HEAD_DIM = 128
PATCH = 96
SPAN = 15
SHORT_SLOTS = 48
LONG_SLOTS = 4
CHUNK = 16 * SPAN
GROUPS = 2
GROUP = HEADS // GROUPS
WIDE = 3 * GROUP * HEAD_DIM

EPSILON = 1e-05
NEG_LARGE = -1e30
SCALE = HEAD_DIM ** (-0.5)
AXES = ("fsdp", "dp")
F32 = jnp.float32
BF16 = jnp.bfloat16


class Place:
    def __init__(self):
        self.fsdp = lax.axis_size("fsdp")
        self.dp = lax.axis_size("dp")
        self.tuned = self.fsdp == 8 and self.dp == 4
        self.f = lax.axis_index("fsdp")
        d = lax.axis_index("dp")
        self.line = self.fsdp // 2
        self.z, self.y = self.f // 2, self.f % 2
        self.x, self.c = d // 2, d % 2

    def move(self, value, line=0, pair=0, side=0, core=0):
        pairs = []
        for f in range(self.fsdp):
            for d in range(self.dp):
                z, y, x, c = f // 2, f % 2, d // 2, d % 2
                to_f = ((z + line) % self.line) * 2 + (y ^ pair)
                to_d = (x ^ side) * 2 + (c ^ core)
                pairs.append((f * self.dp + d, to_f * self.dp + to_d))
        return lax.ppermute(value, AXES, pairs)

    def along(self, value, steps):
        pairs = [(s, (s + steps) % self.fsdp) for s in range(self.fsdp)]
        return lax.ppermute(value, "fsdp", pairs)


def pick(value, index, axis):
    return lax.dynamic_index_in_dim(value, index, axis, keepdims=False)


class Chain:
    def __init__(self, place, stages):
        self.place, self.stages, self.result = place, stages, None
        self.sends = self.take(None)

    def take(self, got):
        try:
            return self.stages.send(got)
        except StopIteration as end:
            self.result = end.value
            return []

    def launch(self, arrays):
        if self.sends:
            got = [self.place.move(a, **where) for a, (_, where) in zip(arrays, self.sends)]
            self.sends = self.take(got)

    def finish(self):
        while self.sends:
            self.launch([a for a, _ in self.sends])
        return self.result


def tied(value, *chains):
    pending = [[a for a, _ in chain.sends] for chain in chains]
    if not any(pending):
        return value
    value, pending = lax.optimization_barrier((value, pending))
    for chain, arrays in zip(chains, pending):
        chain.launch(arrays)
    return value


def assemble_kernel(rows, info, own, *refs):
    z, y, x, c = info[0], info[1], info[2], info[3]
    half, quarter = rows // 2, rows // 4
    *parts, out, sem = refs
    near, far = parts[:6], parts[6:]
    count = len(far) // 4
    each = 4 // count
    jobs = []

    def add(src, src_row, dst_row, count):
        jobs.append(
            pltpu.make_async_copy(
                src.at[pl.ds(src_row, count), :],
                out.at[pl.ds(pl.multiple_of(dst_row, 16), count), :],
                sem.at[len(jobs)],
            )
        )

    add(own, 0, (z * 2 + y) * rows, rows)
    for step in (1, 2, 3):
        base = (lax.rem(z + 4 - step, 4) * 2 + y) * rows
        add(near[step - 1], 0, base + c * half, half)
        add(near[step + 2], 0, base + (1 - c) * half, half)
    for step in range(4):
        base = (lax.rem(z + 4 - step, 4) * 2 + (1 - y)) * rows
        for kind, (core, side) in enumerate(((c, x), (c, 1 - x), (1 - c, x), (1 - c, 1 - x))):
            src = far[kind * count + step // each]
            add(src, (step % each) * quarter, base + core * half + side * quarter, quarter)
    for job in jobs:
        job.start()
    for job in jobs:
        job.wait()


def assemble(info, shard, near, far):
    rows, columns = shard.shape
    parts = list(near) + list(far)
    return pl.pallas_call(
        lambda *refs: assemble_kernel(rows, *refs),
        out_shape=jax.ShapeDtypeStruct((8 * rows, columns), shard.dtype),
        in_specs=[pl.BlockSpec(memory_space=pltpu.SMEM)]
        + [pl.BlockSpec(memory_space=pl.ANY)] * (1 + len(parts)),
        out_specs=pl.BlockSpec(memory_space=pltpu.VMEM),
        scratch_shapes=[pltpu.SemaphoreType.DMA((23,))],
        cost_estimate=pl.CostEstimate(
            flops=0, bytes_accessed=32 * rows * columns, transcendentals=0
        ),
        name="assemble",
    )(info, shard, *parts)


def gather_rest(place, heads_out, expand, reduce):
    dp = place.dp
    wide = heads_out.shape[1]
    pieces = [heads_out, reduce] + [expand[:, i : i + wide] for i in range(0, expand.shape[1], wide)]
    mine = lambda a: pick(a.reshape(dp, -1, wide), lax.axis_index("dp"), 0)
    every = lax.all_gather(jnp.concatenate([mine(a) for a in pieces], 0), AXES, axis=0)
    whole, low = [], 0
    for a in pieces:
        high = low + a.shape[0] // dp
        whole.append(every[:, low:high].reshape(-1, wide))
        low = high
    return whole[0], jnp.concatenate(whole[2:], 1), whole[1]


def gather_first(place, info, shard):
    if not place.tuned:
        return lax.all_gather(shard, "fsdp", axis=0, tiled=True)
    half, quarter = shard.shape[0] // 2, shard.shape[0] // 4
    own = lax.dynamic_slice_in_dim(shard, place.c * half, half, 0)
    piece = lambda a: lax.dynamic_slice_in_dim(a, place.x * quarter, quarter, 0)
    move = place.move
    a1 = move(own, line=1)
    b01 = move(jnp.concatenate([piece(own), piece(a1)], 0), pair=1)
    a2 = move(a1, line=1)
    n1 = move(a1, core=1)
    a3 = move(a2, line=1)
    x01 = move(b01, side=1)
    n2, m01 = move(a2, core=1), move(b01, core=1)
    b23 = move(jnp.concatenate([piece(a2), piece(a3)], 0), pair=1)
    n3, w01 = move(a3, core=1), move(x01, core=1)
    x23, m23 = move(b23, side=1), move(b23, core=1)
    w23 = move(x23, core=1)
    return assemble(info, shard, [a1, a2, a3, n1, n2, n3], [b01, b23, x01, x23, m01, m23, w01, w23])


def gather_small(place, packed):
    copies = jnp.broadcast_to(packed, (place.fsdp,) + packed.shape)
    return lax.all_to_all(copies, "fsdp", 0, 0, tiled=True)


def plus(a, *others):
    total = a.astype(F32)
    for other in others:
        total = total + other.astype(F32)
    return total.astype(BF16)


def reduce_stages(place, grads, side_first):
    if not place.tuned:
        parts = [
            lax.psum_scatter(g.astype(F32), "fsdp", scatter_dimension=0, tiled=True) for g in grads
        ]
        return [lax.psum(part.astype(BF16), "dp").astype(F32) for part in parts]
    z, y, x, c = place.z, place.y, place.x, place.c
    columns = grads[0].shape[1]
    views = [g.reshape(8, 2, -1, columns) for g in grads]
    got = yield [(pick(view, 1 - c, 1), dict(core=1)) for view in views]
    value = [plus(pick(view, c, 1), other) for view, other in zip(views, got)]
    value = value[0] if len(value) == 1 else jnp.concatenate(value, 1)
    half = value.shape[1]
    if side_first:
        value = value.reshape(8, 2, half // 2, columns)
        (got,) = yield [(pick(value, 1 - x, 1), dict(side=1))]
        value = plus(pick(value, x, 1), got)
    value = value.reshape(4, 2, *value.shape[1:])
    (got,) = yield [(pick(value, 1 - y, 1), dict(pair=1))]
    value = plus(pick(value, y, 1), got)
    got = yield [(pick(value, (z + k) % 4, 0), dict(line=k)) for k in (1, 2, 3)]
    value = plus(pick(value, z, 0), *got)
    (got,) = yield [(value, dict(side=1))]
    if side_first:
        low, high = jnp.where(x == 0, value, got), jnp.where(x == 0, got, value)
        value = jnp.concatenate([low, high], 0)
    else:
        value = plus(value, got)
    (got,) = yield [(value, dict(core=1))]
    low, high = jnp.where(c == 0, value, got), jnp.where(c == 0, got, value)
    results, row = [], 0
    for view in views:
        rows = slice(row, row + view.shape[2])
        results.append(jnp.concatenate([low[rows], high[rows]], 0).astype(F32))
        row += view.shape[2]
    return results


def sum_replicas(place, part):
    copies = jnp.broadcast_to(part, (place.dp,) + part.shape)
    return jnp.sum(lax.all_to_all(copies, "dp", 0, 0, tiled=True), 0)


def layer_norm(inputs, gain_row, shift_row):
    center = inputs - jnp.mean(inputs, axis=-1, keepdims=True)
    spread = jnp.mean(center * center, axis=-1, keepdims=True)
    return center * lax.rsqrt(spread + EPSILON) * gain_row + shift_row


def exact_gelu(inputs):
    return jax.nn.gelu(inputs, approximate=False)


def dot_t(a, b):
    return lax.dot_general(a, b, (((1,), (1,)), ((), ())), preferred_element_type=F32)


def dot_l(a, b):
    return lax.dot_general(a, b, (((0,), (0,)), ((), ())), preferred_element_type=F32)


def dot_n(a, b):
    return lax.dot_general(a, b, (((1,), (0,)), ((), ())), preferred_element_type=F32)


def slot_of(index):
    return jnp.floor((index.astype(F32) + 0.5) * (1.0 / SPAN))


def short_bias():
    row = lax.broadcasted_iota(jnp.int32, (CHUNK, CHUNK), 0)
    column = lax.broadcasted_iota(jnp.int32, (CHUNK, CHUNK), 1)
    keep = (slot_of(row) == slot_of(column)) & (column <= row)
    return jnp.where(keep, 0.0, NEG_LARGE)


def short_forward_kernel(q_ref, k_ref, v_ref, out_ref, bias_ref):
    @pl.when(pl.program_id(0) == 0)
    def _():
        bias_ref[...] = short_bias()

    bias = bias_ref[...]
    for chunk in range(SHORT_SLOTS * SPAN // CHUNK):
        rows = pl.ds(chunk * CHUNK, CHUNK)
        scores = dot_t(q_ref[rows, :], k_ref[rows, :]) * SCALE + bias
        top = jnp.max(scores, axis=-1, keepdims=True)
        weights = jnp.exp(scores - top)
        total = jnp.sum(weights, axis=-1, keepdims=True)
        low = (weights * (1.0 / total)).astype(BF16)
        out_ref[rows, :] = dot_n(low, v_ref[rows, :]).astype(BF16)


def block_of(rows, part):
    return pl.BlockSpec(
        (rows, HEAD_DIM), lambda h: (0, (h // GROUP) * 3 * GROUP + part * GROUP + h % GROUP)
    )


def short_forward(projected, rows):
    short_rows = SHORT_SLOTS * SPAN
    return pl.pallas_call(
        short_forward_kernel,
        grid=(HEADS,),
        out_shape=jax.ShapeDtypeStruct((rows, D), BF16),
        in_specs=[block_of(short_rows, part) for part in range(3)],
        out_specs=pl.BlockSpec((short_rows, HEAD_DIM), lambda h: (0, h)),
        scratch_shapes=[pltpu.VMEM((CHUNK, CHUNK), F32)],
        cost_estimate=pl.CostEstimate(
            flops=4 * short_rows * CHUNK * D,
            bytes_accessed=8 * rows * D,
            transcendentals=short_rows * CHUNK * HEADS,
        ),
        name="short_forward",
    )(projected, projected, projected)


def short_backward_kernel(q_ref, k_ref, v_ref, g_ref, out_ref, bias_ref):
    head = pl.program_id(0)

    @pl.when(head == 0)
    def _():
        bias_ref[...] = short_bias()

    bias = bias_ref[...]
    lanes = lambda part: pl.ds(pl.multiple_of((part * GROUP + head) * HEAD_DIM, HEAD_DIM), HEAD_DIM)
    for chunk in range(SHORT_SLOTS * SPAN // CHUNK):
        rows = pl.ds(chunk * CHUNK, CHUNK)
        query, key, grad = q_ref[rows, :], k_ref[rows, :], g_ref[rows, :]
        scores = dot_t(query, key) * SCALE + bias
        top = jnp.max(scores, axis=-1, keepdims=True)
        weights = jnp.exp(scores - top)
        probs = weights * (1.0 / jnp.sum(weights, axis=-1, keepdims=True))
        grad_probs = dot_t(grad, v_ref[rows, :])
        inner = jnp.sum(probs * grad_probs, axis=-1, keepdims=True)
        grad_scores = (probs * (grad_probs - inner)).astype(BF16)
        out_ref[rows, lanes(0)] = (dot_n(grad_scores, key) * SCALE).astype(BF16)
        out_ref[rows, lanes(1)] = (dot_l(grad_scores, query) * SCALE).astype(BF16)
        out_ref[rows, lanes(2)] = dot_l(probs.astype(BF16), grad).astype(BF16)


def short_backward(projected, grad_mixture, group):
    rows = grad_mixture.shape[0]
    short_rows = SHORT_SLOTS * SPAN
    block = lambda first: pl.BlockSpec((short_rows, HEAD_DIM), lambda h: (0, first + h))
    return pl.pallas_call(
        short_backward_kernel,
        grid=(GROUP,),
        out_shape=jax.ShapeDtypeStruct((rows, WIDE), BF16),
        in_specs=[block((group * 3 + part) * GROUP) for part in range(3)] + [block(group * GROUP)],
        out_specs=pl.BlockSpec((rows, WIDE), lambda h: (0, 0)),
        scratch_shapes=[pltpu.VMEM((CHUNK, CHUNK), F32)],
        cost_estimate=pl.CostEstimate(
            flops=10 * short_rows * CHUNK * D // GROUPS,
            bytes_accessed=14 * rows * D // GROUPS,
            transcendentals=short_rows * CHUNK * GROUP,
        ),
        name="short_backward",
    )(projected, projected, projected, grad_mixture)


def long_biases(quarter_ref):
    rows = LONG_SLOTS * SPAN
    row = lax.broadcasted_iota(jnp.int32, (rows, rows), 0)
    column = lax.broadcasted_iota(jnp.int32, (rows, rows), 1)
    slot = slot_of(row)
    same = slot == slot_of(column)
    quarter = jnp.zeros((rows, rows), jnp.int32)
    for index in range(LONG_SLOTS):
        quarter = jnp.where(slot == float(index), quarter_ref[index], quarter)
    keeps = [same & (column <= row)] + [same & (step <= quarter) for step in (1, 2, 3)]
    return [jnp.where(keep, 0.0, NEG_LARGE) for keep in keeps]


def long_probs(query, keys, biases):
    scores = [dot_t(query, key) * SCALE + bias for key, bias in zip(keys, biases)]
    top = scores[0]
    for member in scores[1:]:
        top = jnp.maximum(top, member)
    top = jnp.max(top, axis=-1, keepdims=True)
    weights = [jnp.exp(member - top) for member in scores]
    total = weights[0] + weights[1] + weights[2] + weights[3]
    scale = 1.0 / jnp.sum(total, axis=-1, keepdims=True)
    return [member * scale for member in weights]


def long_forward_kernel(quarter_ref, q, k0, v0, k1, v1, k2, v2, k3, v3, out_ref):
    biases = long_biases(quarter_ref)
    probs = long_probs(q[...], [k[...] for k in (k0, k1, k2, k3)], biases)
    total = None
    for member, value in zip(probs, (v0, v1, v2, v3)):
        part = dot_n(member.astype(BF16), value[...])
        total = part if total is None else total + part
    out_ref[...] = total.astype(BF16)


def long_specs(rows):
    sent = lambda part: pl.BlockSpec(
        (rows, HEAD_DIM), lambda h: (0, (h // GROUP) * 2 * GROUP + part * GROUP + h % GROUP)
    )
    return [block_of(rows, part) for part in range(3)] + [sent(0), sent(1)] * 3


def long_forward(quarter_index, own, priors):
    rows = own.shape[0]
    spread = [member for prior in priors for member in (prior, prior)]
    return pl.pallas_call(
        long_forward_kernel,
        grid=(HEADS,),
        out_shape=jax.ShapeDtypeStruct((rows, D), BF16),
        in_specs=[pl.BlockSpec(memory_space=pltpu.SMEM)] + long_specs(rows),
        out_specs=pl.BlockSpec((rows, HEAD_DIM), lambda h: (0, h)),
        cost_estimate=pl.CostEstimate(
            flops=16 * rows * rows * D, bytes_accessed=20 * rows * D, transcendentals=0
        ),
        name="long_forward",
    )(quarter_index, own, own, own, *spread)


def long_backward_kernel(
    quarter_ref, q, k0, v0, k1, v1, k2, v2, k3, v3, g, dq_ref, own_ref, s1_ref, s2_ref, s3_ref
):
    biases = long_biases(quarter_ref)
    query, grad = q[...], g[...]
    keys = [k[...] for k in (k0, k1, k2, k3)]
    probs = long_probs(query, keys, biases)
    grads = [dot_t(grad, value[...]) for value in (v0, v1, v2, v3)]
    inner = None
    for member, part in zip(probs, grads):
        inner = member * part if inner is None else inner + member * part
    inner = jnp.sum(inner, axis=-1, keepdims=True)
    total = None
    for index, out in enumerate((own_ref, s1_ref, s2_ref, s3_ref)):
        grad_scores = (probs[index] * (grads[index] - inner)).astype(BF16)
        part = dot_n(grad_scores, keys[index])
        total = part if total is None else total + part
        out[0, :, :] = (dot_l(grad_scores, query) * SCALE).astype(out.dtype)
        out[1, :, :] = dot_l(probs[index].astype(BF16), grad).astype(out.dtype)
    dq_ref[...] = (total * SCALE).astype(BF16)


def long_backward(quarter_index, own, priors, grad_mixture):
    rows = own.shape[0]
    spread = [member for prior in priors for member in (prior, prior)]
    flat = pl.BlockSpec((rows, HEAD_DIM), lambda h: (0, h))
    pair = pl.BlockSpec((2, rows, HEAD_DIM), lambda h: (0, 0, h))
    return pl.pallas_call(
        long_backward_kernel,
        grid=(HEADS,),
        out_shape=[jax.ShapeDtypeStruct((rows, D), BF16)]
        + [jax.ShapeDtypeStruct((2, rows, D), kind) for kind in (F32, BF16, BF16, BF16)],
        in_specs=[pl.BlockSpec(memory_space=pltpu.SMEM)] + long_specs(rows) + [flat],
        out_specs=[flat] + [pair] * 4,
        cost_estimate=pl.CostEstimate(
            flops=40 * rows * rows * D, bytes_accessed=40 * rows * D, transcendentals=0
        ),
        name="long_backward",
    )(quarter_index, own, own, own, *spread, grad_mixture)


def body(
    series_values,
    quarter_index,
    patch_weight,
    heads_in,
    heads_out,
    expand_weight,
    reduce_weight_shard,
    norm_gains,
    bias_rows,
    expand_bias,
    cotangent,
):
    place = Place()
    fsdp = place.fsdp
    width = patch_weight.shape[1]
    info = jnp.stack([place.z, place.y, place.x, place.c]).astype(jnp.int32)
    row_count = series_values.shape[0]
    slot_count = row_count // SPAN
    short_rows = SHORT_SLOTS * SPAN
    long_rows = row_count - short_rows

    grouped = series_values.reshape(slot_count, SPAN * PATCH)
    slot_sums = jnp.stack([jnp.sum(grouped, 1), jnp.sum(grouped * grouped, 1)], 1)
    rows_of = lambda a: a.astype(F32).reshape(-1, width)
    sums_row = slot_sums[SHORT_SLOTS:].reshape(1, 2 * LONG_SLOTS)
    sums_row = jnp.pad(sums_row, ((0, 7), (0, width - 2 * LONG_SLOTS)))
    pieces = [rows_of(a) for a in (patch_weight, norm_gains, bias_rows, expand_bias)]
    small_rows = sum(piece.shape[0] for piece in pieces)
    small = gather_small(place, jnp.concatenate(pieces + [sums_row], 0))
    chain = small[:, small_rows, : 2 * LONG_SLOTS].reshape(fsdp, LONG_SLOTS, 2)
    offset = jnp.arange(fsdp)[:, None] - place.f + quarter_index[None, :]
    member = ((offset + fsdp) % fsdp < 4).astype(F32)[:, :, None]
    chain_sum = jnp.sum(chain * member, 0)

    wide = lambda low, high: small[:, low:high].transpose(1, 0, 2).reshape(high - low, D)
    patch_all = wide(0, PATCH).astype(BF16)
    gains_all = wide(PATCH, PATCH + 2)
    biases_all = wide(PATCH + 2, PATCH + 6)
    expand_shift = small[:, PATCH + 6 : small_rows].reshape(-1)

    mixed_columns = heads_in.reshape(-1, 3, GROUPS, GROUP * HEAD_DIM).transpose(0, 2, 1, 3)
    heads_in_all = gather_first(place, info, mixed_columns.reshape(-1, 3 * D))
    heads_out_all, expand_all, reduce_all = gather_rest(
        place, heads_out, expand_weight, reduce_weight_shard
    )

    totals = jnp.concatenate([slot_sums[:SHORT_SLOTS], chain_sum], 0)
    counts = jnp.where(jnp.arange(slot_count) < SHORT_SLOTS, SPAN * PATCH, 4 * SPAN * PATCH).astype(
        F32
    )
    slot_mean = totals[:, 0] / counts
    inv_spread = lax.rsqrt(totals[:, 1] / counts - slot_mean * slot_mean + EPSILON)
    normed_slots = (grouped - slot_mean[:, None]) * inv_spread[:, None]
    normed_low = normed_slots.reshape(row_count, PATCH).astype(BF16)
    embedded = dot_n(normed_low, patch_all) + biases_all[0]
    first_value, first_back = jax.vjp(layer_norm, embedded, gains_all[0], biases_all[1])
    first_norm = first_value.astype(BF16)
    own_long = dot_n(first_norm[short_rows:], heads_in_all).astype(BF16)

    group_columns = lambda g, low, high: slice(
        (g * 3 + low) * GROUP * HEAD_DIM, (g * 3 + high) * GROUP * HEAD_DIM
    )
    long_pairs = jnp.concatenate([own_long[:, group_columns(g, 1, 3)] for g in range(GROUPS)], 1)
    priors = [place.along(long_pairs, step) for step in (1, 2, 3)]
    first_norm_short, heads_in_all = lax.optimization_barrier(
        (first_norm[:short_rows], heads_in_all, long_pairs)
    )[:2]
    projected = dot_n(first_norm_short, heads_in_all).astype(BF16)
    projected, priors = lax.optimization_barrier((projected, priors))
    mixed_short = short_forward(projected, row_count)
    mixed_long = long_forward(quarter_index, own_long, priors)
    mixed_all = lax.dynamic_update_slice(mixed_short, mixed_long, (short_rows, 0))
    middle = embedded + dot_n(mixed_all, heads_out_all)
    second_value, second_back = jax.vjp(layer_norm, middle, gains_all[1], biases_all[2])
    second_norm = second_value.astype(BF16)

    pre_act = dot_n(second_norm, expand_all) + expand_shift
    act_value, gelu_back = jax.vjp(exact_gelu, pre_act)
    activation = act_value.astype(BF16)
    grad_reduce = Chain(
        place, reduce_stages(place, [dot_l(activation, cotangent).astype(BF16)], False)
    )
    cotangent = tied(cotangent, grad_reduce)

    grad_act = dot_t(cotangent, reduce_all)
    grad_pre = tied(gelu_back(grad_act)[0].astype(BF16), grad_reduce)
    grad_expand = dot_l(second_norm, grad_pre).astype(BF16)
    grad_expand_bias = jnp.sum(grad_pre.astype(F32), 0)
    grad_second = dot_t(grad_pre, expand_all)
    middle_back, gain_two, shift_two = second_back(grad_second)
    grad_middle = cotangent.astype(F32) + middle_back
    grad_branch = grad_middle.astype(BF16)
    grad_heads_out = dot_l(mixed_all, grad_branch).astype(BF16)
    grad_rest = Chain(
        place, reduce_stages(place, [grad_expand[:, :D], grad_expand[:, D:], grad_heads_out], True)
    )
    heads_out_all = tied(heads_out_all, grad_rest)
    grad_mixture = dot_t(grad_branch, heads_out_all).astype(BF16)
    grad_mixture, activation = tied((grad_mixture, activation), grad_rest, grad_reduce)
    layer_output = (middle + dot_n(activation, reduce_all) + biases_all[3]).astype(BF16)

    long_query, own_grads, *sent = long_backward(
        quarter_index, own_long, priors, grad_mixture[short_rows:]
    )
    for step, sent_back in zip((1, 2, 3), sent):
        own_grads = own_grads + place.along(sent_back, -step).astype(F32)
    own_grads = own_grads.astype(BF16)

    def grad_group(g, grad_mixture):
        columns = slice(g * GROUP * HEAD_DIM, (g + 1) * GROUP * HEAD_DIM)
        grad_long = jnp.concatenate([a[:, columns] for a in (long_query, *own_grads)], 1)
        short = short_backward(projected, grad_mixture, g)
        return lax.dynamic_update_slice(short, grad_long, (short_rows, 0))

    low_grad = tied(grad_group(0, grad_mixture), grad_reduce)
    grad_low = Chain(place, reduce_stages(place, [dot_l(first_norm, low_grad).astype(BF16)], False))
    grad_mixture = tied(grad_mixture, grad_low)
    high_grad = tied(grad_group(1, grad_mixture), grad_low, grad_reduce, grad_rest)
    grad_high = Chain(
        place, reduce_stages(place, [dot_l(first_norm, high_grad).astype(BF16)], True)
    )
    heads_in_all = tied(heads_in_all, grad_high)
    grad_first = dot_t(low_grad, heads_in_all[:, :WIDE]) + dot_t(high_grad, heads_in_all[:, WIDE:])
    embed_back, gain_one, shift_one = first_back(grad_first)
    grad_embedded = (grad_middle + embed_back).astype(BF16)
    grad_embedded = tied(grad_embedded, grad_high)
    grad_patch = dot_l(normed_low, grad_embedded)
    shift_zero = jnp.sum(grad_embedded.astype(F32), 0)
    grad_normed = dot_t(grad_embedded, patch_all).reshape(slot_count, SPAN * PATCH)
    slot_grads = jnp.stack([jnp.sum(grad_normed, 1), jnp.sum(grad_normed * normed_slots, 1)], 1)
    shift_three = jnp.sum(cotangent.astype(F32), 0)
    split = lambda a: a.reshape(-1, fsdp, width).transpose(1, 0, 2)
    chain_row = slot_grads[SHORT_SLOTS:].reshape(1, 2 * LONG_SLOTS)
    chain_row = jnp.pad(chain_row, ((0, 7), (0, width - 2 * LONG_SLOTS)))
    packed = jnp.concatenate(
        [
            split(grad_patch),
            split(jnp.stack([gain_one, gain_two, shift_zero, shift_one, shift_two, shift_three])),
            grad_expand_bias.reshape(fsdp, -1, width),
            jnp.broadcast_to(chain_row, (fsdp,) + chain_row.shape),
        ],
        1,
    )
    packed = tied(packed, grad_low, grad_rest)
    parts = lax.all_to_all(packed, "fsdp", 0, 0, tiled=True)
    chain_grads = parts[:, small_rows, : 2 * LONG_SLOTS].reshape(fsdp, LONG_SLOTS, 2)
    chain_grad = jnp.sum(chain_grads * member, 0)
    small_sums = tied(jnp.sum(parts[:, :small_rows], 0), grad_high, grad_low, grad_rest)
    small_grads = sum_replicas(place, small_sums)
    grad_totals = jnp.concatenate([slot_grads[:SHORT_SLOTS], chain_grad], 0)
    series_grad = (
        inv_spread[:, None]
        * (
            grad_normed
            - grad_totals[:, 0:1] / counts[:, None]
            - normed_slots * grad_totals[:, 1:2] / counts[:, None]
        )
    ).reshape(row_count, PATCH)
    grouped_grads = jnp.stack([grad_low.finish()[0], grad_high.finish()[0]], 1)
    grad_heads_in = grouped_grads.reshape(-1, GROUPS, 3, GROUP * HEAD_DIM).transpose(0, 2, 1, 3)
    expand_low, expand_high, grad_heads_out = grad_rest.finish()
    return (
        layer_output,
        series_grad,
        small_grads[:PATCH],
        grad_heads_in.reshape(-1, 3 * D),
        grad_heads_out,
        jnp.concatenate([expand_low, expand_high], 1),
        grad_reduce.finish()[0],
        small_grads[PATCH : PATCH + 2],
        small_grads[PATCH + 2 : PATCH + 6],
        small_grads[PATCH + 6 :].reshape(-1),
    )


def solution(mesh):
    in_specs = (
        P(("fsdp", "dp"), None),
        P(("fsdp", "dp")),
        P(None, "fsdp"),
        P("fsdp", None),
        P("fsdp", None),
        P("fsdp", None),
        P("fsdp", None),
        P(None, "fsdp"),
        P(None, "fsdp"),
        P("fsdp"),
        P(("fsdp", "dp"), None),
    )
    out_specs = (
        P(("fsdp", "dp"), None),
        P(("fsdp", "dp"), None),
        P(None, "fsdp"),
        P("fsdp", None),
        P("fsdp", None),
        P("fsdp", None),
        P("fsdp", None),
        P(None, "fsdp"),
        P(None, "fsdp"),
        P("fsdp"),
    )
    return jax.shard_map(body, mesh=mesh, in_specs=in_specs, out_specs=out_specs, check_vma=False)
```

```python
import jax
import jax.numpy as jnp
from jax import lax
from jax.experimental import pallas as pl
from jax.experimental.pallas import tpu as pltpu
from jax.sharding import Mesh, PartitionSpec as P

D = 1024
HEADS = 8
HEAD_DIM = 128
PATCH = 96
SPAN = 15
SHORT_SLOTS = 48
LONG_SLOTS = 4
CHUNK = 16 * SPAN
GROUPS = 2
GROUP = HEADS // GROUPS
WIDE = 3 * GROUP * HEAD_DIM

EPSILON = 1e-05
NEG_LARGE = -1e30
SCALE = HEAD_DIM ** (-0.5)
F32 = jnp.float32
BF16 = jnp.bfloat16


class Place:
    def __init__(self, tuned):
        self.tuned = tuned
        self.fsdp_axes = ("z", "y") if tuned else ("fsdp",)
        self.dp_axes = ("x", "c") if tuned else ("dp",)

    def enter(self):
        self.fsdp = lax.axis_size(self.fsdp_axes)
        self.dp = lax.axis_size(self.dp_axes)
        self.f = lax.axis_index(self.fsdp_axes)
        self.d = lax.axis_index(self.dp_axes)

    def along(self, value, steps):
        pairs = [(s, (s + steps) % self.fsdp) for s in range(self.fsdp)]
        return lax.ppermute(value, self.fsdp_axes, pairs)

    def move(self, value, axes):
        if axes == "core":
            return lax.ppermute(value, "c", [(0, 1), (1, 0)])
        return lax.all_to_all(value, axes, 0, 0, tiled=True)


def copies(value, count):
    return jnp.broadcast_to(value, (count,) + value.shape)


def pick(value, index, axis):
    return lax.dynamic_index_in_dim(value, index, axis, keepdims=False)


class Chain:
    def __init__(self, place, stages):
        self.place, self.stages, self.result = place, stages, None
        self.sends = self.take(None)

    def take(self, got):
        try:
            return self.stages.send(got)
        except StopIteration as end:
            self.result = end.value
            return []

    def launch(self, arrays):
        if self.sends:
            got = [self.place.move(a, axes) for a, (_, axes) in zip(arrays, self.sends)]
            self.sends = self.take(got)

    def finish(self):
        while self.sends:
            self.launch([a for a, _ in self.sends])
        return self.result


def tied(value, *chains):
    pending = [[a for a, _ in chain.sends] for chain in chains]
    if not any(pending):
        return value
    value, pending = lax.optimization_barrier((value, pending))
    for chain, arrays in zip(chains, pending):
        chain.launch(arrays)
    return value


def assemble_kernel(spans, info, own, other, *refs):
    *outs, sem = refs
    core = info[0]
    jobs = []
    for src, side in ((own, core), (other, 1 - core)):
        for y in range(2):
            for x in range(2):
                for row, rows, out, column in spans:
                    width = src.shape[4]
                    jobs.append(
                        pltpu.make_async_copy(
                            src.at[y, x, :, pl.ds(row, rows), :],
                            outs[out].at[:, y, x, side, :, pl.ds(column, width)],
                            sem.at[len(jobs)],
                        )
                    )
    for job in jobs:
        job.start()
    for job in jobs:
        job.wait()


def gather_stages(place, *shards):
    if not place.tuned:
        return [lax.all_gather(shard, "fsdp", axis=0, tiled=True) for shard in shards]
    width = min(shard.shape[1] for shard in shards)
    pieces, spans, row = [], [], 0
    for out, shard in enumerate(shards):
        rows = shard.shape[0] // 4
        mine = pick(shard.reshape(4, rows, shard.shape[1]), place.d, 0)
        for column in range(0, shard.shape[1], width):
            pieces.append(mine[:, column : column + width])
            spans.append((row, rows, out, column))
            row += rows
    mine = jnp.concatenate(pieces, 0)
    (mine,) = yield [(copies(mine, 4), "z")]
    (mine,) = yield [(copies(mine, 4), ("y", "x"))]
    mine = mine.reshape(2, 2, *mine.shape[1:])
    (other,) = yield [(mine, "core")]
    whole = pl.pallas_call(
        lambda *refs: assemble_kernel(spans, *refs),
        out_shape=[
            jax.ShapeDtypeStruct((4, 2, 2, 2, shard.shape[0] // 4, shard.shape[1]), shard.dtype)
            for shard in shards
        ],
        in_specs=[pl.BlockSpec(memory_space=pltpu.SMEM)]
        + [pl.BlockSpec(memory_space=pl.ANY)] * 2,
        out_specs=[pl.BlockSpec(memory_space=pltpu.VMEM)] * len(shards),
        scratch_shapes=[pltpu.SemaphoreType.DMA((8 * len(spans),))],
        cost_estimate=pl.CostEstimate(
            flops=0, bytes_accessed=128 * row * width, transcendentals=0
        ),
        name="assemble",
    )(lax.axis_index("c").reshape(1), mine, other)
    return [a.reshape(8 * shard.shape[0], shard.shape[1]) for a, shard in zip(whole, shards)]


def gather_small(place, packed):
    return place.move(copies(packed, place.fsdp), place.fsdp_axes)


def reduce_stages(place, *grads):
    if not place.tuned:
        parts = [
            lax.psum_scatter(g.astype(F32), "fsdp", scatter_dimension=0, tiled=True) for g in grads
        ]
        return [lax.psum(part.astype(BF16), "dp").astype(F32) for part in parts]
    core = lax.axis_index("c")
    columns = grads[0].shape[1]
    total = lambda a: jnp.sum(a.astype(F32), 0).astype(BF16)
    views = [g.reshape(4, 2, 2, 2, -1, columns) for g in grads]
    got = yield [(pick(view, 1 - core, 3), "core") for view in views]
    value = [
        (pick(view, core, 3).astype(F32) + other.astype(F32)).astype(BF16).transpose(1, 2, 0, 3, 4)
        for view, other in zip(views, got)
    ]
    value = value[0] if len(value) == 1 else jnp.concatenate(value, 3)
    (got,) = yield [(value.reshape(4, *value.shape[2:]), ("y", "x"))]
    (got,) = yield [(total(got), "z")]
    (got,) = yield [(copies(total(got), 4), ("x", "c"))]
    results, row = [], 0
    for view in views:
        rows = view.shape[4]
        results.append(got[:, row : row + rows].reshape(4 * rows, columns).astype(F32))
        row += rows
    return results


def sum_replicas(place, part):
    return jnp.sum(place.move(copies(part, place.dp), place.dp_axes), 0)


def layer_norm(inputs, gain_row, shift_row):
    center = inputs - jnp.mean(inputs, axis=-1, keepdims=True)
    spread = jnp.mean(center * center, axis=-1, keepdims=True)
    return center * lax.rsqrt(spread + EPSILON) * gain_row + shift_row


def exact_gelu(inputs):
    return jax.nn.gelu(inputs, approximate=False)


def dot_t(a, b):
    return lax.dot_general(a, b, (((1,), (1,)), ((), ())), preferred_element_type=F32)


def dot_l(a, b):
    return lax.dot_general(a, b, (((0,), (0,)), ((), ())), preferred_element_type=F32)


def dot_n(a, b):
    return lax.dot_general(a, b, (((1,), (0,)), ((), ())), preferred_element_type=F32)


def slot_of(index):
    return jnp.floor((index.astype(F32) + 0.5) * (1.0 / SPAN))


def short_bias():
    row = lax.broadcasted_iota(jnp.int32, (CHUNK, CHUNK), 0)
    column = lax.broadcasted_iota(jnp.int32, (CHUNK, CHUNK), 1)
    keep = (slot_of(row) == slot_of(column)) & (column <= row)
    return jnp.where(keep, 0.0, NEG_LARGE)


def short_forward_kernel(q_ref, k_ref, v_ref, out_ref, bias_ref):
    @pl.when(pl.program_id(0) == 0)
    def _():
        bias_ref[...] = short_bias()

    bias = bias_ref[...]
    for chunk in range(SHORT_SLOTS * SPAN // CHUNK):
        rows = pl.ds(chunk * CHUNK, CHUNK)
        scores = dot_t(q_ref[rows, :], k_ref[rows, :]) * SCALE + bias
        top = jnp.max(scores, axis=-1, keepdims=True)
        weights = jnp.exp(scores - top)
        total = jnp.sum(weights, axis=-1, keepdims=True)
        low = (weights * (1.0 / total)).astype(BF16)
        out_ref[rows, :] = dot_n(low, v_ref[rows, :]).astype(BF16)


def block_of(rows, part):
    return pl.BlockSpec(
        (rows, HEAD_DIM), lambda h: (0, (h // GROUP) * 3 * GROUP + part * GROUP + h % GROUP)
    )


def short_forward(projected, rows):
    short_rows = SHORT_SLOTS * SPAN
    return pl.pallas_call(
        short_forward_kernel,
        grid=(HEADS,),
        out_shape=jax.ShapeDtypeStruct((rows, D), BF16),
        in_specs=[block_of(short_rows, part) for part in range(3)],
        out_specs=pl.BlockSpec((short_rows, HEAD_DIM), lambda h: (0, h)),
        scratch_shapes=[pltpu.VMEM((CHUNK, CHUNK), F32)],
        cost_estimate=pl.CostEstimate(
            flops=4 * short_rows * CHUNK * D,
            bytes_accessed=8 * rows * D,
            transcendentals=short_rows * CHUNK * HEADS,
        ),
        name="short_forward",
    )(projected, projected, projected)


def short_backward_kernel(q_ref, k_ref, v_ref, g_ref, out_ref, bias_ref):
    head = pl.program_id(0)

    @pl.when(head == 0)
    def _():
        bias_ref[...] = short_bias()

    bias = bias_ref[...]
    lanes = lambda part: pl.ds(pl.multiple_of((part * GROUP + head) * HEAD_DIM, HEAD_DIM), HEAD_DIM)
    for chunk in range(SHORT_SLOTS * SPAN // CHUNK):
        rows = pl.ds(chunk * CHUNK, CHUNK)
        query, key, grad = q_ref[rows, :], k_ref[rows, :], g_ref[rows, :]
        scores = dot_t(query, key) * SCALE + bias
        top = jnp.max(scores, axis=-1, keepdims=True)
        weights = jnp.exp(scores - top)
        probs = weights * (1.0 / jnp.sum(weights, axis=-1, keepdims=True))
        grad_probs = dot_t(grad, v_ref[rows, :])
        inner = jnp.sum(probs * grad_probs, axis=-1, keepdims=True)
        grad_scores = (probs * (grad_probs - inner)).astype(BF16)
        out_ref[rows, lanes(0)] = (dot_n(grad_scores, key) * SCALE).astype(BF16)
        out_ref[rows, lanes(1)] = (dot_l(grad_scores, query) * SCALE).astype(BF16)
        out_ref[rows, lanes(2)] = dot_l(probs.astype(BF16), grad).astype(BF16)


def short_backward(projected, grad_mixture, group):
    rows = grad_mixture.shape[0]
    short_rows = SHORT_SLOTS * SPAN
    block = lambda first: pl.BlockSpec((short_rows, HEAD_DIM), lambda h: (0, first + h))
    return pl.pallas_call(
        short_backward_kernel,
        grid=(GROUP,),
        out_shape=jax.ShapeDtypeStruct((rows, WIDE), BF16),
        in_specs=[block((group * 3 + part) * GROUP) for part in range(3)] + [block(group * GROUP)],
        out_specs=pl.BlockSpec((rows, WIDE), lambda h: (0, 0)),
        scratch_shapes=[pltpu.VMEM((CHUNK, CHUNK), F32)],
        cost_estimate=pl.CostEstimate(
            flops=10 * short_rows * CHUNK * D // GROUPS,
            bytes_accessed=14 * rows * D // GROUPS,
            transcendentals=short_rows * CHUNK * GROUP,
        ),
        name="short_backward",
    )(projected, projected, projected, grad_mixture)


def long_biases(quarter_ref):
    rows = LONG_SLOTS * SPAN
    row = lax.broadcasted_iota(jnp.int32, (rows, rows), 0)
    column = lax.broadcasted_iota(jnp.int32, (rows, rows), 1)
    slot = slot_of(row)
    same = slot == slot_of(column)
    quarter = jnp.zeros((rows, rows), jnp.int32)
    for index in range(LONG_SLOTS):
        quarter = jnp.where(slot == float(index), quarter_ref[index], quarter)
    keeps = [same & (column <= row)] + [same & (step <= quarter) for step in (1, 2, 3)]
    return [jnp.where(keep, 0.0, NEG_LARGE) for keep in keeps]


def long_probs(query, keys, biases):
    scores = [dot_t(query, key) * SCALE + bias for key, bias in zip(keys, biases)]
    top = scores[0]
    for member in scores[1:]:
        top = jnp.maximum(top, member)
    top = jnp.max(top, axis=-1, keepdims=True)
    weights = [jnp.exp(member - top) for member in scores]
    total = weights[0] + weights[1] + weights[2] + weights[3]
    scale = 1.0 / jnp.sum(total, axis=-1, keepdims=True)
    return [member * scale for member in weights]


def long_forward_kernel(quarter_ref, q, k0, v0, k1, v1, k2, v2, k3, v3, out_ref):
    biases = long_biases(quarter_ref)
    probs = long_probs(q[...], [k[...] for k in (k0, k1, k2, k3)], biases)
    total = None
    for member, value in zip(probs, (v0, v1, v2, v3)):
        part = dot_n(member.astype(BF16), value[...])
        total = part if total is None else total + part
    out_ref[...] = total.astype(BF16)


def long_specs(rows):
    return [block_of(rows, part) for part in range(3)] + [block_of(rows, 1), block_of(rows, 2)] * 3


def long_forward(quarter_index, own, priors):
    rows = own.shape[0]
    spread = [member for prior in priors for member in (prior, prior)]
    return pl.pallas_call(
        long_forward_kernel,
        grid=(HEADS,),
        out_shape=jax.ShapeDtypeStruct((rows, D), BF16),
        in_specs=[pl.BlockSpec(memory_space=pltpu.SMEM)] + long_specs(rows),
        out_specs=pl.BlockSpec((rows, HEAD_DIM), lambda h: (0, h)),
        cost_estimate=pl.CostEstimate(
            flops=16 * rows * rows * D, bytes_accessed=20 * rows * D, transcendentals=0
        ),
        name="long_forward",
    )(quarter_index, own, own, own, *spread)


def long_backward_kernel(
    quarter_ref, q, k0, v0, k1, v1, k2, v2, k3, v3, g, dq_ref, own_ref, s1_ref, s2_ref, s3_ref
):
    biases = long_biases(quarter_ref)
    query, grad = q[...], g[...]
    keys = [k[...] for k in (k0, k1, k2, k3)]
    probs = long_probs(query, keys, biases)
    grads = [dot_t(grad, value[...]) for value in (v0, v1, v2, v3)]
    inner = None
    for member, part in zip(probs, grads):
        inner = member * part if inner is None else inner + member * part
    inner = jnp.sum(inner, axis=-1, keepdims=True)
    total = None
    for index, out in enumerate((own_ref, s1_ref, s2_ref, s3_ref)):
        grad_scores = (probs[index] * (grads[index] - inner)).astype(BF16)
        part = dot_n(grad_scores, keys[index])
        total = part if total is None else total + part
        out[0, :, :] = (dot_l(grad_scores, query) * SCALE).astype(out.dtype)
        out[1, :, :] = dot_l(probs[index].astype(BF16), grad).astype(out.dtype)
    dq_ref[...] = (total * SCALE).astype(BF16)


def long_backward(quarter_index, own, priors, grad_mixture):
    rows = own.shape[0]
    spread = [member for prior in priors for member in (prior, prior)]
    flat = pl.BlockSpec((rows, HEAD_DIM), lambda h: (0, h))
    pair = pl.BlockSpec((2, rows, HEAD_DIM), lambda h: (0, 0, h))
    return pl.pallas_call(
        long_backward_kernel,
        grid=(HEADS,),
        out_shape=[jax.ShapeDtypeStruct((rows, D), BF16)]
        + [jax.ShapeDtypeStruct((2, rows, D), kind) for kind in (F32, BF16, BF16, BF16)],
        in_specs=[pl.BlockSpec(memory_space=pltpu.SMEM)] + long_specs(rows) + [flat],
        out_specs=[flat] + [pair] * 4,
        cost_estimate=pl.CostEstimate(
            flops=40 * rows * rows * D, bytes_accessed=40 * rows * D, transcendentals=0
        ),
        name="long_backward",
    )(quarter_index, own, own, own, *spread, grad_mixture)


def body(
    place,
    series_values,
    quarter_index,
    patch_weight,
    heads_in,
    heads_out,
    expand_weight,
    reduce_weight_shard,
    norm_gains,
    bias_rows,
    expand_bias,
    cotangent,
):
    place.enter()
    fsdp = place.fsdp
    width = patch_weight.shape[1]
    row_count = series_values.shape[0]
    slot_count = row_count // SPAN
    short_rows = SHORT_SLOTS * SPAN
    long_rows = row_count - short_rows

    grouped = series_values.reshape(slot_count, SPAN * PATCH)
    slot_sums = jnp.stack([jnp.sum(grouped, 1), jnp.sum(grouped * grouped, 1)], 1)
    rows_of = lambda a: a.astype(F32).reshape(-1, width)
    sums_row = slot_sums[SHORT_SLOTS:].reshape(1, 2 * LONG_SLOTS)
    sums_row = jnp.pad(sums_row, ((0, 7), (0, width - 2 * LONG_SLOTS)))
    pieces = [rows_of(a) for a in (patch_weight, norm_gains, bias_rows, expand_bias)]
    small_rows = sum(piece.shape[0] for piece in pieces)
    small = gather_small(place, jnp.concatenate(pieces + [sums_row], 0))
    chain = small[:, small_rows, : 2 * LONG_SLOTS].reshape(fsdp, LONG_SLOTS, 2)
    offset = jnp.arange(fsdp)[:, None] - place.f + quarter_index[None, :]
    member = ((offset + fsdp) % fsdp < 4).astype(F32)[:, :, None]
    chain_sum = jnp.sum(chain * member, 0)

    wide = lambda low, high: small[:, low:high].transpose(1, 0, 2).reshape(high - low, D)
    patch_all = wide(0, PATCH).astype(BF16)
    gains_all = wide(PATCH, PATCH + 2)
    biases_all = wide(PATCH + 2, PATCH + 6)
    expand_shift = small[:, PATCH + 6 : small_rows].reshape(-1)

    mixed_columns = heads_in.reshape(-1, 3, GROUPS, GROUP * HEAD_DIM).transpose(0, 2, 1, 3)
    gather_in, gather_out, gather_rest = [
        Chain(place, gather_stages(place, *shards))
        for shards in (
            (mixed_columns.reshape(-1, 3 * D),),
            (heads_out,),
            (expand_weight, reduce_weight_shard),
        )
    ]
    gather_in.launch([a for a, _ in gather_in.sends])
    tied((), gather_in, gather_out, gather_rest)
    tied((), gather_in, gather_out)
    (heads_in_all,) = gather_in.finish()

    totals = jnp.concatenate([slot_sums[:SHORT_SLOTS], chain_sum], 0)
    counts = jnp.where(jnp.arange(slot_count) < SHORT_SLOTS, SPAN * PATCH, 4 * SPAN * PATCH).astype(
        F32
    )
    slot_mean = totals[:, 0] / counts
    inv_spread = lax.rsqrt(totals[:, 1] / counts - slot_mean * slot_mean + EPSILON)
    normed_slots = (grouped - slot_mean[:, None]) * inv_spread[:, None]
    normed_low = normed_slots.reshape(row_count, PATCH).astype(BF16)
    embedded = dot_n(normed_low, patch_all) + biases_all[0]
    first_value, first_back = jax.vjp(layer_norm, embedded, gains_all[0], biases_all[1])
    first_norm = first_value.astype(BF16)
    heads_in_all = tied(heads_in_all, gather_out, gather_rest)
    long_norm = first_norm[short_rows:]
    prior_norms = [place.along(long_norm, step) for step in (1, 2, 3)]

    projected = dot_n(first_norm, heads_in_all).astype(BF16)
    own_long = projected[short_rows:]
    prior_all = dot_n(jnp.concatenate(prior_norms, 0), heads_in_all).astype(BF16)
    priors = [prior_all[i * long_rows : (i + 1) * long_rows] for i in range(3)]
    mixed_short = short_forward(projected, row_count)
    mixed_long = long_forward(quarter_index, own_long, priors)
    (heads_out_all,) = gather_out.finish()
    heads_out_all, mixed_long = tied((heads_out_all, mixed_long), gather_rest)
    mixed_all = lax.dynamic_update_slice(mixed_short, mixed_long, (short_rows, 0))
    middle = embedded + dot_n(mixed_all, heads_out_all)
    second_value, second_back = jax.vjp(layer_norm, middle, gains_all[1], biases_all[2])
    second_norm = second_value.astype(BF16)

    expand_all, reduce_all = gather_rest.finish()
    pre_act = dot_n(second_norm, expand_all) + expand_shift
    act_value, gelu_back = jax.vjp(exact_gelu, pre_act)
    activation = act_value.astype(BF16)
    grad_reduce = Chain(place, reduce_stages(place, dot_l(activation, cotangent).astype(BF16)))
    cotangent = tied(cotangent, grad_reduce)

    grad_act = dot_t(cotangent, reduce_all)
    grad_pre = tied(gelu_back(grad_act)[0].astype(BF16), grad_reduce)
    grad_expand = dot_l(second_norm, grad_pre).astype(BF16)
    grad_expand_bias = jnp.sum(grad_pre.astype(F32), 0)
    grad_second = dot_t(grad_pre, expand_all)
    middle_back, gain_two, shift_two = second_back(grad_second)
    grad_middle = cotangent.astype(F32) + middle_back
    grad_branch = grad_middle.astype(BF16)
    grad_heads_out = dot_l(mixed_all, grad_branch).astype(BF16)
    grad_rest = Chain(
        place, reduce_stages(place, grad_expand[:, :D], grad_expand[:, D:], grad_heads_out)
    )
    heads_out_all = tied(heads_out_all, grad_rest)
    grad_mixture = dot_t(grad_branch, heads_out_all).astype(BF16)
    grad_mixture, activation = tied((grad_mixture, activation), grad_rest, grad_reduce)
    layer_output = (middle + dot_n(activation, reduce_all) + biases_all[3]).astype(BF16)

    long_query, own_grads, *sent = long_backward(
        quarter_index, own_long, priors, grad_mixture[short_rows:]
    )
    for step, sent_back in zip((1, 2, 3), sent):
        own_grads = own_grads + place.along(sent_back, -step).astype(F32)
    own_grads = own_grads.astype(BF16)

    def grad_group(g, grad_mixture):
        columns = slice(g * GROUP * HEAD_DIM, (g + 1) * GROUP * HEAD_DIM)
        grad_long = jnp.concatenate([a[:, columns] for a in (long_query, *own_grads)], 1)
        short = short_backward(projected, grad_mixture, g)
        return lax.dynamic_update_slice(short, grad_long, (short_rows, 0))

    low_grad = grad_group(0, grad_mixture)
    grad_low = Chain(place, reduce_stages(place, dot_l(first_norm, low_grad).astype(BF16)))
    grad_mixture = tied(grad_mixture, grad_low, grad_rest)
    high_grad = tied(grad_group(1, grad_mixture), grad_low, grad_reduce)
    grad_high = Chain(place, reduce_stages(place, dot_l(first_norm, high_grad).astype(BF16)))
    heads_in_all = tied(heads_in_all, grad_high, grad_rest)
    grad_first = dot_t(low_grad, heads_in_all[:, :WIDE]) + dot_t(high_grad, heads_in_all[:, WIDE:])
    embed_back, gain_one, shift_one = first_back(grad_first)
    grad_embedded = (grad_middle + embed_back).astype(BF16)
    grad_embedded = tied(grad_embedded, grad_high, grad_low)
    grad_patch = dot_l(normed_low, grad_embedded)
    shift_zero = jnp.sum(grad_embedded.astype(F32), 0)
    grad_normed = dot_t(grad_embedded, patch_all).reshape(slot_count, SPAN * PATCH)
    slot_grads = jnp.stack([jnp.sum(grad_normed, 1), jnp.sum(grad_normed * normed_slots, 1)], 1)
    shift_three = jnp.sum(cotangent.astype(F32), 0)
    split = lambda a: a.reshape(-1, fsdp, width).transpose(1, 0, 2)
    chain_row = slot_grads[SHORT_SLOTS:].reshape(1, 2 * LONG_SLOTS)
    chain_row = jnp.pad(chain_row, ((0, 7), (0, width - 2 * LONG_SLOTS)))
    packed = jnp.concatenate(
        [
            split(grad_patch),
            split(jnp.stack([gain_one, gain_two, shift_zero, shift_one, shift_two, shift_three])),
            grad_expand_bias.reshape(fsdp, -1, width),
            jnp.broadcast_to(chain_row, (fsdp,) + chain_row.shape),
        ],
        1,
    )
    parts = place.move(packed, place.fsdp_axes)
    chain_grads = parts[:, small_rows, : 2 * LONG_SLOTS].reshape(fsdp, LONG_SLOTS, 2)
    chain_grad = jnp.sum(chain_grads * member, 0)
    small_sums = tied(jnp.sum(parts[:, :small_rows], 0), grad_high, grad_low)
    small_grads = sum_replicas(place, small_sums)
    grad_totals = jnp.concatenate([slot_grads[:SHORT_SLOTS], chain_grad], 0)
    series_grad = (
        inv_spread[:, None]
        * (
            grad_normed
            - grad_totals[:, 0:1] / counts[:, None]
            - normed_slots * grad_totals[:, 1:2] / counts[:, None]
        )
    ).reshape(row_count, PATCH)
    grouped_grads = jnp.stack([grad_low.finish()[0], grad_high.finish()[0]], 1)
    grad_heads_in = grouped_grads.reshape(-1, GROUPS, 3, GROUP * HEAD_DIM).transpose(0, 2, 1, 3)
    expand_low, expand_high, grad_heads_out = grad_rest.finish()
    return (
        layer_output,
        series_grad,
        small_grads[:PATCH],
        grad_heads_in.reshape(-1, 3 * D),
        grad_heads_out,
        jnp.concatenate([expand_low, expand_high], 1),
        grad_reduce.finish()[0],
        small_grads[PATCH : PATCH + 2],
        small_grads[PATCH + 2 : PATCH + 6],
        small_grads[PATCH + 6 :].reshape(-1),
    )


def solution(mesh):
    tuned = mesh.shape["fsdp"] == 8 and mesh.shape["dp"] == 4
    if tuned:
        mesh = Mesh(mesh.devices.reshape(4, 2, 2, 2), ("z", "y", "x", "c"))
    place = Place(tuned)
    fsdp, both = place.fsdp_axes, place.fsdp_axes + place.dp_axes
    in_specs = (
        P(both, None),
        P(both),
        P(None, fsdp),
        P(fsdp, None),
        P(fsdp, None),
        P(fsdp, None),
        P(fsdp, None),
        P(None, fsdp),
        P(None, fsdp),
        P(fsdp),
        P(both, None),
    )
    out_specs = (
        P(both, None),
        P(both, None),
        P(None, fsdp),
        P(fsdp, None),
        P(fsdp, None),
        P(fsdp, None),
        P(fsdp, None),
        P(None, fsdp),
        P(None, fsdp),
        P(fsdp),
    )
    layer = lambda *arguments: body(place, *arguments)
    return jax.shard_map(layer, mesh=mesh, in_specs=in_specs, out_specs=out_specs, check_vma=False)
```

```python
import jax
import jax.numpy as jnp
from jax import lax
from jax.experimental import pallas as pl
from jax.experimental.pallas import tpu as pltpu
from jax.sharding import PartitionSpec as P

D = 1024
HEADS = 8
HEAD_DIM = 128
PATCH = 96
SPAN = 15
SHORT_SLOTS = 48
LONG_SLOTS = 4
CHUNK = 16 * SPAN
GROUPS = 2
GROUP = HEADS // GROUPS
WIDE = 3 * GROUP * HEAD_DIM

EPSILON = 1e-05
NEG_LARGE = -1e30
SCALE = HEAD_DIM ** (-0.5)
AXES = ("fsdp", "dp")
F32 = jnp.float32
BF16 = jnp.bfloat16


class Place:
    def __init__(self):
        self.fsdp = lax.axis_size("fsdp")
        self.dp = lax.axis_size("dp")
        self.tuned = self.fsdp == 8 and self.dp == 4
        self.f = lax.axis_index("fsdp")
        d = lax.axis_index("dp")
        self.line = self.fsdp // 2
        self.z, self.y = self.f // 2, self.f % 2
        self.x, self.c = d // 2, d % 2

    def move(self, value, line=0, pair=0, side=0, core=0):
        pairs = []
        for f in range(self.fsdp):
            for d in range(self.dp):
                z, y, x, c = f // 2, f % 2, d // 2, d % 2
                to_f = ((z + line) % self.line) * 2 + (y ^ pair)
                to_d = (x ^ side) * 2 + (c ^ core)
                pairs.append((f * self.dp + d, to_f * self.dp + to_d))
        return lax.ppermute(value, AXES, pairs)

    def along(self, value, steps):
        pairs = [(s, (s + steps) % self.fsdp) for s in range(self.fsdp)]
        return lax.ppermute(value, "fsdp", pairs)


def pick(value, index, axis):
    return lax.dynamic_index_in_dim(value, index, axis, keepdims=False)


class Chain:
    def __init__(self, place, stages):
        self.place, self.stages, self.result = place, stages, None
        self.sends = self.take(None)

    def take(self, got):
        try:
            return self.stages.send(got)
        except StopIteration as end:
            self.result = end.value
            return []

    def launch(self, arrays):
        if self.sends:
            got = [self.place.move(a, **where) for a, (_, where) in zip(arrays, self.sends)]
            self.sends = self.take(got)

    def finish(self):
        while self.sends:
            self.launch([a for a, _ in self.sends])
        return self.result


def tied(value, *chains):
    pending = [[a for a, _ in chain.sends] for chain in chains]
    if not any(pending):
        return value
    value, pending = lax.optimization_barrier((value, pending))
    for chain, arrays in zip(chains, pending):
        chain.launch(arrays)
    return value


def assemble_kernel(rows, info, own, *refs):
    z, y, x, c = info[0], info[1], info[2], info[3]
    half, quarter = rows // 2, rows // 4
    *parts, out, sem = refs
    near, far = parts[:6], parts[6:]
    count = len(far) // 4
    each = 4 // count
    jobs = []

    def add(src, src_row, dst_row, count):
        jobs.append(
            pltpu.make_async_copy(
                src.at[pl.ds(src_row, count), :],
                out.at[pl.ds(pl.multiple_of(dst_row, 16), count), :],
                sem.at[len(jobs)],
            )
        )

    add(own, 0, (z * 2 + y) * rows, rows)
    for step in (1, 2, 3):
        base = (lax.rem(z + 4 - step, 4) * 2 + y) * rows
        add(near[step - 1], 0, base + c * half, half)
        add(near[step + 2], 0, base + (1 - c) * half, half)
    for step in range(4):
        base = (lax.rem(z + 4 - step, 4) * 2 + (1 - y)) * rows
        for kind, (core, side) in enumerate(((c, x), (c, 1 - x), (1 - c, x), (1 - c, 1 - x))):
            src = far[kind * count + step // each]
            add(src, (step % each) * quarter, base + core * half + side * quarter, quarter)
    for job in jobs:
        job.start()
    for job in jobs:
        job.wait()


def assemble(info, shard, near, far):
    rows, columns = shard.shape
    parts = list(near) + list(far)
    return pl.pallas_call(
        lambda *refs: assemble_kernel(rows, *refs),
        out_shape=jax.ShapeDtypeStruct((8 * rows, columns), shard.dtype),
        in_specs=[pl.BlockSpec(memory_space=pltpu.SMEM)]
        + [pl.BlockSpec(memory_space=pl.ANY)] * (1 + len(parts)),
        out_specs=pl.BlockSpec(memory_space=pltpu.VMEM),
        scratch_shapes=[pltpu.SemaphoreType.DMA((23,))],
        cost_estimate=pl.CostEstimate(
            flops=0, bytes_accessed=32 * rows * columns, transcendentals=0
        ),
        name="assemble",
    )(info, shard, *parts)


def gather_rest(place, heads_out, expand, reduce):
    dp = place.dp
    wide = heads_out.shape[1]
    pieces = [heads_out, reduce] + [expand[:, i : i + wide] for i in range(0, expand.shape[1], wide)]
    mine = lambda a: pick(a.reshape(dp, -1, wide), lax.axis_index("dp"), 0)
    every = lax.all_gather(jnp.concatenate([mine(a) for a in pieces], 0), AXES, axis=0)
    whole, low = [], 0
    for a in pieces:
        high = low + a.shape[0] // dp
        whole.append(every[:, low:high].reshape(-1, wide))
        low = high
    return whole[0], jnp.concatenate(whole[2:], 1), whole[1]


def gather_first(place, info, shard):
    if not place.tuned:
        return lax.all_gather(shard, "fsdp", axis=0, tiled=True)
    half, quarter = shard.shape[0] // 2, shard.shape[0] // 4
    own = lax.dynamic_slice_in_dim(shard, place.c * half, half, 0)
    piece = lambda a: lax.dynamic_slice_in_dim(a, place.x * quarter, quarter, 0)
    move = place.move
    a1 = move(own, line=1)
    b01 = move(jnp.concatenate([piece(own), piece(a1)], 0), pair=1)
    a2 = move(a1, line=1)
    n1 = move(a1, core=1)
    a3 = move(a2, line=1)
    x01 = move(b01, side=1)
    n2, m01 = move(a2, core=1), move(b01, core=1)
    b23 = move(jnp.concatenate([piece(a2), piece(a3)], 0), pair=1)
    n3, w01 = move(a3, core=1), move(x01, core=1)
    x23, m23 = move(b23, side=1), move(b23, core=1)
    w23 = move(x23, core=1)
    return assemble(info, shard, [a1, a2, a3, n1, n2, n3], [b01, b23, x01, x23, m01, m23, w01, w23])


def gather_small(place, packed):
    copies = jnp.broadcast_to(packed, (place.fsdp,) + packed.shape)
    return lax.all_to_all(copies, "fsdp", 0, 0, tiled=True)


def plus(a, *others):
    total = a.astype(F32)
    for other in others:
        total = total + other.astype(F32)
    return total.astype(BF16)


def weight_grad(place, left, right):
    if not place.tuned:
        return dot_l(left, right).astype(BF16)
    half = right.shape[1] // 2
    columns = lambda core: lax.dynamic_slice_in_dim(right, core * half, half, 1)
    got = place.move(dot_l(left, columns(1 - place.c)).astype(BF16), core=1)
    return (dot_l(left, columns(place.c)) + got.astype(F32)).astype(BF16)


def reduce_stages(place, *grads):
    if not place.tuned:
        parts = [
            lax.psum_scatter(g.astype(F32), "fsdp", scatter_dimension=0, tiled=True) for g in grads
        ]
        return [(lax.psum(part.astype(BF16), "dp").astype(F32),) for part in parts]
    z, y, x, c = place.z, place.y, place.x, place.c
    columns = grads[0].shape[1]
    views = [g.reshape(8, -1, columns) for g in grads]
    value = views[0] if len(views) == 1 else jnp.concatenate(views, 1)
    value = value.reshape(8, 2, -1, columns)
    (got,) = yield [(pick(value, 1 - x, 1), dict(side=1))]
    value = plus(pick(value, x, 1), got)
    value = value.reshape(4, 2, *value.shape[1:])
    (got,) = yield [(pick(value, 1 - y, 1), dict(pair=1))]
    value = plus(pick(value, y, 1), got)
    got = yield [(pick(value, (z + k) % 4, 0), dict(line=k)) for k in (1, 2, 3)]
    value = plus(pick(value, z, 0), *got)
    (got,) = yield [(value, dict(side=1))]
    low, high = jnp.where(x == 0, value, got), jnp.where(x == 0, got, value)
    value = jnp.concatenate([low, high], 0)
    (got,) = yield [(value, dict(core=1))]
    low, high = jnp.where(c == 0, value, got), jnp.where(c == 0, got, value)
    results, row = [], 0
    for view in views:
        rows = slice(row, row + view.shape[1])
        results.append((low[rows].astype(F32), high[rows].astype(F32)))
        row += view.shape[1]
    return results


def joined(*pairs):
    return jnp.concatenate([part for side in zip(*pairs) for part in side], 1)


def sum_replicas(place, part):
    copies = jnp.broadcast_to(part, (place.dp,) + part.shape)
    return jnp.sum(lax.all_to_all(copies, "dp", 0, 0, tiled=True), 0)


def layer_norm(inputs, gain_row, shift_row):
    center = inputs - jnp.mean(inputs, axis=-1, keepdims=True)
    spread = jnp.mean(center * center, axis=-1, keepdims=True)
    return center * lax.rsqrt(spread + EPSILON) * gain_row + shift_row


def exact_gelu(inputs):
    return jax.nn.gelu(inputs, approximate=False)


def dot_t(a, b):
    return lax.dot_general(a, b, (((1,), (1,)), ((), ())), preferred_element_type=F32)


def dot_l(a, b):
    return lax.dot_general(a, b, (((0,), (0,)), ((), ())), preferred_element_type=F32)


def dot_n(a, b):
    return lax.dot_general(a, b, (((1,), (0,)), ((), ())), preferred_element_type=F32)


def slot_of(index):
    return jnp.floor((index.astype(F32) + 0.5) * (1.0 / SPAN))


def short_bias():
    row = lax.broadcasted_iota(jnp.int32, (CHUNK, CHUNK), 0)
    column = lax.broadcasted_iota(jnp.int32, (CHUNK, CHUNK), 1)
    keep = (slot_of(row) == slot_of(column)) & (column <= row)
    return jnp.where(keep, 0.0, NEG_LARGE)


def short_forward_kernel(q_ref, k_ref, v_ref, out_ref, bias_ref):
    @pl.when(pl.program_id(0) == 0)
    def _():
        bias_ref[...] = short_bias()

    bias = bias_ref[...]
    for chunk in range(SHORT_SLOTS * SPAN // CHUNK):
        rows = pl.ds(chunk * CHUNK, CHUNK)
        scores = dot_t(q_ref[rows, :], k_ref[rows, :]) * SCALE + bias
        top = jnp.max(scores, axis=-1, keepdims=True)
        weights = jnp.exp(scores - top)
        total = jnp.sum(weights, axis=-1, keepdims=True)
        low = (weights * (1.0 / total)).astype(BF16)
        out_ref[rows, :] = dot_n(low, v_ref[rows, :]).astype(BF16)


def block_of(rows, part):
    return pl.BlockSpec(
        (rows, HEAD_DIM), lambda h: (0, (h // GROUP) * 3 * GROUP + part * GROUP + h % GROUP)
    )


def short_forward(projected, rows):
    short_rows = SHORT_SLOTS * SPAN
    return pl.pallas_call(
        short_forward_kernel,
        grid=(HEADS,),
        out_shape=jax.ShapeDtypeStruct((rows, D), BF16),
        in_specs=[block_of(short_rows, part) for part in range(3)],
        out_specs=pl.BlockSpec((short_rows, HEAD_DIM), lambda h: (0, h)),
        scratch_shapes=[pltpu.VMEM((CHUNK, CHUNK), F32)],
        cost_estimate=pl.CostEstimate(
            flops=4 * short_rows * CHUNK * D,
            bytes_accessed=8 * rows * D,
            transcendentals=short_rows * CHUNK * HEADS,
        ),
        name="short_forward",
    )(projected, projected, projected)


def short_backward_kernel(q_ref, k_ref, v_ref, g_ref, out_ref, bias_ref):
    head = pl.program_id(0)

    @pl.when(head == 0)
    def _():
        bias_ref[...] = short_bias()

    bias = bias_ref[...]
    lanes = lambda part: pl.ds(pl.multiple_of((part * GROUP + head) * HEAD_DIM, HEAD_DIM), HEAD_DIM)
    for chunk in range(SHORT_SLOTS * SPAN // CHUNK):
        rows = pl.ds(chunk * CHUNK, CHUNK)
        query, key, grad = q_ref[rows, :], k_ref[rows, :], g_ref[rows, :]
        scores = dot_t(query, key) * SCALE + bias
        top = jnp.max(scores, axis=-1, keepdims=True)
        weights = jnp.exp(scores - top)
        probs = weights * (1.0 / jnp.sum(weights, axis=-1, keepdims=True))
        grad_probs = dot_t(grad, v_ref[rows, :])
        inner = jnp.sum(probs * grad_probs, axis=-1, keepdims=True)
        grad_scores = (probs * (grad_probs - inner)).astype(BF16)
        out_ref[rows, lanes(0)] = (dot_n(grad_scores, key) * SCALE).astype(BF16)
        out_ref[rows, lanes(1)] = (dot_l(grad_scores, query) * SCALE).astype(BF16)
        out_ref[rows, lanes(2)] = dot_l(probs.astype(BF16), grad).astype(BF16)


def short_backward(projected, grad_mixture, group):
    rows = grad_mixture.shape[0]
    short_rows = SHORT_SLOTS * SPAN
    block = lambda first: pl.BlockSpec((short_rows, HEAD_DIM), lambda h: (0, first + h))
    return pl.pallas_call(
        short_backward_kernel,
        grid=(GROUP,),
        out_shape=jax.ShapeDtypeStruct((rows, WIDE), BF16),
        in_specs=[block((group * 3 + part) * GROUP) for part in range(3)] + [block(group * GROUP)],
        out_specs=pl.BlockSpec((rows, WIDE), lambda h: (0, 0)),
        scratch_shapes=[pltpu.VMEM((CHUNK, CHUNK), F32)],
        cost_estimate=pl.CostEstimate(
            flops=10 * short_rows * CHUNK * D // GROUPS,
            bytes_accessed=14 * rows * D // GROUPS,
            transcendentals=short_rows * CHUNK * GROUP,
        ),
        name="short_backward",
    )(projected, projected, projected, grad_mixture)


def long_biases(quarter_ref):
    rows = LONG_SLOTS * SPAN
    row = lax.broadcasted_iota(jnp.int32, (rows, rows), 0)
    column = lax.broadcasted_iota(jnp.int32, (rows, rows), 1)
    slot = slot_of(row)
    same = slot == slot_of(column)
    quarter = jnp.zeros((rows, rows), jnp.int32)
    for index in range(LONG_SLOTS):
        quarter = jnp.where(slot == float(index), quarter_ref[index], quarter)
    keeps = [same & (column <= row)] + [same & (step <= quarter) for step in (1, 2, 3)]
    return [jnp.where(keep, 0.0, NEG_LARGE) for keep in keeps]


def long_probs(query, keys, biases):
    scores = [dot_t(query, key) * SCALE + bias for key, bias in zip(keys, biases)]
    top = scores[0]
    for member in scores[1:]:
        top = jnp.maximum(top, member)
    top = jnp.max(top, axis=-1, keepdims=True)
    weights = [jnp.exp(member - top) for member in scores]
    total = weights[0] + weights[1] + weights[2] + weights[3]
    scale = 1.0 / jnp.sum(total, axis=-1, keepdims=True)
    return [member * scale for member in weights]


def long_forward_kernel(quarter_ref, q, k0, v0, k1, v1, k2, v2, k3, v3, out_ref):
    biases = long_biases(quarter_ref)
    probs = long_probs(q[...], [k[...] for k in (k0, k1, k2, k3)], biases)
    total = None
    for member, value in zip(probs, (v0, v1, v2, v3)):
        part = dot_n(member.astype(BF16), value[...])
        total = part if total is None else total + part
    out_ref[...] = total.astype(BF16)


def long_specs(rows):
    return [block_of(rows, part) for part in range(3)] + [block_of(rows, 1), block_of(rows, 2)] * 3


def long_forward(quarter_index, own, priors):
    rows = own.shape[0]
    spread = [member for prior in priors for member in (prior, prior)]
    return pl.pallas_call(
        long_forward_kernel,
        grid=(HEADS,),
        out_shape=jax.ShapeDtypeStruct((rows, D), BF16),
        in_specs=[pl.BlockSpec(memory_space=pltpu.SMEM)] + long_specs(rows),
        out_specs=pl.BlockSpec((rows, HEAD_DIM), lambda h: (0, h)),
        cost_estimate=pl.CostEstimate(
            flops=16 * rows * rows * D, bytes_accessed=20 * rows * D, transcendentals=0
        ),
        name="long_forward",
    )(quarter_index, own, own, own, *spread)


def long_backward_kernel(
    quarter_ref, q, k0, v0, k1, v1, k2, v2, k3, v3, g, dq_ref, own_ref, s1_ref, s2_ref, s3_ref
):
    biases = long_biases(quarter_ref)
    query, grad = q[...], g[...]
    keys = [k[...] for k in (k0, k1, k2, k3)]
    probs = long_probs(query, keys, biases)
    grads = [dot_t(grad, value[...]) for value in (v0, v1, v2, v3)]
    inner = None
    for member, part in zip(probs, grads):
        inner = member * part if inner is None else inner + member * part
    inner = jnp.sum(inner, axis=-1, keepdims=True)
    total = None
    for index, out in enumerate((own_ref, s1_ref, s2_ref, s3_ref)):
        grad_scores = (probs[index] * (grads[index] - inner)).astype(BF16)
        part = dot_n(grad_scores, keys[index])
        total = part if total is None else total + part
        out[0, :, :] = (dot_l(grad_scores, query) * SCALE).astype(out.dtype)
        out[1, :, :] = dot_l(probs[index].astype(BF16), grad).astype(out.dtype)
    dq_ref[...] = (total * SCALE).astype(BF16)


def long_backward(quarter_index, own, priors, grad_mixture):
    rows = own.shape[0]
    spread = [member for prior in priors for member in (prior, prior)]
    flat = pl.BlockSpec((rows, HEAD_DIM), lambda h: (0, h))
    pair = pl.BlockSpec((2, rows, HEAD_DIM), lambda h: (0, 0, h))
    return pl.pallas_call(
        long_backward_kernel,
        grid=(HEADS,),
        out_shape=[jax.ShapeDtypeStruct((rows, D), BF16)]
        + [jax.ShapeDtypeStruct((2, rows, D), kind) for kind in (F32, BF16, BF16, BF16)],
        in_specs=[pl.BlockSpec(memory_space=pltpu.SMEM)] + long_specs(rows) + [flat],
        out_specs=[flat] + [pair] * 4,
        cost_estimate=pl.CostEstimate(
            flops=40 * rows * rows * D, bytes_accessed=40 * rows * D, transcendentals=0
        ),
        name="long_backward",
    )(quarter_index, own, own, own, *spread, grad_mixture)


def body(
    series_values,
    quarter_index,
    patch_weight,
    heads_in,
    heads_out,
    expand_weight,
    reduce_weight_shard,
    norm_gains,
    bias_rows,
    expand_bias,
    cotangent,
):
    place = Place()
    fsdp = place.fsdp
    width = patch_weight.shape[1]
    info = jnp.stack([place.z, place.y, place.x, place.c]).astype(jnp.int32)
    row_count = series_values.shape[0]
    slot_count = row_count // SPAN
    short_rows = SHORT_SLOTS * SPAN
    long_rows = row_count - short_rows

    grouped = series_values.reshape(slot_count, SPAN * PATCH)
    slot_sums = jnp.stack([jnp.sum(grouped, 1), jnp.sum(grouped * grouped, 1)], 1)
    rows_of = lambda a: a.astype(F32).reshape(-1, width)
    sums_row = slot_sums[SHORT_SLOTS:].reshape(1, 2 * LONG_SLOTS)
    sums_row = jnp.pad(sums_row, ((0, 7), (0, width - 2 * LONG_SLOTS)))
    pieces = [rows_of(a) for a in (patch_weight, norm_gains, bias_rows, expand_bias)]
    small_rows = sum(piece.shape[0] for piece in pieces)
    small = gather_small(place, jnp.concatenate(pieces + [sums_row], 0))
    chain = small[:, small_rows, : 2 * LONG_SLOTS].reshape(fsdp, LONG_SLOTS, 2)
    offset = jnp.arange(fsdp)[:, None] - place.f + quarter_index[None, :]
    member = ((offset + fsdp) % fsdp < 4).astype(F32)[:, :, None]
    chain_sum = jnp.sum(chain * member, 0)

    wide = lambda low, high: small[:, low:high].transpose(1, 0, 2).reshape(high - low, D)
    patch_all = wide(0, PATCH).astype(BF16)
    gains_all = wide(PATCH, PATCH + 2)
    biases_all = wide(PATCH + 2, PATCH + 6)
    expand_shift = small[:, PATCH + 6 : small_rows].reshape(-1)

    mixed_columns = heads_in.reshape(-1, 3, GROUPS, GROUP * HEAD_DIM).transpose(0, 2, 1, 3)
    heads_in_all = gather_first(place, info, mixed_columns.reshape(-1, 3 * D))
    heads_out_all, expand_all, reduce_all = gather_rest(
        place, heads_out, expand_weight, reduce_weight_shard
    )

    totals = jnp.concatenate([slot_sums[:SHORT_SLOTS], chain_sum], 0)
    counts = jnp.where(jnp.arange(slot_count) < SHORT_SLOTS, SPAN * PATCH, 4 * SPAN * PATCH).astype(
        F32
    )
    slot_mean = totals[:, 0] / counts
    inv_spread = lax.rsqrt(totals[:, 1] / counts - slot_mean * slot_mean + EPSILON)
    normed_slots = (grouped - slot_mean[:, None]) * inv_spread[:, None]
    normed_low = normed_slots.reshape(row_count, PATCH).astype(BF16)
    embedded = dot_n(normed_low, patch_all) + biases_all[0]
    first_value, first_back = jax.vjp(layer_norm, embedded, gains_all[0], biases_all[1])
    first_norm = first_value.astype(BF16)
    long_norm = first_norm[short_rows:]
    prior_norms = jnp.concatenate([place.along(long_norm, step) for step in (1, 2, 3)], 0)
    prior_norms, heads_in_all = lax.optimization_barrier((prior_norms, heads_in_all))
    projected = dot_n(first_norm, heads_in_all).astype(BF16)
    own_long = projected[short_rows:]
    prior_all = dot_n(prior_norms, heads_in_all).astype(BF16)
    priors = [prior_all[i * long_rows : (i + 1) * long_rows] for i in range(3)]

    mixed_short = short_forward(projected, row_count)
    mixed_long = long_forward(quarter_index, own_long, priors)
    mixed_all = lax.dynamic_update_slice(mixed_short, mixed_long, (short_rows, 0))
    middle = embedded + dot_n(mixed_all, heads_out_all)
    second_value, second_back = jax.vjp(layer_norm, middle, gains_all[1], biases_all[2])
    second_norm = second_value.astype(BF16)

    pre_act = dot_n(second_norm, expand_all) + expand_shift
    act_value, gelu_back = jax.vjp(exact_gelu, pre_act)
    activation = act_value.astype(BF16)
    grad_reduce = Chain(place, reduce_stages(place, weight_grad(place, activation, cotangent)))

    grad_act = dot_t(cotangent, reduce_all)
    grad_pre = tied(gelu_back(grad_act)[0].astype(BF16), grad_reduce)
    grad_expand = weight_grad(place, second_norm, grad_pre)
    grad_expand_bias = jnp.sum(grad_pre.astype(F32), 0)
    grad_second = dot_t(grad_pre, expand_all)
    middle_back, gain_two, shift_two = second_back(grad_second)
    grad_middle = cotangent.astype(F32) + middle_back
    grad_branch = grad_middle.astype(BF16)
    grad_heads_out = weight_grad(place, mixed_all, grad_branch)
    wide = grad_heads_out.shape[1]
    grad_rest = Chain(
        place,
        reduce_stages(place, grad_expand[:, :wide], grad_expand[:, wide:], grad_heads_out),
    )
    grad_mixture = dot_t(grad_branch, heads_out_all).astype(BF16)
    grad_mixture, activation = tied((grad_mixture, activation), grad_rest)
    layer_output = (middle + dot_n(activation, reduce_all) + biases_all[3]).astype(BF16)

    long_query, own_grads, *sent = long_backward(
        quarter_index, own_long, priors, grad_mixture[short_rows:]
    )
    for step, sent_back in zip((1, 2, 3), sent):
        own_grads = own_grads + place.along(sent_back, -step).astype(F32)
    own_grads = own_grads.astype(BF16)

    def grad_group(g, grad_mixture):
        columns = slice(g * GROUP * HEAD_DIM, (g + 1) * GROUP * HEAD_DIM)
        grad_long = jnp.concatenate([a[:, columns] for a in (long_query, *own_grads)], 1)
        short = short_backward(projected, grad_mixture, g)
        return lax.dynamic_update_slice(short, grad_long, (short_rows, 0))

    grad_mixture, long_query = tied((grad_mixture, long_query), grad_reduce)
    low_grad = grad_group(0, grad_mixture)
    grad_low = Chain(place, reduce_stages(place, weight_grad(place, first_norm, low_grad)))
    grad_mixture = tied(grad_mixture, grad_reduce)
    high_grad = tied(grad_group(1, grad_mixture), grad_low, grad_rest)
    grad_high = Chain(place, reduce_stages(place, weight_grad(place, first_norm, high_grad)))
    heads_in_all = tied(heads_in_all, grad_reduce)
    grad_first = dot_t(low_grad, heads_in_all[:, :WIDE]) + dot_t(high_grad, heads_in_all[:, WIDE:])
    embed_back, gain_one, shift_one = first_back(grad_first)
    grad_embedded = (grad_middle + embed_back).astype(BF16)
    grad_embedded = tied(grad_embedded, grad_high)
    grad_patch = dot_l(normed_low, grad_embedded)
    shift_zero = jnp.sum(grad_embedded.astype(F32), 0)
    grad_normed = dot_t(grad_embedded, patch_all).reshape(slot_count, SPAN * PATCH)
    slot_grads = jnp.stack([jnp.sum(grad_normed, 1), jnp.sum(grad_normed * normed_slots, 1)], 1)
    shift_three = jnp.sum(cotangent.astype(F32), 0)
    split = lambda a: a.reshape(-1, fsdp, width).transpose(1, 0, 2)
    chain_row = slot_grads[SHORT_SLOTS:].reshape(1, 2 * LONG_SLOTS)
    chain_row = jnp.pad(chain_row, ((0, 7), (0, width - 2 * LONG_SLOTS)))
    packed = jnp.concatenate(
        [
            split(grad_patch),
            split(jnp.stack([gain_one, gain_two, shift_zero, shift_one, shift_two, shift_three])),
            grad_expand_bias.reshape(fsdp, -1, width),
            jnp.broadcast_to(chain_row, (fsdp,) + chain_row.shape),
        ],
        1,
    )
    packed = tied(packed, grad_low, grad_rest)
    parts = lax.all_to_all(packed, "fsdp", 0, 0, tiled=True)
    chain_grads = parts[:, small_rows, : 2 * LONG_SLOTS].reshape(fsdp, LONG_SLOTS, 2)
    chain_grad = jnp.sum(chain_grads * member, 0)
    small_sums = tied(jnp.sum(parts[:, :small_rows], 0), grad_high, grad_low, grad_rest)
    small_grads = sum_replicas(place, small_sums)
    grad_totals = jnp.concatenate([slot_grads[:SHORT_SLOTS], chain_grad], 0)
    series_grad = (
        inv_spread[:, None]
        * (
            grad_normed
            - grad_totals[:, 0:1] / counts[:, None]
            - normed_slots * grad_totals[:, 1:2] / counts[:, None]
        )
    ).reshape(row_count, PATCH)
    grouped_grads = jnp.stack([joined(grad_low.finish()[0]), joined(grad_high.finish()[0])], 1)
    grad_heads_in = grouped_grads.reshape(-1, GROUPS, 3, GROUP * HEAD_DIM).transpose(0, 2, 1, 3)
    *expand_pairs, heads_out_pair = grad_rest.finish()
    return (
        layer_output,
        series_grad,
        small_grads[:PATCH],
        grad_heads_in.reshape(-1, 3 * D),
        joined(heads_out_pair),
        joined(*expand_pairs),
        joined(grad_reduce.finish()[0]),
        small_grads[PATCH : PATCH + 2],
        small_grads[PATCH + 2 : PATCH + 6],
        small_grads[PATCH + 6 :].reshape(-1),
    )


def solution(mesh):
    in_specs = (
        P(("fsdp", "dp"), None),
        P(("fsdp", "dp")),
        P(None, "fsdp"),
        P("fsdp", None),
        P("fsdp", None),
        P("fsdp", None),
        P("fsdp", None),
        P(None, "fsdp"),
        P(None, "fsdp"),
        P("fsdp"),
        P(("fsdp", "dp"), None),
    )
    out_specs = (
        P(("fsdp", "dp"), None),
        P(("fsdp", "dp"), None),
        P(None, "fsdp"),
        P("fsdp", None),
        P("fsdp", None),
        P("fsdp", None),
        P("fsdp", None),
        P(None, "fsdp"),
        P(None, "fsdp"),
        P("fsdp"),
    )
    return jax.shard_map(body, mesh=mesh, in_specs=in_specs, out_specs=out_specs, check_vma=False)
```

```python
import math

import jax
import jax.numpy as jnp
from jax import lax
from jax.experimental import pallas as pl
from jax.experimental.pallas import tpu as pltpu
from jax.sharding import Mesh, PartitionSpec as P

D = 1024
HEADS = 8
HEAD_DIM = 128
PATCH = 96
SPAN = 15
SHORT_SLOTS = 48
LONG_SLOTS = 4
CHUNK = 16 * SPAN
GROUPS = 1
GROUP = HEADS // GROUPS
WIDE = 3 * GROUP * HEAD_DIM

EPSILON = 1e-05
NEG_LARGE = -1e30
SCALE = HEAD_DIM ** (-0.5)
F32 = jnp.float32
BF16 = jnp.bfloat16


class Place:
    def __init__(self, tuned):
        self.tuned = tuned
        self.fsdp_axes = ("z", "y") if tuned else ("fsdp",)
        self.dp_axes = ("x", "c") if tuned else ("dp",)

    def enter(self):
        self.fsdp = lax.axis_size(self.fsdp_axes)
        self.dp = lax.axis_size(self.dp_axes)
        self.f = lax.axis_index(self.fsdp_axes)
        self.d = lax.axis_index(self.dp_axes)
        if self.tuned:
            self.z, self.y, self.x, self.c = [lax.axis_index(axis) for axis in "zyxc"]

    def move(self, value, line=0, pair=0, side=0, core=0, every=()):
        if every:
            return lax.all_to_all(value, every, 0, 0, tiled=True)
        pairs = []
        for f in range(self.fsdp):
            for d in range(self.dp):
                z, y, x, c = f // 2, f % 2, d // 2, d % 2
                to_f = ((z + line) % 4) * 2 + (y ^ pair)
                to_d = (x ^ side) * 2 + (c ^ core)
                pairs.append((f * self.dp + d, to_f * self.dp + to_d))
        return lax.ppermute(value, self.fsdp_axes + self.dp_axes, pairs)

    def along(self, value, steps):
        pairs = [(s, (s + steps) % self.fsdp) for s in range(self.fsdp)]
        return lax.ppermute(value, self.fsdp_axes, pairs)


def copies(value, count):
    return jnp.broadcast_to(value, (count,) + value.shape)


def pick(value, index, axis):
    return lax.dynamic_index_in_dim(value, index, axis, keepdims=False)


class Chain:
    def __init__(self, place, stages):
        self.place, self.stages = place, stages
        self.got, self.result = [], None
        self.sends = self.take(None)

    def take(self, got):
        try:
            return self.stages.send(got)
        except StopIteration as end:
            self.result = end.value
            return []

    def prepare(self):
        if self.got:
            self.sends, self.got = self.take(self.got), []

    def launch(self, arrays):
        self.got = [self.place.move(a, **where) for a, (_, where) in zip(arrays, self.sends)]
        self.sends = []

    def finish(self):
        self.prepare()
        while self.sends:
            self.launch([a for a, _ in self.sends])
            self.prepare()
        return self.result


def tied(value, *chains):
    if any(chain.got for chain in chains):
        value, got = lax.optimization_barrier((value, [chain.got for chain in chains]))
        for chain, arrays in zip(chains, got):
            chain.got = arrays
            chain.prepare()
    pending = [[a for a, _ in chain.sends] for chain in chains]
    if any(pending):
        value, pending = lax.optimization_barrier((value, pending))
        for chain, arrays in zip(chains, pending):
            chain.launch(arrays)
    return value


def assemble_kernel(rows, info, own, *refs):
    z, y, x, c = info[0], info[1], info[2], info[3]
    half, quarter = rows // 2, rows // 4
    *parts, out, sem = refs
    near, far = parts[:6], parts[6:]
    count = len(far) // 4
    each = 4 // count
    jobs = []

    def add(src, src_row, dst_row, count):
        jobs.append(
            pltpu.make_async_copy(
                src.at[pl.ds(src_row, count), :],
                out.at[pl.ds(pl.multiple_of(dst_row, 16), count), :],
                sem.at[len(jobs)],
            )
        )

    add(own, 0, (z * 2 + y) * rows, rows)
    for step in (1, 2, 3):
        base = (lax.rem(z + 4 - step, 4) * 2 + y) * rows
        add(near[step - 1], 0, base + c * half, half)
        add(near[step + 2], 0, base + (1 - c) * half, half)
    for step in range(4):
        base = (lax.rem(z + 4 - step, 4) * 2 + (1 - y)) * rows
        for kind, (core, side) in enumerate(((c, x), (c, 1 - x), (1 - c, x), (1 - c, 1 - x))):
            src = far[kind * count + step // each]
            add(src, (step % each) * quarter, base + core * half + side * quarter, quarter)
    for job in jobs:
        job.start()
    for job in jobs:
        job.wait()


def assemble(info, shard, near, far):
    rows, columns = shard.shape
    parts = list(near) + list(far)
    return pl.pallas_call(
        lambda *refs: assemble_kernel(rows, *refs),
        out_shape=jax.ShapeDtypeStruct((8 * rows, columns), shard.dtype),
        in_specs=[pl.BlockSpec(memory_space=pltpu.SMEM)]
        + [pl.BlockSpec(memory_space=pl.ANY)] * (1 + len(parts)),
        out_specs=pl.BlockSpec(memory_space=pltpu.VMEM),
        scratch_shapes=[pltpu.SemaphoreType.DMA((23,))],
        cost_estimate=pl.CostEstimate(
            flops=0, bytes_accessed=32 * rows * columns, transcendentals=0
        ),
        name="assemble",
    )(info, shard, *parts)


def spread_kernel(spans, info, own, other, *refs):
    *outs, sem = refs
    core = info[0]
    jobs = []
    for src, side in ((own, core), (other, 1 - core)):
        for y in range(2):
            for x in range(2):
                for row, rows, out, column in spans:
                    width = src.shape[4]
                    jobs.append(
                        pltpu.make_async_copy(
                            src.at[y, x, :, pl.ds(row, rows), :],
                            outs[out].at[:, y, x, side, :, pl.ds(column, width)],
                            sem.at[len(jobs)],
                        )
                    )
    for job in jobs:
        job.start()
    for job in jobs:
        job.wait()


def gather_stages(place, *shards):
    if not place.tuned:
        return [lax.all_gather(shard, "fsdp", axis=0, tiled=True) for shard in shards]
    width = min(shard.shape[1] for shard in shards)
    pieces, spans, row = [], [], 0
    for out, shard in enumerate(shards):
        rows = shard.shape[0] // 4
        mine = pick(shard.reshape(4, rows, shard.shape[1]), place.d, 0)
        for column in range(0, shard.shape[1], width):
            pieces.append(mine[:, column : column + width])
            spans.append((row, rows, out, column))
            row += rows
    mine = jnp.concatenate(pieces, 0)
    (mine,) = yield [(copies(mine, 4), dict(every=("z",)))]
    (mine,) = yield [(copies(mine, 4), dict(every=("y", "x")))]
    mine = mine.reshape(2, 2, *mine.shape[1:])
    (other,) = yield [(mine, dict(core=1))]
    whole = pl.pallas_call(
        lambda *refs: spread_kernel(spans, *refs),
        out_shape=[
            jax.ShapeDtypeStruct((4, 2, 2, 2, shard.shape[0] // 4, shard.shape[1]), shard.dtype)
            for shard in shards
        ],
        in_specs=[pl.BlockSpec(memory_space=pltpu.SMEM)]
        + [pl.BlockSpec(memory_space=pl.ANY)] * 2,
        out_specs=[pl.BlockSpec(memory_space=pltpu.VMEM)] * len(shards),
        scratch_shapes=[pltpu.SemaphoreType.DMA((8 * len(spans),))],
        cost_estimate=pl.CostEstimate(
            flops=0, bytes_accessed=128 * row * width, transcendentals=0
        ),
        name="spread",
    )(lax.axis_index("c").reshape(1), mine, other)
    return [a.reshape(8 * shard.shape[0], shard.shape[1]) for a, shard in zip(whole, shards)]


def first_step(place, shard, others):
    if not place.tuned:
        return (), others
    half = shard.shape[0] // 2
    own = lax.dynamic_slice_in_dim(shard, place.c * half, half, 0)
    a1, others = lax.optimization_barrier((place.move(own, line=1), others))
    return (own, a1), others


def gather_first(place, info, shard, begun, second, third):
    if not place.tuned:
        return lax.all_gather(shard, "fsdp", axis=0, tiled=True)
    quarter = shard.shape[0] // 4
    own, a1 = begun
    piece = lambda a: lax.dynamic_slice_in_dim(a, place.x * quarter, quarter, 0)
    move = place.move
    b01 = move(jnp.concatenate([piece(own), piece(a1)], 0), pair=1)
    a2 = move(a1, line=1)
    n1 = move(a1, core=1)
    a3 = tied(move(a2, line=1), second)
    x01 = move(b01, side=1)
    n2, m01 = move(a2, core=1), move(b01, core=1)
    b23 = move(jnp.concatenate([piece(a2), piece(a3)], 0), pair=1)
    n3, w01 = move(a3, core=1), move(x01, core=1)
    b23 = tied(b23, third)
    x23, m23 = move(b23, side=1), move(b23, core=1)
    w23 = move(x23, core=1)
    return assemble(info, shard, [a1, a2, a3, n1, n2, n3], [b01, b23, x01, x23, m01, m23, w01, w23])


def gather_small(place, packed):
    return place.move(copies(packed, place.fsdp), every=place.fsdp_axes)


def plus(a, *others):
    total = a.astype(F32)
    for other in others:
        total = total + other.astype(F32)
    return total.astype(BF16)


def weight_grad(place, left, right):
    if not place.tuned:
        return dot_l(left, right).astype(BF16)
    half = right.shape[1] // 2
    columns = lambda core: lax.dynamic_slice_in_dim(right, core * half, half, 1)
    got = place.move(dot_l(left, columns(1 - place.c)).astype(BF16), core=1)
    return (dot_l(left, columns(place.c)) + got.astype(F32)).astype(BF16)


def reduce_stages(place, *grads):
    if not place.tuned:
        parts = [
            lax.psum_scatter(g.astype(F32), "fsdp", scatter_dimension=0, tiled=True) for g in grads
        ]
        return [(lax.psum(part.astype(BF16), "dp").astype(F32),) for part in parts]
    z, y, x, c = place.z, place.y, place.x, place.c
    columns = grads[0].shape[1]
    views = [g.reshape(8, -1, columns) for g in grads]
    value = views[0] if len(views) == 1 else jnp.concatenate(views, 1)
    value = value.reshape(8, 2, -1, columns)
    (got,) = yield [(pick(value, 1 - x, 1), dict(side=1))]
    value = plus(pick(value, x, 1), got)
    value = value.reshape(4, 2, *value.shape[1:])
    (got,) = yield [(pick(value, 1 - y, 1), dict(pair=1))]
    value = plus(pick(value, y, 1), got)
    got = yield [(pick(value, (z + k) % 4, 0), dict(line=k)) for k in (1, 2, 3)]
    value = plus(pick(value, z, 0), *got)
    (got,) = yield [(value, dict(side=1))]
    low, high = jnp.where(x == 0, value, got), jnp.where(x == 0, got, value)
    value = jnp.concatenate([low, high], 0)
    (got,) = yield [(value, dict(core=1))]
    low, high = jnp.where(c == 0, value, got), jnp.where(c == 0, got, value)
    results, row = [], 0
    for view in views:
        rows = slice(row, row + view.shape[1])
        results.append((low[rows].astype(F32), high[rows].astype(F32)))
        row += view.shape[1]
    return results


def joined(*pairs):
    return jnp.concatenate([part for side in zip(*pairs) for part in side], 1)


def sum_replicas(place, part):
    return jnp.sum(place.move(copies(part, place.dp), every=place.dp_axes), 0)


def layer_norm(inputs, gain_row, shift_row):
    center = inputs - jnp.mean(inputs, axis=-1, keepdims=True)
    spread = jnp.mean(center * center, axis=-1, keepdims=True)
    return center * lax.rsqrt(spread + EPSILON) * gain_row + shift_row


def exact_gelu(inputs):
    size = jnp.abs(inputs)
    falling = jnp.exp(-0.5 * inputs * inputs)
    t = 1.0 / (1.0 + (0.3275911 * 0.5**0.5) * size)
    poly = 1.061405429
    for term in (-1.453152027, 1.421413741, -0.284496736, 0.254829592):
        poly = poly * t + term
    tail = 0.5 * poly * t * falling
    phi = jnp.where(inputs < 0, tail, 1.0 - tail)
    return inputs * phi, phi + inputs * falling * (0.5 / math.pi) ** 0.5


def dot_t(a, b):
    return lax.dot_general(a, b, (((1,), (1,)), ((), ())), preferred_element_type=F32)


def dot_l(a, b):
    return lax.dot_general(a, b, (((0,), (0,)), ((), ())), preferred_element_type=F32)


def dot_n(a, b):
    return lax.dot_general(a, b, (((1,), (0,)), ((), ())), preferred_element_type=F32)


def slot_of(index):
    return jnp.floor((index.astype(F32) + 0.5) * (1.0 / SPAN))


def short_bias():
    row = lax.broadcasted_iota(jnp.int32, (CHUNK, CHUNK), 0)
    column = lax.broadcasted_iota(jnp.int32, (CHUNK, CHUNK), 1)
    keep = (slot_of(row) == slot_of(column)) & (column <= row)
    return jnp.where(keep, 0.0, NEG_LARGE)


def short_forward_kernel(q_ref, k_ref, v_ref, out_ref, bias_ref):
    @pl.when(pl.program_id(0) == 0)
    def _():
        bias_ref[...] = short_bias()

    bias = bias_ref[...]
    for chunk in range(SHORT_SLOTS * SPAN // CHUNK):
        rows = pl.ds(chunk * CHUNK, CHUNK)
        scores = dot_t(q_ref[rows, :], k_ref[rows, :]) * SCALE + bias
        top = jnp.max(scores, axis=-1, keepdims=True)
        weights = jnp.exp(scores - top)
        total = jnp.sum(weights, axis=-1, keepdims=True)
        low = (weights * (1.0 / total)).astype(BF16)
        out_ref[rows, :] = dot_n(low, v_ref[rows, :]).astype(BF16)


def block_of(rows, part):
    return pl.BlockSpec(
        (rows, HEAD_DIM), lambda h: (0, (h // GROUP) * 3 * GROUP + part * GROUP + h % GROUP)
    )


def short_forward(projected, rows):
    short_rows = SHORT_SLOTS * SPAN
    return pl.pallas_call(
        short_forward_kernel,
        grid=(HEADS,),
        out_shape=jax.ShapeDtypeStruct((rows, D), BF16),
        in_specs=[block_of(short_rows, part) for part in range(3)],
        out_specs=pl.BlockSpec((short_rows, HEAD_DIM), lambda h: (0, h)),
        scratch_shapes=[pltpu.VMEM((CHUNK, CHUNK), F32)],
        cost_estimate=pl.CostEstimate(
            flops=4 * short_rows * CHUNK * D,
            bytes_accessed=8 * rows * D,
            transcendentals=short_rows * CHUNK * HEADS,
        ),
        name="short_forward",
    )(projected, projected, projected)


def short_backward_kernel(q_ref, k_ref, v_ref, g_ref, out_ref, bias_ref):
    head = pl.program_id(0)

    @pl.when(head == 0)
    def _():
        bias_ref[...] = short_bias()

    bias = bias_ref[...]
    lanes = lambda part: pl.ds(pl.multiple_of((part * GROUP + head) * HEAD_DIM, HEAD_DIM), HEAD_DIM)
    for chunk in range(SHORT_SLOTS * SPAN // CHUNK):
        rows = pl.ds(chunk * CHUNK, CHUNK)
        query, key, grad = q_ref[rows, :], k_ref[rows, :], g_ref[rows, :]
        scores = dot_t(query, key) * SCALE + bias
        top = jnp.max(scores, axis=-1, keepdims=True)
        weights = jnp.exp(scores - top)
        probs = weights * (1.0 / jnp.sum(weights, axis=-1, keepdims=True))
        grad_probs = dot_t(grad, v_ref[rows, :])
        inner = jnp.sum(probs * grad_probs, axis=-1, keepdims=True)
        grad_scores = (probs * (grad_probs - inner)).astype(BF16)
        out_ref[rows, lanes(0)] = (dot_n(grad_scores, key) * SCALE).astype(BF16)
        out_ref[rows, lanes(1)] = (dot_l(grad_scores, query) * SCALE).astype(BF16)
        out_ref[rows, lanes(2)] = dot_l(probs.astype(BF16), grad).astype(BF16)


def short_backward(projected, grad_mixture, group):
    rows = grad_mixture.shape[0]
    short_rows = SHORT_SLOTS * SPAN
    block = lambda first: pl.BlockSpec((short_rows, HEAD_DIM), lambda h: (0, first + h))
    return pl.pallas_call(
        short_backward_kernel,
        grid=(GROUP,),
        out_shape=jax.ShapeDtypeStruct((rows, WIDE), BF16),
        in_specs=[block((group * 3 + part) * GROUP) for part in range(3)] + [block(group * GROUP)],
        out_specs=pl.BlockSpec((rows, WIDE), lambda h: (0, 0)),
        scratch_shapes=[pltpu.VMEM((CHUNK, CHUNK), F32)],
        cost_estimate=pl.CostEstimate(
            flops=10 * short_rows * CHUNK * D // GROUPS,
            bytes_accessed=14 * rows * D // GROUPS,
            transcendentals=short_rows * CHUNK * GROUP,
        ),
        name="short_backward",
    )(projected, projected, projected, grad_mixture)


def long_biases(quarter_ref):
    rows = LONG_SLOTS * SPAN
    row = lax.broadcasted_iota(jnp.int32, (rows, rows), 0)
    column = lax.broadcasted_iota(jnp.int32, (rows, rows), 1)
    slot = slot_of(row)
    same = slot == slot_of(column)
    quarter = jnp.zeros((rows, rows), jnp.int32)
    for index in range(LONG_SLOTS):
        quarter = jnp.where(slot == float(index), quarter_ref[index], quarter)
    keeps = [same & (column <= row)] + [same & (step <= quarter) for step in (1, 2, 3)]
    return [jnp.where(keep, 0.0, NEG_LARGE) for keep in keeps]


def long_probs(query, keys, biases):
    scores = [dot_t(query, key) * SCALE + bias for key, bias in zip(keys, biases)]
    top = scores[0]
    for member in scores[1:]:
        top = jnp.maximum(top, member)
    top = jnp.max(top, axis=-1, keepdims=True)
    weights = [jnp.exp(member - top) for member in scores]
    total = weights[0] + weights[1] + weights[2] + weights[3]
    scale = 1.0 / jnp.sum(total, axis=-1, keepdims=True)
    return [member * scale for member in weights]


def long_forward_kernel(quarter_ref, q, k0, v0, k1, v1, k2, v2, k3, v3, out_ref):
    biases = long_biases(quarter_ref)
    probs = long_probs(q[...], [k[...] for k in (k0, k1, k2, k3)], biases)
    total = None
    for member, value in zip(probs, (v0, v1, v2, v3)):
        part = dot_n(member.astype(BF16), value[...])
        total = part if total is None else total + part
    out_ref[...] = total.astype(BF16)


def long_specs(rows):
    return [block_of(rows, part) for part in range(3)] + [block_of(rows, 1), block_of(rows, 2)] * 3


def long_forward(quarter_index, own, priors):
    rows = own.shape[0]
    spread = [member for prior in priors for member in (prior, prior)]
    return pl.pallas_call(
        long_forward_kernel,
        grid=(HEADS,),
        out_shape=jax.ShapeDtypeStruct((rows, D), BF16),
        in_specs=[pl.BlockSpec(memory_space=pltpu.SMEM)] + long_specs(rows),
        out_specs=pl.BlockSpec((rows, HEAD_DIM), lambda h: (0, h)),
        cost_estimate=pl.CostEstimate(
            flops=16 * rows * rows * D, bytes_accessed=20 * rows * D, transcendentals=0
        ),
        name="long_forward",
    )(quarter_index, own, own, own, *spread)


def long_backward_kernel(
    quarter_ref, q, k0, v0, k1, v1, k2, v2, k3, v3, g, dq_ref, own_ref, s1_ref, s2_ref, s3_ref
):
    biases = long_biases(quarter_ref)
    query, grad = q[...], g[...]
    keys = [k[...] for k in (k0, k1, k2, k3)]
    probs = long_probs(query, keys, biases)
    grads = [dot_t(grad, value[...]) for value in (v0, v1, v2, v3)]
    inner = None
    for member, part in zip(probs, grads):
        inner = member * part if inner is None else inner + member * part
    inner = jnp.sum(inner, axis=-1, keepdims=True)
    total = None
    for index, out in enumerate((own_ref, s1_ref, s2_ref, s3_ref)):
        grad_scores = (probs[index] * (grads[index] - inner)).astype(BF16)
        part = dot_n(grad_scores, keys[index])
        total = part if total is None else total + part
        out[0, :, :] = (dot_l(grad_scores, query) * SCALE).astype(out.dtype)
        out[1, :, :] = dot_l(probs[index].astype(BF16), grad).astype(out.dtype)
    dq_ref[...] = (total * SCALE).astype(BF16)


def long_backward(quarter_index, own, priors, grad_mixture):
    rows = own.shape[0]
    spread = [member for prior in priors for member in (prior, prior)]
    flat = pl.BlockSpec((rows, HEAD_DIM), lambda h: (0, h))
    pair = pl.BlockSpec((2, rows, HEAD_DIM), lambda h: (0, 0, h))
    return pl.pallas_call(
        long_backward_kernel,
        grid=(HEADS,),
        out_shape=[jax.ShapeDtypeStruct((rows, D), BF16)]
        + [jax.ShapeDtypeStruct((2, rows, D), kind) for kind in (F32, BF16, BF16, BF16)],
        in_specs=[pl.BlockSpec(memory_space=pltpu.SMEM)] + long_specs(rows) + [flat],
        out_specs=[flat] + [pair] * 4,
        cost_estimate=pl.CostEstimate(
            flops=40 * rows * rows * D, bytes_accessed=40 * rows * D, transcendentals=0
        ),
        name="long_backward",
    )(quarter_index, own, own, own, *spread, grad_mixture)


def body(
    place,
    series_values,
    quarter_index,
    patch_weight,
    heads_in,
    heads_out,
    expand_weight,
    reduce_weight_shard,
    norm_gains,
    bias_rows,
    expand_bias,
    cotangent,
):
    place.enter()
    fsdp = place.fsdp
    width = patch_weight.shape[1]
    info = jnp.stack([place.z, place.y, place.x, place.c]).astype(jnp.int32) if place.tuned else None
    row_count = series_values.shape[0]
    slot_count = row_count // SPAN
    short_rows = SHORT_SLOTS * SPAN
    long_rows = row_count - short_rows

    mixed_columns = heads_in.reshape(-1, 3, GROUPS, GROUP * HEAD_DIM).transpose(0, 2, 1, 3)
    mixed_columns = mixed_columns.reshape(-1, 3 * D)
    begun, series_values = first_step(place, mixed_columns, series_values)

    long_values = series_values[short_rows:]
    prior_values = [place.along(long_values, step) for step in (1, 2, 3)]

    grouped = series_values.reshape(slot_count, SPAN * PATCH)
    slot_sums = jnp.stack([jnp.sum(grouped, 1), jnp.sum(grouped * grouped, 1)], 1)
    rows_of = lambda a: a.astype(F32).reshape(-1, width)
    sums_row = slot_sums[SHORT_SLOTS:].reshape(1, 2 * LONG_SLOTS)
    sums_row = jnp.pad(sums_row, ((0, 7), (0, width - 2 * LONG_SLOTS)))
    pieces = [rows_of(a) for a in (patch_weight, norm_gains, bias_rows, expand_bias)]
    small_rows = sum(piece.shape[0] for piece in pieces)
    small = gather_small(place, jnp.concatenate(pieces + [sums_row], 0))
    chain = small[:, small_rows, : 2 * LONG_SLOTS].reshape(fsdp, LONG_SLOTS, 2)
    offset = jnp.arange(fsdp)[:, None] - place.f + quarter_index[None, :]
    member = ((offset + fsdp) % fsdp < 4).astype(F32)[:, :, None]
    chain_sum = jnp.sum(chain * member, 0)

    wide = lambda low, high: small[:, low:high].transpose(1, 0, 2).reshape(high - low, D)
    patch_all = wide(0, PATCH).astype(BF16)
    gains_all = wide(PATCH, PATCH + 2)
    biases_all = wide(PATCH + 2, PATCH + 6)
    expand_shift = small[:, PATCH + 6 : small_rows].reshape(-1)

    gather_near = Chain(place, gather_stages(place, heads_out, expand_weight))
    gather_far = Chain(place, gather_stages(place, reduce_weight_shard))
    heads_in_all = gather_first(place, info, mixed_columns, begun, gather_near, gather_far)
    heads_in_all = tied(heads_in_all, gather_near)

    totals = jnp.concatenate([slot_sums[:SHORT_SLOTS], chain_sum], 0)
    counts = jnp.where(jnp.arange(slot_count) < SHORT_SLOTS, SPAN * PATCH, 4 * SPAN * PATCH).astype(
        F32
    )
    slot_mean = totals[:, 0] / counts
    inv_spread = lax.rsqrt(totals[:, 1] / counts - slot_mean * slot_mean + EPSILON)
    normed_slots = (grouped - slot_mean[:, None]) * inv_spread[:, None]
    normed_low = normed_slots.reshape(row_count, PATCH).astype(BF16)
    embedded = dot_n(normed_low, patch_all) + biases_all[0]
    first_value, first_back = jax.vjp(layer_norm, embedded, gains_all[0], biases_all[1])
    first_norm = first_value.astype(BF16)
    prior_normed = [
        (
            (a.reshape(LONG_SLOTS, -1) - slot_mean[SHORT_SLOTS:, None])
            * inv_spread[SHORT_SLOTS:, None]
        ).reshape(long_rows, PATCH)
        for a in prior_values
    ]
    prior_low = jnp.concatenate(prior_normed, 0).astype(BF16)
    prior_embedded = dot_n(prior_low, patch_all) + biases_all[0]
    prior_norms = layer_norm(prior_embedded, gains_all[0], biases_all[1]).astype(BF16)
    prior_norms, heads_in_all = lax.optimization_barrier((prior_norms, heads_in_all))
    projected = dot_n(first_norm, heads_in_all).astype(BF16)
    own_long = projected[short_rows:]
    prior_all = dot_n(prior_norms, heads_in_all).astype(BF16)
    priors = [prior_all[i * long_rows : (i + 1) * long_rows] for i in range(3)]

    mixed_short = short_forward(projected, row_count)
    mixed_long = long_forward(quarter_index, own_long, priors)
    mixed_short, mixed_long = tied((mixed_short, mixed_long), gather_near, gather_far)
    heads_out_all, expand_all = gather_near.finish()
    mixed_all = lax.dynamic_update_slice(mixed_short, mixed_long, (short_rows, 0))
    middle = embedded + dot_n(mixed_all, heads_out_all)
    second_value, second_back = jax.vjp(layer_norm, middle, gains_all[1], biases_all[2])
    second_norm = second_value.astype(BF16)

    pre_act = dot_n(second_norm, expand_all) + expand_shift
    act_value, act_slope = exact_gelu(pre_act)
    activation = tied(act_value.astype(BF16), gather_far)
    grad_reduce = weight_grad(place, activation, cotangent)

    (reduce_all,) = gather_far.finish()
    grad_act = dot_t(cotangent, reduce_all)
    grad_pre = (grad_act * act_slope).astype(BF16)
    grad_expand = weight_grad(place, second_norm, grad_pre)
    grad_expand_bias = jnp.sum(grad_pre.astype(F32), 0)
    grad_second = dot_t(grad_pre, expand_all)
    middle_back, gain_two, shift_two = second_back(grad_second)
    grad_middle = cotangent.astype(F32) + middle_back
    grad_branch = grad_middle.astype(BF16)
    grad_heads_out = weight_grad(place, mixed_all, grad_branch)
    wide = grad_heads_out.shape[1]
    grad_rest = Chain(
        place,
        reduce_stages(
            place, grad_expand[:, :wide], grad_expand[:, wide:], grad_heads_out, grad_reduce
        ),
    )
    grad_mixture = dot_t(grad_branch, heads_out_all).astype(BF16)
    grad_mixture = tied(grad_mixture, grad_rest)

    long_query, own_grads, *sent = long_backward(
        quarter_index, own_long, priors, grad_mixture[short_rows:]
    )
    for step, sent_back in zip((1, 2, 3), sent):
        own_grads = own_grads + place.along(sent_back, -step).astype(F32)
    own_grads = own_grads.astype(BF16)

    def grad_group(g, grad_mixture):
        columns = slice(g * GROUP * HEAD_DIM, (g + 1) * GROUP * HEAD_DIM)
        grad_long = jnp.concatenate([a[:, columns] for a in (long_query, *own_grads)], 1)
        short = short_backward(projected, grad_mixture, g)
        return lax.dynamic_update_slice(short, grad_long, (short_rows, 0))

    grad_projected = grad_group(0, grad_mixture)
    grad_in = Chain(place, reduce_stages(place, weight_grad(place, first_norm, grad_projected)))
    grad_first = dot_t(grad_projected, heads_in_all)
    embed_back, gain_one, shift_one = first_back(grad_first)
    grad_embedded = tied((grad_middle + embed_back).astype(BF16), grad_in)
    grad_patch = dot_l(normed_low, grad_embedded)
    shift_zero = jnp.sum(grad_embedded.astype(F32), 0)
    grad_normed = dot_t(grad_embedded, patch_all).reshape(slot_count, SPAN * PATCH)
    slot_grads = jnp.stack([jnp.sum(grad_normed, 1), jnp.sum(grad_normed * normed_slots, 1)], 1)
    shift_three = jnp.sum(cotangent.astype(F32), 0)
    split = lambda a: a.reshape(-1, fsdp, width).transpose(1, 0, 2)
    chain_row = slot_grads[SHORT_SLOTS:].reshape(1, 2 * LONG_SLOTS)
    chain_row = jnp.pad(chain_row, ((0, 7), (0, width - 2 * LONG_SLOTS)))
    packed = jnp.concatenate(
        [
            split(grad_patch),
            split(jnp.stack([gain_one, gain_two, shift_zero, shift_one, shift_two, shift_three])),
            grad_expand_bias.reshape(fsdp, -1, width),
            jnp.broadcast_to(chain_row, (fsdp,) + chain_row.shape),
        ],
        1,
    )
    packed, activation = tied((packed, activation), grad_rest)
    parts = place.move(packed, every=place.fsdp_axes)
    layer_output = (middle + dot_n(activation, reduce_all) + biases_all[3]).astype(BF16)
    layer_output = tied(layer_output, grad_in)
    layer_output, parts = lax.optimization_barrier((layer_output, parts))
    chain_grads = parts[:, small_rows, : 2 * LONG_SLOTS].reshape(fsdp, LONG_SLOTS, 2)
    chain_grad = jnp.sum(chain_grads * member, 0)
    small_sums = tied(jnp.sum(parts[:, :small_rows], 0), grad_rest)
    small_grads = sum_replicas(place, small_sums)
    grad_totals = jnp.concatenate([slot_grads[:SHORT_SLOTS], chain_grad], 0)
    series_grad = (
        inv_spread[:, None]
        * (
            grad_normed
            - grad_totals[:, 0:1] / counts[:, None]
            - normed_slots * grad_totals[:, 1:2] / counts[:, None]
        )
    ).reshape(row_count, PATCH)
    grad_heads_in = joined(grad_in.finish()[0])
    *expand_pairs, heads_out_pair, reduce_pair = grad_rest.finish()
    return (
        layer_output,
        series_grad,
        small_grads[:PATCH],
        grad_heads_in,
        joined(heads_out_pair),
        joined(*expand_pairs),
        joined(reduce_pair),
        small_grads[PATCH : PATCH + 2],
        small_grads[PATCH + 2 : PATCH + 6],
        small_grads[PATCH + 6 :].reshape(-1),
    )


def solution(mesh):
    tuned = mesh.shape["fsdp"] == 8 and mesh.shape["dp"] == 4
    if tuned:
        mesh = Mesh(mesh.devices.reshape(4, 2, 2, 2), ("z", "y", "x", "c"))
    place = Place(tuned)
    fsdp, both = place.fsdp_axes, place.fsdp_axes + place.dp_axes
    in_specs = (
        P(both, None),
        P(both),
        P(None, fsdp),
        P(fsdp, None),
        P(fsdp, None),
        P(fsdp, None),
        P(fsdp, None),
        P(None, fsdp),
        P(None, fsdp),
        P(fsdp),
        P(both, None),
    )
    out_specs = (
        P(both, None),
        P(both, None),
        P(None, fsdp),
        P(fsdp, None),
        P(fsdp, None),
        P(fsdp, None),
        P(fsdp, None),
        P(None, fsdp),
        P(None, fsdp),
        P(fsdp),
    )
    layer = lambda *arguments: body(place, *arguments)
    return jax.shard_map(layer, mesh=mesh, in_specs=in_specs, out_specs=out_specs, check_vma=False)
```

```python
import math

import jax
import jax.numpy as jnp
from jax import lax
from jax.experimental import pallas as pl
from jax.experimental.pallas import tpu as pltpu
from jax.sharding import Mesh, PartitionSpec as P

D = 1024
HEADS = 8
HEAD_DIM = 128
PATCH = 96
SPAN = 15
SHORT_SLOTS = 48
LONG_SLOTS = 4
CHUNK = 16 * SPAN
GROUPS = 1
GROUP = HEADS // GROUPS
WIDE = 3 * GROUP * HEAD_DIM

EPSILON = 1e-05
NEG_LARGE = -1e30
SCALE = HEAD_DIM ** (-0.5)
F32 = jnp.float32
BF16 = jnp.bfloat16


class Place:
    def __init__(self, tuned):
        self.tuned = tuned
        self.fsdp_axes = ("z", "y") if tuned else ("fsdp",)
        self.dp_axes = ("x", "c") if tuned else ("dp",)

    def enter(self):
        self.fsdp = lax.axis_size(self.fsdp_axes)
        self.dp = lax.axis_size(self.dp_axes)
        self.f = lax.axis_index(self.fsdp_axes)
        self.d = lax.axis_index(self.dp_axes)
        if self.tuned:
            self.z, self.y, self.x, self.c = [lax.axis_index(axis) for axis in "zyxc"]

    def move(self, value, line=0, pair=0, side=0, core=0, every=()):
        if every:
            return lax.all_to_all(value, every, 0, 0, tiled=True)
        pairs = []
        for f in range(self.fsdp):
            for d in range(self.dp):
                z, y, x, c = f // 2, f % 2, d // 2, d % 2
                to_f = ((z + line) % 4) * 2 + (y ^ pair)
                to_d = (x ^ side) * 2 + (c ^ core)
                pairs.append((f * self.dp + d, to_f * self.dp + to_d))
        return lax.ppermute(value, self.fsdp_axes + self.dp_axes, pairs)

    def along(self, value, steps):
        pairs = [(s, (s + steps) % self.fsdp) for s in range(self.fsdp)]
        return lax.ppermute(value, self.fsdp_axes, pairs)


def copies(value, count):
    return jnp.broadcast_to(value, (count,) + value.shape)


def pick(value, index, axis):
    return lax.dynamic_index_in_dim(value, index, axis, keepdims=False)


class Chain:
    def __init__(self, place, stages):
        self.place, self.stages = place, stages
        self.got, self.result = [], None
        self.sends = self.take(None)

    def take(self, got):
        try:
            return self.stages.send(got)
        except StopIteration as end:
            self.result = end.value
            return []

    def prepare(self):
        if self.got:
            self.sends, self.got = self.take(self.got), []

    def launch(self, arrays):
        self.got = [self.place.move(a, **where) for a, (_, where) in zip(arrays, self.sends)]
        self.sends = []

    def finish(self):
        self.prepare()
        while self.sends:
            self.launch([a for a, _ in self.sends])
            self.prepare()
        return self.result


def tied(value, *chains):
    if any(chain.got for chain in chains):
        value, got = lax.optimization_barrier((value, [chain.got for chain in chains]))
        for chain, arrays in zip(chains, got):
            chain.got = arrays
            chain.prepare()
    pending = [[a for a, _ in chain.sends] for chain in chains]
    if any(pending):
        value, pending = lax.optimization_barrier((value, pending))
        for chain, arrays in zip(chains, pending):
            chain.launch(arrays)
    return value


def assemble_kernel(rows, info, own, *refs):
    z, y, x, c = info[0], info[1], info[2], info[3]
    half, quarter = rows // 2, rows // 4
    *parts, out, sem = refs
    near, far = parts[:6], parts[6:]
    count = len(far) // 4
    each = 4 // count
    jobs = []

    def add(src, src_row, dst_row, count):
        jobs.append(
            pltpu.make_async_copy(
                src.at[pl.ds(src_row, count), :],
                out.at[pl.ds(pl.multiple_of(dst_row, 16), count), :],
                sem.at[len(jobs)],
            )
        )

    add(own, 0, (z * 2 + y) * rows, rows)
    for step in (1, 2, 3):
        base = (lax.rem(z + 4 - step, 4) * 2 + y) * rows
        add(near[step - 1], 0, base + c * half, half)
        add(near[step + 2], 0, base + (1 - c) * half, half)
    for step in range(4):
        base = (lax.rem(z + 4 - step, 4) * 2 + (1 - y)) * rows
        for kind, (core, side) in enumerate(((c, x), (c, 1 - x), (1 - c, x), (1 - c, 1 - x))):
            src = far[kind * count + step // each]
            add(src, (step % each) * quarter, base + core * half + side * quarter, quarter)
    for job in jobs:
        job.start()
    for job in jobs:
        job.wait()


def assemble(info, shard, near, far):
    rows, columns = shard.shape
    parts = list(near) + list(far)
    return pl.pallas_call(
        lambda *refs: assemble_kernel(rows, *refs),
        out_shape=jax.ShapeDtypeStruct((8 * rows, columns), shard.dtype),
        in_specs=[pl.BlockSpec(memory_space=pltpu.SMEM)]
        + [pl.BlockSpec(memory_space=pl.ANY)] * (1 + len(parts)),
        out_specs=pl.BlockSpec(memory_space=pltpu.VMEM),
        scratch_shapes=[pltpu.SemaphoreType.DMA((23,))],
        cost_estimate=pl.CostEstimate(
            flops=0, bytes_accessed=32 * rows * columns, transcendentals=0
        ),
        name="assemble",
    )(info, shard, *parts)


def spread_kernel(spans, info, own, other, *refs):
    *outs, sem = refs
    core = info[0]
    jobs = []
    for src, side in ((own, core), (other, 1 - core)):
        for y in range(2):
            for x in range(2):
                for row, rows, out, column in spans:
                    width = src.shape[4]
                    jobs.append(
                        pltpu.make_async_copy(
                            src.at[y, x, :, pl.ds(row, rows), :],
                            outs[out].at[:, y, x, side, :, pl.ds(column, width)],
                            sem.at[len(jobs)],
                        )
                    )
    for job in jobs:
        job.start()
    for job in jobs:
        job.wait()


def gather_stages(place, *shards):
    if not place.tuned:
        return [lax.all_gather(shard, "fsdp", axis=0, tiled=True) for shard in shards]
    width = min(shard.shape[1] for shard in shards)
    pieces, spans, row = [], [], 0
    for out, shard in enumerate(shards):
        rows = shard.shape[0] // 4
        mine = pick(shard.reshape(4, rows, shard.shape[1]), place.d, 0)
        for column in range(0, shard.shape[1], width):
            pieces.append(mine[:, column : column + width])
            spans.append((row, rows, out, column))
            row += rows
    mine = jnp.concatenate(pieces, 0)
    (mine,) = yield [(copies(mine, 4), dict(every=("z",)))]
    (mine,) = yield [(copies(mine, 4), dict(every=("y", "x")))]
    mine = mine.reshape(2, 2, *mine.shape[1:])
    (other,) = yield [(mine, dict(core=1))]
    whole = pl.pallas_call(
        lambda *refs: spread_kernel(spans, *refs),
        out_shape=[
            jax.ShapeDtypeStruct((4, 2, 2, 2, shard.shape[0] // 4, shard.shape[1]), shard.dtype)
            for shard in shards
        ],
        in_specs=[pl.BlockSpec(memory_space=pltpu.SMEM)]
        + [pl.BlockSpec(memory_space=pl.ANY)] * 2,
        out_specs=[pl.BlockSpec(memory_space=pltpu.VMEM)] * len(shards),
        scratch_shapes=[pltpu.SemaphoreType.DMA((8 * len(spans),))],
        cost_estimate=pl.CostEstimate(
            flops=0, bytes_accessed=128 * row * width, transcendentals=0
        ),
        name="spread",
    )(lax.axis_index("c").reshape(1), mine, other)
    return [a.reshape(8 * shard.shape[0], shard.shape[1]) for a, shard in zip(whole, shards)]


def first_step(place, shard, others):
    if not place.tuned:
        return (), others
    half = shard.shape[0] // 2
    own = lax.dynamic_slice_in_dim(shard, place.c * half, half, 0)
    a1, others = lax.optimization_barrier((place.move(own, line=1), others))
    return (own, a1), others


def gather_first(place, info, shard, begun, second, third):
    if not place.tuned:
        return lax.all_gather(shard, "fsdp", axis=0, tiled=True)
    quarter = shard.shape[0] // 4
    own, a1 = begun
    piece = lambda a: lax.dynamic_slice_in_dim(a, place.x * quarter, quarter, 0)
    move = place.move
    b01 = move(jnp.concatenate([piece(own), piece(a1)], 0), pair=1)
    a2 = move(a1, line=1)
    n1 = move(a1, core=1)
    a3 = tied(move(a2, line=1), second)
    x01 = move(b01, side=1)
    n2, m01 = move(a2, core=1), move(b01, core=1)
    b23 = move(jnp.concatenate([piece(a2), piece(a3)], 0), pair=1)
    n3, w01 = move(a3, core=1), move(x01, core=1)
    b23 = tied(b23, third)
    x23, m23 = move(b23, side=1), move(b23, core=1)
    w23 = move(x23, core=1)
    return assemble(info, shard, [a1, a2, a3, n1, n2, n3], [b01, b23, x01, x23, m01, m23, w01, w23])


def gather_small(place, packed):
    return place.move(copies(packed, place.fsdp), every=place.fsdp_axes)


def plus(a, *others):
    total = a.astype(F32)
    for other in others:
        total = total + other.astype(F32)
    return total.astype(BF16)


def weight_grad(place, left, right):
    if not place.tuned:
        return dot_l(left, right).astype(BF16)
    half = right.shape[1] // 2
    columns = lambda core: lax.dynamic_slice_in_dim(right, core * half, half, 1)
    got = place.move(dot_l(left, columns(1 - place.c)).astype(BF16), core=1)
    return (dot_l(left, columns(place.c)) + got.astype(F32)).astype(BF16)


def side_half(place, grad):
    if not place.tuned:
        return grad, ()
    view = grad.reshape(8, 2, -1, grad.shape[1])
    return pick(view, place.x, 1), pick(view, 1 - place.x, 1)


def send_side(place, values):
    return [place.move(a, side=1) for a in values] if place.tuned else values


def native_sums(grads):
    parts = [
        lax.psum_scatter(g.astype(F32), "fsdp", scatter_dimension=0, tiled=True) for g in grads
    ]
    return [(lax.psum(part.astype(BF16), "dp").astype(F32),) for part in parts]


def last_stages(place, value):
    (z, x, c) = place.z, place.x, place.c
    got = yield [(pick(value, (z + k) % 4, 0), dict(line=k)) for k in (1, 2, 3)]
    value = plus(pick(value, z, 0), *got)
    (got,) = yield [(value, dict(side=1))]
    low, high = jnp.where(x == 0, value, got), jnp.where(x == 0, got, value)
    value = jnp.concatenate([low, high], -2)
    (got,) = yield [(value, dict(core=1))]
    low, high = jnp.where(c == 0, value, got), jnp.where(c == 0, got, value)
    return low.astype(F32), high.astype(F32)


def merged_stages(place, owns, gots):
    if not place.tuned:
        return native_sums(owns)
    width = min(own.shape[2] for own in owns)
    pieces = []
    for own, got in zip(owns, gots):
        value = plus(own, got)
        pieces += [value[:, :, i : i + width] for i in range(0, own.shape[2], width)]
    value = jnp.concatenate(pieces, 1).reshape(4, 2, -1, width)
    (got,) = yield [(pick(value, 1 - place.y, 1), dict(pair=1))]
    low, high = yield from last_stages(place, plus(pick(value, place.y, 1), got))
    results, row = [], 0
    halves = lambda a: a.reshape(2, -1, width)
    for own in owns:
        rows, parts = own.shape[1], []
        for side in (halves(low), halves(high)):
            for i in range(0, own.shape[2], width):
                start = row + i // width * rows
                parts.append(side[:, start : start + rows].reshape(2 * rows, width))
        row += rows * (own.shape[2] // width)
        results.append(parts)
    return results


def reduce_stages(place, grad, side_first):
    if not place.tuned:
        return native_sums([grad])[0]
    x, y = place.x, place.y
    columns = grad.shape[1]
    if side_first:
        value = grad.reshape(8, 2, -1, columns)
        (got,) = yield [(pick(value, 1 - x, 1), dict(side=1))]
        value = plus(pick(value, x, 1), got).reshape(4, 2, -1, columns)
        (got,) = yield [(pick(value, 1 - y, 1), dict(pair=1))]
        value = plus(pick(value, y, 1), got)
    else:
        value = grad.reshape(4, 2, -1, columns)
        (got,) = yield [(pick(value, 1 - y, 1), dict(pair=1))]
        value = plus(pick(value, y, 1), got).reshape(4, 2, -1, columns)
        (got,) = yield [(pick(value, 1 - x, 1), dict(side=1))]
        value = plus(pick(value, x, 1), got)
    return (yield from last_stages(place, value))


def sum_replicas(place, part):
    return jnp.sum(place.move(copies(part, place.dp), every=place.dp_axes), 0)


def layer_norm(inputs, gain_row, shift_row):
    center = inputs - jnp.mean(inputs, axis=-1, keepdims=True)
    spread = jnp.mean(center * center, axis=-1, keepdims=True)
    return center * lax.rsqrt(spread + EPSILON) * gain_row + shift_row


def exact_gelu(inputs):
    size = jnp.abs(inputs)
    falling = jnp.exp(-0.5 * inputs * inputs)
    t = 1.0 / (1.0 + (0.3275911 * 0.5**0.5) * size)
    poly = 1.061405429
    for term in (-1.453152027, 1.421413741, -0.284496736, 0.254829592):
        poly = poly * t + term
    tail = 0.5 * poly * t * falling
    phi = jnp.where(inputs < 0, tail, 1.0 - tail)
    return inputs * phi, phi + inputs * falling * (0.5 / math.pi) ** 0.5


def dot_t(a, b):
    return lax.dot_general(a, b, (((1,), (1,)), ((), ())), preferred_element_type=F32)


def dot_l(a, b):
    return lax.dot_general(a, b, (((0,), (0,)), ((), ())), preferred_element_type=F32)


def dot_n(a, b):
    return lax.dot_general(a, b, (((1,), (0,)), ((), ())), preferred_element_type=F32)


def slot_of(index):
    return jnp.floor((index.astype(F32) + 0.5) * (1.0 / SPAN))


def short_bias():
    row = lax.broadcasted_iota(jnp.int32, (CHUNK, CHUNK), 0)
    column = lax.broadcasted_iota(jnp.int32, (CHUNK, CHUNK), 1)
    keep = (slot_of(row) == slot_of(column)) & (column <= row)
    return jnp.where(keep, 0.0, NEG_LARGE)


def short_forward_kernel(q_ref, k_ref, v_ref, out_ref, bias_ref):
    @pl.when(pl.program_id(0) == 0)
    def _():
        bias_ref[...] = short_bias()

    bias = bias_ref[...]
    for chunk in range(SHORT_SLOTS * SPAN // CHUNK):
        rows = pl.ds(chunk * CHUNK, CHUNK)
        scores = dot_t(q_ref[rows, :], k_ref[rows, :]) * SCALE + bias
        top = jnp.max(scores, axis=-1, keepdims=True)
        weights = jnp.exp(scores - top)
        total = jnp.sum(weights, axis=-1, keepdims=True)
        low = (weights * (1.0 / total)).astype(BF16)
        out_ref[rows, :] = dot_n(low, v_ref[rows, :]).astype(BF16)


def block_of(rows, part):
    return pl.BlockSpec(
        (rows, HEAD_DIM), lambda h: (0, (h // GROUP) * 3 * GROUP + part * GROUP + h % GROUP)
    )


def short_forward(projected, rows):
    short_rows = SHORT_SLOTS * SPAN
    return pl.pallas_call(
        short_forward_kernel,
        grid=(HEADS,),
        out_shape=jax.ShapeDtypeStruct((rows, D), BF16),
        in_specs=[block_of(short_rows, part) for part in range(3)],
        out_specs=pl.BlockSpec((short_rows, HEAD_DIM), lambda h: (0, h)),
        scratch_shapes=[pltpu.VMEM((CHUNK, CHUNK), F32)],
        cost_estimate=pl.CostEstimate(
            flops=4 * short_rows * CHUNK * D,
            bytes_accessed=8 * rows * D,
            transcendentals=short_rows * CHUNK * HEADS,
        ),
        name="short_forward",
    )(projected, projected, projected)


def short_backward_kernel(q_ref, k_ref, v_ref, g_ref, out_ref, bias_ref):
    head = pl.program_id(0)

    @pl.when(head == 0)
    def _():
        bias_ref[...] = short_bias()

    bias = bias_ref[...]
    lanes = lambda part: pl.ds(pl.multiple_of((part * GROUP + head) * HEAD_DIM, HEAD_DIM), HEAD_DIM)
    for chunk in range(SHORT_SLOTS * SPAN // CHUNK):
        rows = pl.ds(chunk * CHUNK, CHUNK)
        query, key, grad = q_ref[rows, :], k_ref[rows, :], g_ref[rows, :]
        scores = dot_t(query, key) * SCALE + bias
        top = jnp.max(scores, axis=-1, keepdims=True)
        weights = jnp.exp(scores - top)
        probs = weights * (1.0 / jnp.sum(weights, axis=-1, keepdims=True))
        grad_probs = dot_t(grad, v_ref[rows, :])
        inner = jnp.sum(probs * grad_probs, axis=-1, keepdims=True)
        grad_scores = (probs * (grad_probs - inner)).astype(BF16)
        out_ref[rows, lanes(0)] = (dot_n(grad_scores, key) * SCALE).astype(BF16)
        out_ref[rows, lanes(1)] = (dot_l(grad_scores, query) * SCALE).astype(BF16)
        out_ref[rows, lanes(2)] = dot_l(probs.astype(BF16), grad).astype(BF16)


def short_backward(projected, grad_mixture, group):
    rows = grad_mixture.shape[0]
    short_rows = SHORT_SLOTS * SPAN
    block = lambda first: pl.BlockSpec((short_rows, HEAD_DIM), lambda h: (0, first + h))
    return pl.pallas_call(
        short_backward_kernel,
        grid=(GROUP,),
        out_shape=jax.ShapeDtypeStruct((rows, WIDE), BF16),
        in_specs=[block((group * 3 + part) * GROUP) for part in range(3)] + [block(group * GROUP)],
        out_specs=pl.BlockSpec((rows, WIDE), lambda h: (0, 0)),
        scratch_shapes=[pltpu.VMEM((CHUNK, CHUNK), F32)],
        cost_estimate=pl.CostEstimate(
            flops=10 * short_rows * CHUNK * D // GROUPS,
            bytes_accessed=14 * rows * D // GROUPS,
            transcendentals=short_rows * CHUNK * GROUP,
        ),
        name="short_backward",
    )(projected, projected, projected, grad_mixture)


def long_biases(quarter_ref):
    rows = LONG_SLOTS * SPAN
    row = lax.broadcasted_iota(jnp.int32, (rows, rows), 0)
    column = lax.broadcasted_iota(jnp.int32, (rows, rows), 1)
    slot = slot_of(row)
    same = slot == slot_of(column)
    quarter = jnp.zeros((rows, rows), jnp.int32)
    for index in range(LONG_SLOTS):
        quarter = jnp.where(slot == float(index), quarter_ref[index], quarter)
    keeps = [same & (column <= row)] + [same & (step <= quarter) for step in (1, 2, 3)]
    return [jnp.where(keep, 0.0, NEG_LARGE) for keep in keeps]


def long_probs(query, keys, biases):
    scores = [dot_t(query, key) * SCALE + bias for key, bias in zip(keys, biases)]
    top = scores[0]
    for member in scores[1:]:
        top = jnp.maximum(top, member)
    top = jnp.max(top, axis=-1, keepdims=True)
    weights = [jnp.exp(member - top) for member in scores]
    total = weights[0] + weights[1] + weights[2] + weights[3]
    scale = 1.0 / jnp.sum(total, axis=-1, keepdims=True)
    return [member * scale for member in weights]


def long_forward_kernel(quarter_ref, q, k0, v0, k1, v1, k2, v2, k3, v3, out_ref):
    biases = long_biases(quarter_ref)
    probs = long_probs(q[...], [k[...] for k in (k0, k1, k2, k3)], biases)
    total = None
    for member, value in zip(probs, (v0, v1, v2, v3)):
        part = dot_n(member.astype(BF16), value[...])
        total = part if total is None else total + part
    out_ref[...] = total.astype(BF16)


def long_specs(rows):
    return [block_of(rows, part) for part in range(3)] + [block_of(rows, 1), block_of(rows, 2)] * 3


def long_forward(quarter_index, own, priors):
    rows = own.shape[0]
    spread = [member for prior in priors for member in (prior, prior)]
    return pl.pallas_call(
        long_forward_kernel,
        grid=(HEADS,),
        out_shape=jax.ShapeDtypeStruct((rows, D), BF16),
        in_specs=[pl.BlockSpec(memory_space=pltpu.SMEM)] + long_specs(rows),
        out_specs=pl.BlockSpec((rows, HEAD_DIM), lambda h: (0, h)),
        cost_estimate=pl.CostEstimate(
            flops=16 * rows * rows * D, bytes_accessed=20 * rows * D, transcendentals=0
        ),
        name="long_forward",
    )(quarter_index, own, own, own, *spread)


def long_backward_kernel(
    quarter_ref, q, k0, v0, k1, v1, k2, v2, k3, v3, g, dq_ref, own_ref, s1_ref, s2_ref, s3_ref
):
    biases = long_biases(quarter_ref)
    query, grad = q[...], g[...]
    keys = [k[...] for k in (k0, k1, k2, k3)]
    probs = long_probs(query, keys, biases)
    grads = [dot_t(grad, value[...]) for value in (v0, v1, v2, v3)]
    inner = None
    for member, part in zip(probs, grads):
        inner = member * part if inner is None else inner + member * part
    inner = jnp.sum(inner, axis=-1, keepdims=True)
    total = None
    for index, out in enumerate((own_ref, s1_ref, s2_ref, s3_ref)):
        grad_scores = (probs[index] * (grads[index] - inner)).astype(BF16)
        part = dot_n(grad_scores, keys[index])
        total = part if total is None else total + part
        out[0, :, :] = (dot_l(grad_scores, query) * SCALE).astype(out.dtype)
        out[1, :, :] = dot_l(probs[index].astype(BF16), grad).astype(out.dtype)
    dq_ref[...] = (total * SCALE).astype(BF16)


def long_backward(quarter_index, own, priors, grad_mixture):
    rows = own.shape[0]
    spread = [member for prior in priors for member in (prior, prior)]
    flat = pl.BlockSpec((rows, HEAD_DIM), lambda h: (0, h))
    pair = pl.BlockSpec((2, rows, HEAD_DIM), lambda h: (0, 0, h))
    return pl.pallas_call(
        long_backward_kernel,
        grid=(HEADS,),
        out_shape=[jax.ShapeDtypeStruct((rows, D), BF16)]
        + [jax.ShapeDtypeStruct((2, rows, D), kind) for kind in (F32, BF16, BF16, BF16)],
        in_specs=[pl.BlockSpec(memory_space=pltpu.SMEM)] + long_specs(rows) + [flat],
        out_specs=[flat] + [pair] * 4,
        cost_estimate=pl.CostEstimate(
            flops=40 * rows * rows * D, bytes_accessed=40 * rows * D, transcendentals=0
        ),
        name="long_backward",
    )(quarter_index, own, own, own, *spread, grad_mixture)


def body(
    place,
    series_values,
    quarter_index,
    patch_weight,
    heads_in,
    heads_out,
    expand_weight,
    reduce_weight_shard,
    norm_gains,
    bias_rows,
    expand_bias,
    cotangent,
):
    place.enter()
    fsdp = place.fsdp
    width = patch_weight.shape[1]
    info = jnp.stack([place.z, place.y, place.x, place.c]).astype(jnp.int32) if place.tuned else None
    row_count = series_values.shape[0]
    slot_count = row_count // SPAN
    short_rows = SHORT_SLOTS * SPAN
    long_rows = row_count - short_rows

    mixed_columns = heads_in.reshape(-1, 3, GROUPS, GROUP * HEAD_DIM).transpose(0, 2, 1, 3)
    mixed_columns = mixed_columns.reshape(-1, 3 * D)
    begun, series_values = first_step(place, mixed_columns, series_values)

    long_values = series_values[short_rows:]
    prior_values = [place.along(long_values, step) for step in (1, 2, 3)]

    grouped = series_values.reshape(slot_count, SPAN * PATCH)
    slot_sums = jnp.stack([jnp.sum(grouped, 1), jnp.sum(grouped * grouped, 1)], 1)
    rows_of = lambda a: a.astype(F32).reshape(-1, width)
    sums_row = slot_sums[SHORT_SLOTS:].reshape(1, 2 * LONG_SLOTS)
    sums_row = jnp.pad(sums_row, ((0, 7), (0, width - 2 * LONG_SLOTS)))
    pieces = [rows_of(a) for a in (patch_weight, norm_gains, bias_rows, expand_bias)]
    small_rows = sum(piece.shape[0] for piece in pieces)
    small = gather_small(place, jnp.concatenate(pieces + [sums_row], 0))
    chain = small[:, small_rows, : 2 * LONG_SLOTS].reshape(fsdp, LONG_SLOTS, 2)
    offset = jnp.arange(fsdp)[:, None] - place.f + quarter_index[None, :]
    member = ((offset + fsdp) % fsdp < 4).astype(F32)[:, :, None]
    chain_sum = jnp.sum(chain * member, 0)

    wide = lambda low, high: small[:, low:high].transpose(1, 0, 2).reshape(high - low, D)
    patch_all = wide(0, PATCH).astype(BF16)
    gains_all = wide(PATCH, PATCH + 2)
    biases_all = wide(PATCH + 2, PATCH + 6)
    expand_shift = small[:, PATCH + 6 : small_rows].reshape(-1)

    gather_near = Chain(place, gather_stages(place, heads_out, expand_weight))
    gather_far = Chain(place, gather_stages(place, reduce_weight_shard))
    heads_in_all = gather_first(place, info, mixed_columns, begun, gather_near, gather_far)
    heads_in_all = tied(heads_in_all, gather_near)

    totals = jnp.concatenate([slot_sums[:SHORT_SLOTS], chain_sum], 0)
    counts = jnp.where(jnp.arange(slot_count) < SHORT_SLOTS, SPAN * PATCH, 4 * SPAN * PATCH).astype(
        F32
    )
    slot_mean = totals[:, 0] / counts
    inv_spread = lax.rsqrt(totals[:, 1] / counts - slot_mean * slot_mean + EPSILON)
    normed_slots = (grouped - slot_mean[:, None]) * inv_spread[:, None]
    normed_low = normed_slots.reshape(row_count, PATCH).astype(BF16)
    embedded = dot_n(normed_low, patch_all) + biases_all[0]
    first_value, first_back = jax.vjp(layer_norm, embedded, gains_all[0], biases_all[1])
    first_norm = first_value.astype(BF16)
    prior_normed = [
        (
            (a.reshape(LONG_SLOTS, -1) - slot_mean[SHORT_SLOTS:, None])
            * inv_spread[SHORT_SLOTS:, None]
        ).reshape(long_rows, PATCH)
        for a in prior_values
    ]
    prior_low = jnp.concatenate(prior_normed, 0).astype(BF16)
    prior_embedded = dot_n(prior_low, patch_all) + biases_all[0]
    prior_norms = layer_norm(prior_embedded, gains_all[0], biases_all[1]).astype(BF16)
    prior_norms, heads_in_all = lax.optimization_barrier((prior_norms, heads_in_all))
    projected = dot_n(first_norm, heads_in_all).astype(BF16)
    own_long = projected[short_rows:]
    prior_all = dot_n(prior_norms, heads_in_all).astype(BF16)
    priors = [prior_all[i * long_rows : (i + 1) * long_rows] for i in range(3)]

    mixed_short = short_forward(projected, row_count)
    mixed_long = long_forward(quarter_index, own_long, priors)
    mixed_short, mixed_long = tied((mixed_short, mixed_long), gather_near, gather_far)
    heads_out_all, expand_all = gather_near.finish()
    mixed_all = lax.dynamic_update_slice(mixed_short, mixed_long, (short_rows, 0))
    middle = embedded + dot_n(mixed_all, heads_out_all)
    second_value, second_back = jax.vjp(layer_norm, middle, gains_all[1], biases_all[2])
    second_norm = second_value.astype(BF16)

    pre_act = dot_n(second_norm, expand_all) + expand_shift
    act_value, act_slope = exact_gelu(pre_act)
    activation = tied(act_value.astype(BF16), gather_far)
    grad_reduce = weight_grad(place, activation, cotangent)

    (reduce_all,) = gather_far.finish()
    grad_act = dot_t(cotangent, reduce_all)
    grad_pre = (grad_act * act_slope).astype(BF16)
    own_reduce, sent_reduce = side_half(place, grad_reduce)
    grad_pre, sent_reduce = lax.optimization_barrier((grad_pre, sent_reduce))
    (got_reduce,) = send_side(place, [sent_reduce])
    grad_expand = weight_grad(place, second_norm, grad_pre)
    grad_expand_bias = jnp.sum(grad_pre.astype(F32), 0)
    grad_second = dot_t(grad_pre, expand_all)
    middle_back, gain_two, shift_two = second_back(grad_second)
    grad_middle = cotangent.astype(F32) + middle_back
    grad_branch = grad_middle.astype(BF16)
    grad_heads_out = weight_grad(place, mixed_all, grad_branch)
    own_expand, sent_expand = side_half(place, grad_expand)
    own_out, sent_out = side_half(place, grad_heads_out)
    grad_mixture = dot_t(grad_branch, heads_out_all).astype(BF16)
    grad_mixture, sent = lax.optimization_barrier((grad_mixture, [sent_expand, sent_out]))
    got_expand, got_out = send_side(place, sent)

    long_query, own_grads, *sent = long_backward(
        quarter_index, own_long, priors, grad_mixture[short_rows:]
    )
    for step, sent_back in zip((1, 2, 3), sent):
        own_grads = own_grads + place.along(sent_back, -step).astype(F32)
    own_grads = own_grads.astype(BF16)

    def grad_group(g, grad_mixture):
        columns = slice(g * GROUP * HEAD_DIM, (g + 1) * GROUP * HEAD_DIM)
        grad_long = jnp.concatenate([a[:, columns] for a in (long_query, *own_grads)], 1)
        short = short_backward(projected, grad_mixture, g)
        return lax.dynamic_update_slice(short, grad_long, (short_rows, 0))

    grad_mixture, long_query, got_reduce = lax.optimization_barrier(
        (grad_mixture, long_query, got_reduce)
    )
    grad_projected = grad_group(0, grad_mixture)
    grad_in = weight_grad(place, first_norm, grad_projected)
    heads_in_all, gots = lax.optimization_barrier(
        (heads_in_all, [got_expand, got_out, got_reduce])
    )
    owns = [own_expand, own_out, own_reduce]
    grad_rest = Chain(place, merged_stages(place, owns, gots))
    heads_in_all = tied(heads_in_all, grad_rest)
    middle_column = grad_in.shape[1] // 2
    grad_low = Chain(place, reduce_stages(place, grad_in[:, :middle_column], True))
    grad_high = Chain(place, reduce_stages(place, grad_in[:, middle_column:], False))
    grad_first = dot_t(grad_projected, heads_in_all)
    embed_back, gain_one, shift_one = first_back(grad_first)
    grad_embedded = tied((grad_middle + embed_back).astype(BF16), grad_low, grad_high)
    grad_patch = dot_l(normed_low, grad_embedded)
    shift_zero = jnp.sum(grad_embedded.astype(F32), 0)
    grad_normed = dot_t(grad_embedded, patch_all).reshape(slot_count, SPAN * PATCH)
    slot_grads = jnp.stack([jnp.sum(grad_normed, 1), jnp.sum(grad_normed * normed_slots, 1)], 1)
    shift_three = jnp.sum(cotangent.astype(F32), 0)
    split = lambda a: a.reshape(-1, fsdp, width).transpose(1, 0, 2)
    chain_row = slot_grads[SHORT_SLOTS:].reshape(1, 2 * LONG_SLOTS)
    chain_row = jnp.pad(chain_row, ((0, 7), (0, width - 2 * LONG_SLOTS)))
    packed = jnp.concatenate(
        [
            split(grad_patch),
            split(jnp.stack([gain_one, gain_two, shift_zero, shift_one, shift_two, shift_three])),
            grad_expand_bias.reshape(fsdp, -1, width),
            jnp.broadcast_to(chain_row, (fsdp,) + chain_row.shape),
        ],
        1,
    )
    packed, activation = tied((packed, activation), grad_rest)
    parts = place.move(packed, every=place.fsdp_axes)
    layer_output = (middle + dot_n(activation, reduce_all) + biases_all[3]).astype(BF16)
    layer_output = tied(layer_output, grad_low, grad_high)
    layer_output, parts = lax.optimization_barrier((layer_output, parts))
    chain_grads = parts[:, small_rows, : 2 * LONG_SLOTS].reshape(fsdp, LONG_SLOTS, 2)
    chain_grad = jnp.sum(chain_grads * member, 0)
    small_sums = tied(jnp.sum(parts[:, :small_rows], 0), grad_low, grad_high, grad_rest)
    small_grads = sum_replicas(place, small_sums)
    grad_totals = jnp.concatenate([slot_grads[:SHORT_SLOTS], chain_grad], 0)
    series_grad = (
        inv_spread[:, None]
        * (
            grad_normed
            - grad_totals[:, 0:1] / counts[:, None]
            - normed_slots * grad_totals[:, 1:2] / counts[:, None]
        )
    ).reshape(row_count, PATCH)
    if place.tuned:
        ((low_own, low_other), (high_own, high_other)) = grad_low.finish(), grad_high.finish()
        in_parts = [low_own, high_own, low_other, high_other]
    else:
        in_parts = [*grad_low.finish(), *grad_high.finish()]
    grad_heads_in = jnp.concatenate(in_parts, 1)
    grad_expand, grad_heads_out, grad_reduce = [
        jnp.concatenate(parts, 1) for parts in grad_rest.finish()
    ]
    return (
        layer_output,
        series_grad,
        small_grads[:PATCH],
        grad_heads_in,
        grad_heads_out,
        grad_expand,
        grad_reduce,
        small_grads[PATCH : PATCH + 2],
        small_grads[PATCH + 2 : PATCH + 6],
        small_grads[PATCH + 6 :].reshape(-1),
    )


def solution(mesh):
    tuned = mesh.shape["fsdp"] == 8 and mesh.shape["dp"] == 4
    if tuned:
        mesh = Mesh(mesh.devices.reshape(4, 2, 2, 2), ("z", "y", "x", "c"))
    place = Place(tuned)
    fsdp, both = place.fsdp_axes, place.fsdp_axes + place.dp_axes
    in_specs = (
        P(both, None),
        P(both),
        P(None, fsdp),
        P(fsdp, None),
        P(fsdp, None),
        P(fsdp, None),
        P(fsdp, None),
        P(None, fsdp),
        P(None, fsdp),
        P(fsdp),
        P(both, None),
    )
    out_specs = (
        P(both, None),
        P(both, None),
        P(None, fsdp),
        P(fsdp, None),
        P(fsdp, None),
        P(fsdp, None),
        P(fsdp, None),
        P(None, fsdp),
        P(None, fsdp),
        P(fsdp),
    )
    layer = lambda *arguments: body(place, *arguments)
    return jax.shard_map(layer, mesh=mesh, in_specs=in_specs, out_specs=out_specs, check_vma=False)
```

```python
import math

import jax
import jax.numpy as jnp
from jax import lax
from jax.experimental import pallas as pl
from jax.experimental.pallas import tpu as pltpu
from jax.sharding import Mesh, PartitionSpec as P

D = 1024
HEADS = 8
HEAD_DIM = 128
PATCH = 96
SPAN = 15
SHORT_SLOTS = 48
LONG_SLOTS = 4
CHUNK = 16 * SPAN
GROUPS = 1
GROUP = HEADS // GROUPS
WIDE = 3 * GROUP * HEAD_DIM

EPSILON = 1e-05
NEG_LARGE = -1e30
SCALE = HEAD_DIM ** (-0.5)
F32 = jnp.float32
BF16 = jnp.bfloat16


class Place:
    def __init__(self, tuned):
        self.tuned = tuned
        self.fsdp_axes = ("z", "y") if tuned else ("fsdp",)
        self.dp_axes = ("x", "c") if tuned else ("dp",)

    def enter(self):
        self.fsdp = lax.axis_size(self.fsdp_axes)
        self.dp = lax.axis_size(self.dp_axes)
        self.f = lax.axis_index(self.fsdp_axes)
        self.d = lax.axis_index(self.dp_axes)
        if self.tuned:
            self.z, self.y, self.x, self.c = [lax.axis_index(axis) for axis in "zyxc"]

    def move(self, value, line=0, pair=0, side=0, core=0, every=()):
        if every:
            return lax.all_to_all(value, every, 0, 0, tiled=True)
        pairs = []
        for f in range(self.fsdp):
            for d in range(self.dp):
                z, y, x, c = f // 2, f % 2, d // 2, d % 2
                to_f = ((z + line) % 4) * 2 + (y ^ pair)
                to_d = (x ^ side) * 2 + (c ^ core)
                pairs.append((f * self.dp + d, to_f * self.dp + to_d))
        return lax.ppermute(value, self.fsdp_axes + self.dp_axes, pairs)

    def along(self, value, steps):
        pairs = [(s, (s + steps) % self.fsdp) for s in range(self.fsdp)]
        return lax.ppermute(value, self.fsdp_axes, pairs)


def copies(value, count):
    return jnp.broadcast_to(value, (count,) + value.shape)


def pick(value, index, axis):
    return lax.dynamic_index_in_dim(value, index, axis, keepdims=False)


class Chain:
    def __init__(self, place, stages):
        self.place, self.stages = place, stages
        self.got, self.result = [], None
        self.sends = self.take(None)

    def take(self, got):
        try:
            return self.stages.send(got)
        except StopIteration as end:
            self.result = end.value
            return []

    def prepare(self):
        if self.got:
            self.sends, self.got = self.take(self.got), []

    def launch(self, arrays):
        self.got = [self.place.move(a, **where) for a, (_, where) in zip(arrays, self.sends)]
        self.sends = []

    def finish(self):
        self.prepare()
        while self.sends:
            self.launch([a for a, _ in self.sends])
            self.prepare()
        return self.result


def tied(value, *chains):
    if any(chain.got for chain in chains):
        value, got = lax.optimization_barrier((value, [chain.got for chain in chains]))
        for chain, arrays in zip(chains, got):
            chain.got = arrays
            chain.prepare()
    pending = [[a for a, _ in chain.sends] for chain in chains]
    if any(pending):
        value, pending = lax.optimization_barrier((value, pending))
        for chain, arrays in zip(chains, pending):
            chain.launch(arrays)
    return value


def assemble_kernel(rows, info, own, *refs):
    z, y, x, c = info[0], info[1], info[2], info[3]
    half, quarter = rows // 2, rows // 4
    *parts, out, sem = refs
    near, far = parts[:6], parts[6:]
    count = len(far) // 4
    each = 4 // count
    jobs = []

    def add(src, src_row, dst_row, count):
        jobs.append(
            pltpu.make_async_copy(
                src.at[pl.ds(src_row, count), :],
                out.at[pl.ds(pl.multiple_of(dst_row, 16), count), :],
                sem.at[len(jobs)],
            )
        )

    add(own, 0, (z * 2 + y) * rows, rows)
    for step in (1, 2, 3):
        base = (lax.rem(z + 4 - step, 4) * 2 + y) * rows
        add(near[step - 1], 0, base + c * half, half)
        add(near[step + 2], 0, base + (1 - c) * half, half)
    for step in range(4):
        base = (lax.rem(z + 4 - step, 4) * 2 + (1 - y)) * rows
        for kind, (core, side) in enumerate(((c, x), (c, 1 - x), (1 - c, x), (1 - c, 1 - x))):
            src = far[kind * count + step // each]
            add(src, (step % each) * quarter, base + core * half + side * quarter, quarter)
    for job in jobs:
        job.start()
    for job in jobs:
        job.wait()


def assemble(info, shard, near, far):
    rows, columns = shard.shape
    parts = list(near) + list(far)
    return pl.pallas_call(
        lambda *refs: assemble_kernel(rows, *refs),
        out_shape=jax.ShapeDtypeStruct((8 * rows, columns), shard.dtype),
        in_specs=[pl.BlockSpec(memory_space=pltpu.SMEM)]
        + [pl.BlockSpec(memory_space=pl.ANY)] * (1 + len(parts)),
        out_specs=pl.BlockSpec(memory_space=pltpu.VMEM),
        scratch_shapes=[pltpu.SemaphoreType.DMA((23,))],
        cost_estimate=pl.CostEstimate(
            flops=0, bytes_accessed=32 * rows * columns, transcendentals=0
        ),
        name="assemble",
    )(info, shard, *parts)


def spread_kernel(spans, info, own, other, *refs):
    *outs, sem = refs
    core = info[0]
    jobs = []
    for src, side in ((own, core), (other, 1 - core)):
        for y in range(2):
            for x in range(2):
                for row, rows, out, column in spans:
                    width = src.shape[4]
                    jobs.append(
                        pltpu.make_async_copy(
                            src.at[y, x, :, pl.ds(row, rows), :],
                            outs[out].at[:, y, x, side, :, pl.ds(column, width)],
                            sem.at[len(jobs)],
                        )
                    )
    for job in jobs:
        job.start()
    for job in jobs:
        job.wait()


def gather_stages(place, *shards):
    if not place.tuned:
        return [lax.all_gather(shard, "fsdp", axis=0, tiled=True) for shard in shards]
    width = min(shard.shape[1] for shard in shards)
    pieces, spans, row = [], [], 0
    for out, shard in enumerate(shards):
        rows = shard.shape[0] // 4
        mine = pick(shard.reshape(4, rows, shard.shape[1]), place.d, 0)
        for column in range(0, shard.shape[1], width):
            pieces.append(mine[:, column : column + width])
            spans.append((row, rows, out, column))
            row += rows
    mine = jnp.concatenate(pieces, 0)
    (mine,) = yield [(copies(mine, 4), dict(every=("z",)))]
    (mine,) = yield [(copies(mine, 4), dict(every=("y", "x")))]
    mine = mine.reshape(2, 2, *mine.shape[1:])
    (other,) = yield [(mine, dict(core=1))]
    whole = pl.pallas_call(
        lambda *refs: spread_kernel(spans, *refs),
        out_shape=[
            jax.ShapeDtypeStruct((4, 2, 2, 2, shard.shape[0] // 4, shard.shape[1]), shard.dtype)
            for shard in shards
        ],
        in_specs=[pl.BlockSpec(memory_space=pltpu.SMEM)]
        + [pl.BlockSpec(memory_space=pl.ANY)] * 2,
        out_specs=[pl.BlockSpec(memory_space=pltpu.VMEM)] * len(shards),
        scratch_shapes=[pltpu.SemaphoreType.DMA((8 * len(spans),))],
        cost_estimate=pl.CostEstimate(
            flops=0, bytes_accessed=128 * row * width, transcendentals=0
        ),
        name="spread",
    )(lax.axis_index("c").reshape(1), mine, other)
    return [a.reshape(8 * shard.shape[0], shard.shape[1]) for a, shard in zip(whole, shards)]


def first_step(place, shard, others):
    if not place.tuned:
        return (), others
    half = shard.shape[0] // 2
    own = lax.dynamic_slice_in_dim(shard, place.c * half, half, 0)
    a1, others = lax.optimization_barrier((place.move(own, line=1), others))
    return (own, a1), others


def gather_first(place, info, shard, begun, second, third):
    if not place.tuned:
        return lax.all_gather(shard, "fsdp", axis=0, tiled=True)
    quarter = shard.shape[0] // 4
    own, a1 = begun
    piece = lambda a: lax.dynamic_slice_in_dim(a, place.x * quarter, quarter, 0)
    move = place.move
    b01 = move(jnp.concatenate([piece(own), piece(a1)], 0), pair=1)
    a2 = move(a1, line=1)
    n1 = move(a1, core=1)
    a3 = tied(move(a2, line=1), second)
    x01 = move(b01, side=1)
    n2, m01 = move(a2, core=1), move(b01, core=1)
    b23 = move(jnp.concatenate([piece(a2), piece(a3)], 0), pair=1)
    n3, w01 = move(a3, core=1), move(x01, core=1)
    b23 = tied(b23, third)
    x23, m23 = tied(move(b23, side=1), second), move(b23, core=1)
    w23 = move(x23, core=1)
    return assemble(info, shard, [a1, a2, a3, n1, n2, n3], [b01, b23, x01, x23, m01, m23, w01, w23])


def gather_small(place, packed):
    return place.move(copies(packed, place.fsdp), every=place.fsdp_axes)


def plus(a, *others):
    total = a.astype(F32)
    for other in others:
        total = total + other.astype(F32)
    return total.astype(BF16)


def weight_grad(place, left, right):
    if not place.tuned:
        return dot_l(left, right).astype(BF16)
    half = right.shape[1] // 2
    columns = lambda core: lax.dynamic_slice_in_dim(right, core * half, half, 1)
    got = place.move(dot_l(left, columns(1 - place.c)).astype(BF16), core=1)
    return (dot_l(left, columns(place.c)) + got.astype(F32)).astype(BF16)


def side_half(place, grad):
    if not place.tuned:
        return grad, ()
    view = grad.reshape(8, 2, -1, grad.shape[1])
    return pick(view, place.x, 1), pick(view, 1 - place.x, 1)


def send_side(place, values):
    return [place.move(a, side=1) for a in values] if place.tuned else values


def native_sums(grads):
    parts = [
        lax.psum_scatter(g.astype(F32), "fsdp", scatter_dimension=0, tiled=True) for g in grads
    ]
    return [(lax.psum(part.astype(BF16), "dp").astype(F32),) for part in parts]


def last_stages(place, value):
    (z, x, c) = place.z, place.x, place.c
    got = yield [(pick(value, (z + k) % 4, 0), dict(line=k)) for k in (1, 2, 3)]
    value = plus(pick(value, z, 0), *got)
    (got,) = yield [(value, dict(side=1))]
    low, high = jnp.where(x == 0, value, got), jnp.where(x == 0, got, value)
    value = jnp.concatenate([low, high], -2)
    (got,) = yield [(value, dict(core=1))]
    low, high = jnp.where(c == 0, value, got), jnp.where(c == 0, got, value)
    return low.astype(F32), high.astype(F32)


def merged_stages(place, owns, gots):
    if not place.tuned:
        return native_sums(owns)
    width = min(own.shape[2] for own in owns)
    pieces = []
    for own, got in zip(owns, gots):
        value = plus(own, got)
        pieces += [value[:, :, i : i + width] for i in range(0, own.shape[2], width)]
    value = jnp.concatenate(pieces, 1).reshape(4, 2, -1, width)
    (got,) = yield [(pick(value, 1 - place.y, 1), dict(pair=1))]
    low, high = yield from last_stages(place, plus(pick(value, place.y, 1), got))
    results, row = [], 0
    halves = lambda a: a.reshape(2, -1, width)
    for own in owns:
        rows, parts = own.shape[1], []
        for side in (halves(low), halves(high)):
            for i in range(0, own.shape[2], width):
                start = row + i // width * rows
                parts.append(side[:, start : start + rows].reshape(2 * rows, width))
        row += rows * (own.shape[2] // width)
        results.append(parts)
    return results


def reduce_stages(place, grad, side_first):
    if not place.tuned:
        return native_sums([grad])[0]
    x, y = place.x, place.y
    columns = grad.shape[1]
    if side_first:
        value = grad.reshape(8, 2, -1, columns)
        (got,) = yield [(pick(value, 1 - x, 1), dict(side=1))]
        value = plus(pick(value, x, 1), got).reshape(4, 2, -1, columns)
        (got,) = yield [(pick(value, 1 - y, 1), dict(pair=1))]
        value = plus(pick(value, y, 1), got)
    else:
        value = grad.reshape(4, 2, -1, columns)
        (got,) = yield [(pick(value, 1 - y, 1), dict(pair=1))]
        value = plus(pick(value, y, 1), got).reshape(4, 2, -1, columns)
        (got,) = yield [(pick(value, 1 - x, 1), dict(side=1))]
        value = plus(pick(value, x, 1), got)
    return (yield from last_stages(place, value))


def sum_replicas(place, part):
    return jnp.sum(place.move(copies(part, place.dp), every=place.dp_axes), 0)


def layer_norm(inputs, gain_row, shift_row):
    center = inputs - jnp.mean(inputs, axis=-1, keepdims=True)
    spread = jnp.mean(center * center, axis=-1, keepdims=True)
    return center * lax.rsqrt(spread + EPSILON) * gain_row + shift_row


def exact_gelu(inputs):
    size = jnp.abs(inputs)
    falling = jnp.exp(-0.5 * inputs * inputs)
    t = 1.0 / (1.0 + (0.3275911 * 0.5**0.5) * size)
    poly = 1.061405429
    for term in (-1.453152027, 1.421413741, -0.284496736, 0.254829592):
        poly = poly * t + term
    tail = 0.5 * poly * t * falling
    phi = jnp.where(inputs < 0, tail, 1.0 - tail)
    return inputs * phi, phi + inputs * falling * (0.5 / math.pi) ** 0.5


def dot_t(a, b):
    return lax.dot_general(a, b, (((1,), (1,)), ((), ())), preferred_element_type=F32)


def dot_l(a, b):
    return lax.dot_general(a, b, (((0,), (0,)), ((), ())), preferred_element_type=F32)


def dot_n(a, b):
    return lax.dot_general(a, b, (((1,), (0,)), ((), ())), preferred_element_type=F32)


def slot_of(index):
    return jnp.floor((index.astype(F32) + 0.5) * (1.0 / SPAN))


def short_bias():
    row = lax.broadcasted_iota(jnp.int32, (CHUNK, CHUNK), 0)
    column = lax.broadcasted_iota(jnp.int32, (CHUNK, CHUNK), 1)
    keep = (slot_of(row) == slot_of(column)) & (column <= row)
    return jnp.where(keep, 0.0, NEG_LARGE)


def short_forward_kernel(q_ref, k_ref, v_ref, out_ref, bias_ref):
    @pl.when(pl.program_id(0) == 0)
    def _():
        bias_ref[...] = short_bias()

    bias = bias_ref[...]
    for chunk in range(SHORT_SLOTS * SPAN // CHUNK):
        rows = pl.ds(chunk * CHUNK, CHUNK)
        scores = dot_t(q_ref[rows, :], k_ref[rows, :]) * SCALE + bias
        top = jnp.max(scores, axis=-1, keepdims=True)
        weights = jnp.exp(scores - top)
        total = jnp.sum(weights, axis=-1, keepdims=True)
        low = (weights * (1.0 / total)).astype(BF16)
        out_ref[rows, :] = dot_n(low, v_ref[rows, :]).astype(BF16)


def block_of(rows, part):
    return pl.BlockSpec(
        (rows, HEAD_DIM), lambda h: (0, (h // GROUP) * 3 * GROUP + part * GROUP + h % GROUP)
    )


def short_forward(projected, rows):
    short_rows = SHORT_SLOTS * SPAN
    return pl.pallas_call(
        short_forward_kernel,
        grid=(HEADS,),
        out_shape=jax.ShapeDtypeStruct((rows, D), BF16),
        in_specs=[block_of(short_rows, part) for part in range(3)],
        out_specs=pl.BlockSpec((short_rows, HEAD_DIM), lambda h: (0, h)),
        scratch_shapes=[pltpu.VMEM((CHUNK, CHUNK), F32)],
        cost_estimate=pl.CostEstimate(
            flops=4 * short_rows * CHUNK * D,
            bytes_accessed=8 * rows * D,
            transcendentals=short_rows * CHUNK * HEADS,
        ),
        name="short_forward",
    )(projected, projected, projected)


def short_backward_kernel(q_ref, k_ref, v_ref, g_ref, out_ref, bias_ref):
    head = pl.program_id(0)

    @pl.when(head == 0)
    def _():
        bias_ref[...] = short_bias()

    bias = bias_ref[...]
    lanes = lambda part: pl.ds(pl.multiple_of((part * GROUP + head) * HEAD_DIM, HEAD_DIM), HEAD_DIM)
    for chunk in range(SHORT_SLOTS * SPAN // CHUNK):
        rows = pl.ds(chunk * CHUNK, CHUNK)
        query, key, grad = q_ref[rows, :], k_ref[rows, :], g_ref[rows, :]
        scores = dot_t(query, key) * SCALE + bias
        top = jnp.max(scores, axis=-1, keepdims=True)
        weights = jnp.exp(scores - top)
        probs = weights * (1.0 / jnp.sum(weights, axis=-1, keepdims=True))
        grad_probs = dot_t(grad, v_ref[rows, :])
        inner = jnp.sum(probs * grad_probs, axis=-1, keepdims=True)
        grad_scores = (probs * (grad_probs - inner)).astype(BF16)
        out_ref[rows, lanes(0)] = (dot_n(grad_scores, key) * SCALE).astype(BF16)
        out_ref[rows, lanes(1)] = (dot_l(grad_scores, query) * SCALE).astype(BF16)
        out_ref[rows, lanes(2)] = dot_l(probs.astype(BF16), grad).astype(BF16)


def short_backward(projected, grad_mixture, group):
    rows = grad_mixture.shape[0]
    short_rows = SHORT_SLOTS * SPAN
    block = lambda first: pl.BlockSpec((short_rows, HEAD_DIM), lambda h: (0, first + h))
    return pl.pallas_call(
        short_backward_kernel,
        grid=(GROUP,),
        out_shape=jax.ShapeDtypeStruct((rows, WIDE), BF16),
        in_specs=[block((group * 3 + part) * GROUP) for part in range(3)] + [block(group * GROUP)],
        out_specs=pl.BlockSpec((rows, WIDE), lambda h: (0, 0)),
        scratch_shapes=[pltpu.VMEM((CHUNK, CHUNK), F32)],
        cost_estimate=pl.CostEstimate(
            flops=10 * short_rows * CHUNK * D // GROUPS,
            bytes_accessed=14 * rows * D // GROUPS,
            transcendentals=short_rows * CHUNK * GROUP,
        ),
        name="short_backward",
    )(projected, projected, projected, grad_mixture)


def long_biases(quarter_ref):
    rows = LONG_SLOTS * SPAN
    row = lax.broadcasted_iota(jnp.int32, (rows, rows), 0)
    column = lax.broadcasted_iota(jnp.int32, (rows, rows), 1)
    slot = slot_of(row)
    same = slot == slot_of(column)
    quarter = jnp.zeros((rows, rows), jnp.int32)
    for index in range(LONG_SLOTS):
        quarter = jnp.where(slot == float(index), quarter_ref[index], quarter)
    keeps = [same & (column <= row)] + [same & (step <= quarter) for step in (1, 2, 3)]
    return [jnp.where(keep, 0.0, NEG_LARGE) for keep in keeps]


def long_probs(query, keys, biases):
    scores = [dot_t(query, key) * SCALE + bias for key, bias in zip(keys, biases)]
    top = scores[0]
    for member in scores[1:]:
        top = jnp.maximum(top, member)
    top = jnp.max(top, axis=-1, keepdims=True)
    weights = [jnp.exp(member - top) for member in scores]
    total = weights[0] + weights[1] + weights[2] + weights[3]
    scale = 1.0 / jnp.sum(total, axis=-1, keepdims=True)
    return [member * scale for member in weights]


def long_forward_kernel(quarter_ref, q, k0, v0, k1, v1, k2, v2, k3, v3, out_ref):
    biases = long_biases(quarter_ref)
    probs = long_probs(q[...], [k[...] for k in (k0, k1, k2, k3)], biases)
    total = None
    for member, value in zip(probs, (v0, v1, v2, v3)):
        part = dot_n(member.astype(BF16), value[...])
        total = part if total is None else total + part
    out_ref[...] = total.astype(BF16)


def long_specs(rows):
    return [block_of(rows, part) for part in range(3)] + [block_of(rows, 1), block_of(rows, 2)] * 3


def long_forward(quarter_index, own, priors):
    rows = own.shape[0]
    spread = [member for prior in priors for member in (prior, prior)]
    return pl.pallas_call(
        long_forward_kernel,
        grid=(HEADS,),
        out_shape=jax.ShapeDtypeStruct((rows, D), BF16),
        in_specs=[pl.BlockSpec(memory_space=pltpu.SMEM)] + long_specs(rows),
        out_specs=pl.BlockSpec((rows, HEAD_DIM), lambda h: (0, h)),
        cost_estimate=pl.CostEstimate(
            flops=16 * rows * rows * D, bytes_accessed=20 * rows * D, transcendentals=0
        ),
        name="long_forward",
    )(quarter_index, own, own, own, *spread)


def long_backward_kernel(
    quarter_ref, q, k0, v0, k1, v1, k2, v2, k3, v3, g, dq_ref, own_ref, s1_ref, s2_ref, s3_ref
):
    biases = long_biases(quarter_ref)
    query, grad = q[...], g[...]
    keys = [k[...] for k in (k0, k1, k2, k3)]
    probs = long_probs(query, keys, biases)
    grads = [dot_t(grad, value[...]) for value in (v0, v1, v2, v3)]
    inner = None
    for member, part in zip(probs, grads):
        inner = member * part if inner is None else inner + member * part
    inner = jnp.sum(inner, axis=-1, keepdims=True)
    total = None
    for index, out in enumerate((own_ref, s1_ref, s2_ref, s3_ref)):
        grad_scores = (probs[index] * (grads[index] - inner)).astype(BF16)
        part = dot_n(grad_scores, keys[index])
        total = part if total is None else total + part
        out[0, :, :] = (dot_l(grad_scores, query) * SCALE).astype(out.dtype)
        out[1, :, :] = dot_l(probs[index].astype(BF16), grad).astype(out.dtype)
    dq_ref[...] = (total * SCALE).astype(BF16)


def long_backward(quarter_index, own, priors, grad_mixture):
    rows = own.shape[0]
    spread = [member for prior in priors for member in (prior, prior)]
    flat = pl.BlockSpec((rows, HEAD_DIM), lambda h: (0, h))
    pair = pl.BlockSpec((2, rows, HEAD_DIM), lambda h: (0, 0, h))
    return pl.pallas_call(
        long_backward_kernel,
        grid=(HEADS,),
        out_shape=[jax.ShapeDtypeStruct((rows, D), BF16)]
        + [jax.ShapeDtypeStruct((2, rows, D), kind) for kind in (F32, BF16, BF16, BF16)],
        in_specs=[pl.BlockSpec(memory_space=pltpu.SMEM)] + long_specs(rows) + [flat],
        out_specs=[flat] + [pair] * 4,
        cost_estimate=pl.CostEstimate(
            flops=40 * rows * rows * D, bytes_accessed=40 * rows * D, transcendentals=0
        ),
        name="long_backward",
    )(quarter_index, own, own, own, *spread, grad_mixture)


def body(
    place,
    series_values,
    quarter_index,
    patch_weight,
    heads_in,
    heads_out,
    expand_weight,
    reduce_weight_shard,
    norm_gains,
    bias_rows,
    expand_bias,
    cotangent,
):
    place.enter()
    fsdp = place.fsdp
    width = patch_weight.shape[1]
    info = jnp.stack([place.z, place.y, place.x, place.c]).astype(jnp.int32) if place.tuned else None
    row_count = series_values.shape[0]
    slot_count = row_count // SPAN
    short_rows = SHORT_SLOTS * SPAN
    long_rows = row_count - short_rows

    mixed_columns = heads_in.reshape(-1, 3, GROUPS, GROUP * HEAD_DIM).transpose(0, 2, 1, 3)
    mixed_columns = mixed_columns.reshape(-1, 3 * D)
    begun, series_values = first_step(place, mixed_columns, series_values)

    long_values = series_values[short_rows:]
    prior_values = [place.along(long_values, step) for step in (1, 2, 3)]

    grouped = series_values.reshape(slot_count, SPAN * PATCH)
    slot_sums = jnp.stack([jnp.sum(grouped, 1), jnp.sum(grouped * grouped, 1)], 1)
    rows_of = lambda a: a.astype(F32).reshape(-1, width)
    sums_row = slot_sums[SHORT_SLOTS:].reshape(1, 2 * LONG_SLOTS)
    sums_row = jnp.pad(sums_row, ((0, 7), (0, width - 2 * LONG_SLOTS)))
    pieces = [rows_of(a) for a in (patch_weight, norm_gains, bias_rows, expand_bias)]
    small_rows = sum(piece.shape[0] for piece in pieces)
    small = gather_small(place, jnp.concatenate(pieces + [sums_row], 0))
    chain = small[:, small_rows, : 2 * LONG_SLOTS].reshape(fsdp, LONG_SLOTS, 2)
    offset = jnp.arange(fsdp)[:, None] - place.f + quarter_index[None, :]
    member = ((offset + fsdp) % fsdp < 4).astype(F32)[:, :, None]
    chain_sum = jnp.sum(chain * member, 0)

    wide = lambda low, high: small[:, low:high].transpose(1, 0, 2).reshape(high - low, D)
    patch_all = wide(0, PATCH).astype(BF16)
    gains_all = wide(PATCH, PATCH + 2)
    biases_all = wide(PATCH + 2, PATCH + 6)
    expand_shift = small[:, PATCH + 6 : small_rows].reshape(-1)

    gather_near = Chain(place, gather_stages(place, heads_out, expand_weight))
    gather_far = Chain(place, gather_stages(place, reduce_weight_shard))
    heads_in_all = gather_first(place, info, mixed_columns, begun, gather_near, gather_far)

    totals = jnp.concatenate([slot_sums[:SHORT_SLOTS], chain_sum], 0)
    counts = jnp.where(jnp.arange(slot_count) < SHORT_SLOTS, SPAN * PATCH, 4 * SPAN * PATCH).astype(
        F32
    )
    slot_mean = totals[:, 0] / counts
    inv_spread = lax.rsqrt(totals[:, 1] / counts - slot_mean * slot_mean + EPSILON)
    normed_slots = (grouped - slot_mean[:, None]) * inv_spread[:, None]
    normed_low = normed_slots.reshape(row_count, PATCH).astype(BF16)
    embedded = dot_n(normed_low, patch_all) + biases_all[0]
    first_value, first_back = jax.vjp(layer_norm, embedded, gains_all[0], biases_all[1])
    first_norm = first_value.astype(BF16)
    prior_normed = [
        (
            (a.reshape(LONG_SLOTS, -1) - slot_mean[SHORT_SLOTS:, None])
            * inv_spread[SHORT_SLOTS:, None]
        ).reshape(long_rows, PATCH)
        for a in prior_values
    ]
    prior_low = jnp.concatenate(prior_normed, 0).astype(BF16)
    prior_embedded = dot_n(prior_low, patch_all) + biases_all[0]
    prior_norms = layer_norm(prior_embedded, gains_all[0], biases_all[1]).astype(BF16)
    prior_norms, heads_in_all = lax.optimization_barrier((prior_norms, heads_in_all))
    projected = dot_n(first_norm, heads_in_all).astype(BF16)
    own_long = projected[short_rows:]
    prior_all = dot_n(prior_norms, heads_in_all).astype(BF16)
    priors = [prior_all[i * long_rows : (i + 1) * long_rows] for i in range(3)]

    mixed_short = short_forward(projected, row_count)
    mixed_long = long_forward(quarter_index, own_long, priors)
    mixed_short, mixed_long = tied((mixed_short, mixed_long), gather_near, gather_far)
    heads_out_all, expand_all = gather_near.finish()
    mixed_all = lax.dynamic_update_slice(mixed_short, mixed_long, (short_rows, 0))
    middle = embedded + dot_n(mixed_all, heads_out_all)
    second_value, second_back = jax.vjp(layer_norm, middle, gains_all[1], biases_all[2])
    second_norm = second_value.astype(BF16)

    pre_act = dot_n(second_norm, expand_all) + expand_shift
    act_value, act_slope = exact_gelu(pre_act)
    activation = tied(act_value.astype(BF16), gather_far)
    grad_reduce = weight_grad(place, activation, cotangent)

    (reduce_all,) = gather_far.finish()
    grad_act = dot_t(cotangent, reduce_all)
    grad_pre = (grad_act * act_slope).astype(BF16)
    own_reduce, sent_reduce = side_half(place, grad_reduce)
    grad_pre, sent_reduce = lax.optimization_barrier((grad_pre, sent_reduce))
    (got_reduce,) = send_side(place, [sent_reduce])
    grad_expand = weight_grad(place, second_norm, grad_pre)
    grad_expand_bias = jnp.sum(grad_pre.astype(F32), 0)
    grad_second = dot_t(grad_pre, expand_all)
    middle_back, gain_two, shift_two = second_back(grad_second)
    grad_middle = cotangent.astype(F32) + middle_back
    grad_branch = grad_middle.astype(BF16)
    grad_heads_out = weight_grad(place, mixed_all, grad_branch)
    own_expand, sent_expand = side_half(place, grad_expand)
    own_out, sent_out = side_half(place, grad_heads_out)
    grad_mixture = dot_t(grad_branch, heads_out_all).astype(BF16)
    grad_mixture, sent = lax.optimization_barrier((grad_mixture, [sent_expand, sent_out]))
    got_expand, got_out = send_side(place, sent)

    long_query, own_grads, *sent = long_backward(
        quarter_index, own_long, priors, grad_mixture[short_rows:]
    )
    for step, sent_back in zip((1, 2, 3), sent):
        own_grads = own_grads + place.along(sent_back, -step).astype(F32)
    own_grads = own_grads.astype(BF16)

    def grad_group(g, grad_mixture):
        columns = slice(g * GROUP * HEAD_DIM, (g + 1) * GROUP * HEAD_DIM)
        grad_long = jnp.concatenate([a[:, columns] for a in (long_query, *own_grads)], 1)
        short = short_backward(projected, grad_mixture, g)
        return lax.dynamic_update_slice(short, grad_long, (short_rows, 0))

    grad_mixture, long_query, got_reduce = lax.optimization_barrier(
        (grad_mixture, long_query, got_reduce)
    )
    grad_projected = grad_group(0, grad_mixture)
    grad_in = weight_grad(place, first_norm, grad_projected)
    heads_in_all, gots = lax.optimization_barrier(
        (heads_in_all, [got_expand, got_out, got_reduce])
    )
    owns = [own_expand, own_out, own_reduce]
    grad_rest = Chain(place, merged_stages(place, owns, gots))
    heads_in_all = tied(heads_in_all, grad_rest)
    middle_column = grad_in.shape[1] // 2
    grad_low = Chain(place, reduce_stages(place, grad_in[:, :middle_column], True))
    grad_high = Chain(place, reduce_stages(place, grad_in[:, middle_column:], False))
    grad_first = dot_t(grad_projected, heads_in_all)
    embed_back, gain_one, shift_one = first_back(grad_first)
    grad_embedded = tied((grad_middle + embed_back).astype(BF16), grad_low, grad_high)
    grad_patch = dot_l(normed_low, grad_embedded)
    shift_zero = jnp.sum(grad_embedded.astype(F32), 0)
    grad_normed = dot_t(grad_embedded, patch_all).reshape(slot_count, SPAN * PATCH)
    slot_grads = jnp.stack([jnp.sum(grad_normed, 1), jnp.sum(grad_normed * normed_slots, 1)], 1)
    shift_three = jnp.sum(cotangent.astype(F32), 0)
    split = lambda a: a.reshape(-1, fsdp, width).transpose(1, 0, 2)
    chain_row = slot_grads[SHORT_SLOTS:].reshape(1, 2 * LONG_SLOTS)
    chain_row = jnp.pad(chain_row, ((0, 7), (0, width - 2 * LONG_SLOTS)))
    packed = jnp.concatenate(
        [
            split(grad_patch),
            split(jnp.stack([gain_one, gain_two, shift_zero, shift_one, shift_two, shift_three])),
            grad_expand_bias.reshape(fsdp, -1, width),
            jnp.broadcast_to(chain_row, (fsdp,) + chain_row.shape),
        ],
        1,
    )
    packed, activation = tied((packed, activation), grad_rest)
    parts = place.move(packed, every=place.fsdp_axes)
    layer_output = (middle + dot_n(activation, reduce_all) + biases_all[3]).astype(BF16)
    layer_output = tied(layer_output, grad_low, grad_high)
    layer_output, parts = lax.optimization_barrier((layer_output, parts))
    chain_grads = parts[:, small_rows, : 2 * LONG_SLOTS].reshape(fsdp, LONG_SLOTS, 2)
    chain_grad = jnp.sum(chain_grads * member, 0)
    small_sums = tied(jnp.sum(parts[:, :small_rows], 0), grad_low, grad_high, grad_rest)
    small_grads = sum_replicas(place, small_sums)
    grad_totals = jnp.concatenate([slot_grads[:SHORT_SLOTS], chain_grad], 0)
    series_grad = (
        inv_spread[:, None]
        * (
            grad_normed
            - grad_totals[:, 0:1] / counts[:, None]
            - normed_slots * grad_totals[:, 1:2] / counts[:, None]
        )
    ).reshape(row_count, PATCH)
    if place.tuned:
        ((low_own, low_other), (high_own, high_other)) = grad_low.finish(), grad_high.finish()
        in_parts = [low_own, high_own, low_other, high_other]
    else:
        in_parts = [*grad_low.finish(), *grad_high.finish()]
    grad_heads_in = jnp.concatenate(in_parts, 1)
    grad_expand, grad_heads_out, grad_reduce = [
        jnp.concatenate(parts, 1) for parts in grad_rest.finish()
    ]
    return (
        layer_output,
        series_grad,
        small_grads[:PATCH],
        grad_heads_in,
        grad_heads_out,
        grad_expand,
        grad_reduce,
        small_grads[PATCH : PATCH + 2],
        small_grads[PATCH + 2 : PATCH + 6],
        small_grads[PATCH + 6 :].reshape(-1),
    )


def solution(mesh):
    tuned = mesh.shape["fsdp"] == 8 and mesh.shape["dp"] == 4
    if tuned:
        mesh = Mesh(mesh.devices.reshape(4, 2, 2, 2), ("z", "y", "x", "c"))
    place = Place(tuned)
    fsdp, both = place.fsdp_axes, place.fsdp_axes + place.dp_axes
    in_specs = (
        P(both, None),
        P(both),
        P(None, fsdp),
        P(fsdp, None),
        P(fsdp, None),
        P(fsdp, None),
        P(fsdp, None),
        P(None, fsdp),
        P(None, fsdp),
        P(fsdp),
        P(both, None),
    )
    out_specs = (
        P(both, None),
        P(both, None),
        P(None, fsdp),
        P(fsdp, None),
        P(fsdp, None),
        P(fsdp, None),
        P(fsdp, None),
        P(None, fsdp),
        P(None, fsdp),
        P(fsdp),
    )
    layer = lambda *arguments: body(place, *arguments)
    return jax.shard_map(layer, mesh=mesh, in_specs=in_specs, out_specs=out_specs, check_vma=False)
```
